256 devices in a mesh: vocab: 32 (over x, z), dp: 8 (over y, core).
Axes of the slice: x: 4, y: 4, z: 8, core: 2. Of those that a mesh axis runs over, the one named last changes fastest.
Arguments:
- teacher_hidden: bfloat16 [1024, 5376], P('dp'), may hold values from -48 to 48
- student_hidden: bfloat16 [1024, 2560], P('dp'), may hold values from -48 to 48
- teacher_codes: bfloat16 [131072, 5376], P(('vocab', 'dp')), may hold values from -8 to 7, as said below
- teacher_scales: float32 [131072, 42], P(('vocab', 'dp')), may hold values from 0.003 to 0.07
- student_weight: bfloat16 [131072, 2560], P(('vocab', 'dp')), may hold values from -1 to 1
- loss_scale: bfloat16 [1024], P('dp'), may hold values from 2 to 20
Outputs:
- kl: float32 [1024], P('dp')
- grad_hidden: bfloat16 [1024, 2560], P('dp', 'vocab')
- grad_weight: bfloat16 [131072, 2560], P(('vocab', 'dp'))
The draws below stay inside these ranges and needn't reach their ends.
Inputs may be any that keep to these rules, and one draw needn't show every extreme that they name: `teacher_codes`: whole numbers.
All inputs are finite; a program needn't handle non-finite values.
Results may differ from the reference program's by a relative error of at most 0.0085.
Values may be sent and summed in bfloat16 or wider, within the bound.
No kernel may reach another device: no remote copies, remote signals or barrier semaphores. Data moves between devices by JAX's collectives and lax.ppermute only.
A program may use at most 128 MiB of HBM per device.

```python
import math
import jax
import jax.numpy as jnp
from jax import lax

DT = 5376
DS = 2560
GROUP = 128
V_DEV = 512
TOKENS = 1024
VOCAB = 131072
N_VOCAB = 32
N_DP = 8


def code_rows(key, row_ids):
    base_key = jax.random.fold_in(key, 101)

    def single(row_id):
        return jax.random.randint(jax.random.fold_in(base_key, row_id), (DT,), -8, 8).astype(jnp.float32)
    return jax.vmap(single)(row_ids)


def scale_rows(key, row_ids):
    base_key = jax.random.fold_in(key, 202)
    level_low, level_high, rise_total = (0.0085, 0.0105, 1.1)

    def single(row_id):
        key_pair = jax.random.split(jax.random.fold_in(base_key, row_id))
        scale_level = jnp.exp(jax.random.uniform(key_pair[0], (), jnp.float32, math.log(level_low), math.log(level_high)))
        jitter_factor = jnp.exp(jax.random.uniform(key_pair[1], (DT // GROUP,), jnp.float32, math.log(0.8), math.log(1.25)))
        rising_factor = jnp.exp(math.log(rise_total) * row_id.astype(jnp.float32) / VOCAB)
        return scale_level * rising_factor * jitter_factor
    return jax.vmap(single)(row_ids)


def student_rows(key, row_ids):
    base_key = jax.random.fold_in(key, 303)
    level_low, level_high, rise_total = (0.9, 1.2, 1.5)

    def single(row_id):
        key_pair = jax.random.split(jax.random.fold_in(base_key, row_id))
        scale_level = jnp.exp(jax.random.uniform(key_pair[0], (), jnp.float32, math.log(level_low), math.log(level_high)))
        rising_factor = jnp.exp(math.log(rise_total) * row_id.astype(jnp.float32) / VOCAB)
        values = jnp.clip(jax.random.normal(key_pair[1], (DS,), jnp.float32), -4.0, 4.0)
        return jnp.clip(scale_level * rising_factor * values / math.sqrt(DS), -1.0, 1.0)
    return jax.vmap(single)(row_ids).astype(jnp.bfloat16).astype(jnp.float32)


def hidden_draw(key, col_count, salt_value):
    key_list = jax.random.split(jax.random.fold_in(key, salt_value), 2)
    row_scale = jnp.exp(jax.random.uniform(key_list[0], (TOKENS, 1), jnp.float32, math.log(0.9), math.log(1.1)))
    values = jax.random.normal(key_list[1], (TOKENS, col_count), jnp.float32) * row_scale
    return jnp.clip(values, -48.0, 48.0).astype(jnp.bfloat16)


def draw_teacher_hidden(key, part):
    return hidden_draw(key, DT, 505)


def draw_student_hidden(key, part):
    return hidden_draw(key, DS, 606)


def draw_teacher_codes(key, part):
    return code_rows(key, jnp.arange(VOCAB, dtype=jnp.int32)).astype(jnp.bfloat16)


def draw_teacher_scales(key, part):
    return scale_rows(key, jnp.arange(VOCAB, dtype=jnp.int32)).astype(jnp.float32)


def draw_student_weight(key, part):
    return student_rows(key, jnp.arange(VOCAB, dtype=jnp.int32)).astype(jnp.bfloat16)


def steps_of(key, dims, pieces, least, largest):
    gain = 1.0
    for dim, blocks in pieces:
        steps = jax.random.uniform(jax.random.fold_in(jax.random.fold_in(key, 6), dim), (blocks,), jnp.float32, least / len(pieces), largest / len(pieces))
        gain = gain * jnp.repeat(jnp.exp(steps), dims[dim] // blocks).reshape((-1,) + (1,) * (len(dims) - 1 - dim))
    return gain


def setup_inputs(seed: int = 0) -> dict:
    seeds = jax.random.split(jax.random.key(seed), 7)
    return {
        "teacher_hidden": draw_teacher_hidden(jax.random.fold_in(seeds[6], 71), 0),
        "student_hidden": draw_student_hidden(jax.random.fold_in(seeds[6], 71), 0),
        "teacher_codes": draw_teacher_codes(jax.random.fold_in(seeds[6], 71), 0),
        "teacher_scales": draw_teacher_scales(jax.random.fold_in(seeds[6], 71), 0),
        "student_weight": draw_student_weight(jax.random.fold_in(seeds[6], 71), 0),
        "loss_scale": jnp.clip(jnp.exp(math.log(20.0) - 2.3025851 * jax.random.uniform(seeds[5], (TOKENS,), jnp.float32) ** steps_of(seeds[5], (TOKENS,), ((0, 8),), -0.2, 0.2)), 2.0, 20.0).astype(jnp.bfloat16),
    }


def dequantize(code_values, scales):
    row_count = code_values.shape[0]
    grouped = code_values.astype(jnp.float32).reshape(row_count, -1, GROUP) * scales.astype(jnp.float32)[:, :, None]
    return grouped.reshape(row_count, -1).astype(jnp.bfloat16)


def reference(teacher_hidden, student_hidden, teacher_codes, teacher_scales, student_weight, loss_scale):
    blocks = N_VOCAB * N_DP
    teacher_wide = teacher_hidden.astype(jnp.float32)
    student_wide = student_hidden.astype(jnp.float32)
    code_blocks = teacher_codes.reshape(blocks, V_DEV, DT)
    scale_blocks = teacher_scales.reshape(blocks, V_DEV, DT // GROUP)
    weight_blocks = student_weight.reshape(blocks, V_DEV, DS)

    def block_logits(members):
        code_values, scales, weight = members
        dequant_rows = dequantize(code_values, scales).astype(jnp.float32)
        teacher_part = jnp.dot(teacher_wide, dequant_rows.T, preferred_element_type=jnp.float32, precision=lax.Precision.HIGHEST)
        student_part = jnp.dot(student_wide, weight.astype(jnp.float32).T, preferred_element_type=jnp.float32, precision=lax.Precision.HIGHEST)
        return teacher_part, student_part

    teacher_logits, student_logits = lax.map(block_logits, (code_blocks, scale_blocks, weight_blocks))
    teacher_top = jnp.max(teacher_logits, axis=(0, 2))
    student_top = jnp.max(student_logits, axis=(0, 2))
    teacher_exp = jnp.exp(teacher_logits - teacher_top[None, :, None])
    teacher_total = jnp.sum(teacher_exp, axis=(0, 2))
    cross_total = jnp.sum(teacher_exp * (teacher_logits - student_logits), axis=(0, 2))
    student_total = jnp.sum(jnp.exp(student_logits - student_top[None, :, None]), axis=(0, 2))
    teacher_lse = teacher_top + jnp.log(teacher_total)
    student_lse = student_top + jnp.log(student_total)
    kl = cross_total / teacher_total - teacher_lse + student_lse
    teacher_prob = jnp.exp(teacher_logits - teacher_lse[None, :, None])
    student_prob = jnp.exp(student_logits - student_lse[None, :, None])
    logit_grad = (loss_scale.astype(jnp.float32)[None, :, None] * (student_prob - teacher_prob)).astype(jnp.bfloat16)

    def add_block(running, members):
        grad_block, weight = members
        product = jnp.dot(grad_block.astype(jnp.float32), weight.astype(jnp.float32), preferred_element_type=jnp.float32, precision=lax.Precision.HIGHEST)
        return running + product, None

    grad_hidden, unused = lax.scan(add_block, jnp.zeros((TOKENS, DS), jnp.float32), (logit_grad, weight_blocks))

    def weight_block(grad_block):
        product = jnp.dot(grad_block.astype(jnp.float32).T, student_wide, preferred_element_type=jnp.float32, precision=lax.Precision.HIGHEST)
        return product.astype(jnp.bfloat16)

    grad_weight = lax.map(weight_block, logit_grad).reshape(blocks * V_DEV, DS)
    return kl, grad_hidden.astype(jnp.bfloat16), grad_weight
```

```python
import jax
import jax.numpy as jnp
from jax import lax
from jax.sharding import Mesh
from jax.sharding import PartitionSpec as P

GROUP = 128
AXES = ("x", "z", "y", "c")
DP = ("y", "c")
VOCAB = ("x", "z")
F32, BF16 = jnp.float32, jnp.bfloat16


def shift(a, axis, by):
    n = lax.axis_size(axis)
    return lax.ppermute(a, axis, [((i + by) % n, i) for i in range(n)])


def rolled(blocks, start):
    n = blocks.shape[0]
    return lax.dynamic_slice_in_dim(jnp.concatenate([blocks, blocks[:-1]]), start % n, n, 0)


def dequantize(code_values, scales):
    row_count = code_values.shape[0]
    grouped = code_values.astype(F32).reshape(row_count, -1, GROUP) * scales[:, :, None]
    return grouped.reshape(row_count, -1).astype(BF16)


def rows_by_tokens(rows, tokens):
    return lax.dot_general(rows, tokens, (((1,), (1,)), ((), ())), preferred_element_type=F32)


def to_all(a, axes):
    n = lax.axis_size(axes)
    return lax.all_to_all(jnp.broadcast_to(a[None], (n, *a.shape)), axes, 0, 0, tiled=True)


def combine(stats):
    teacher_top = jnp.max(stats[:, 0], axis=0)
    student_top = jnp.max(stats[:, 3], axis=0)
    teacher_factor = jnp.exp(stats[:, 0] - teacher_top)
    student_factor = jnp.exp(stats[:, 3] - student_top)
    return jnp.stack(
        [
            teacher_top,
            jnp.sum(stats[:, 1] * teacher_factor, axis=0),
            jnp.sum(stats[:, 2] * teacher_factor, axis=0),
            student_top,
            jnp.sum(stats[:, 4] * student_factor, axis=0),
        ]
    )


def local(
    teacher_hidden, student_hidden, teacher_codes, teacher_scales, student_weight, loss_scale
):
    tok, width_t = teacher_hidden.shape
    width_s = student_hidden.shape[1]
    n_x, n_z, n_y = (lax.axis_size(a) for a in ("x", "z", "y"))
    x, y = lax.axis_index("x"), lax.axis_index("y")
    part = tok // n_x

    hidden = jnp.concatenate([teacher_hidden, student_hidden], axis=1)
    quarter = shift(lax.dynamic_slice_in_dim(hidden, x * part, part, 0), "y", 2)
    after, before = shift(hidden, "y", 1), shift(hidden, "y", 3)
    quarters = jnp.stack([quarter, *(shift(quarter, "x", k) for k in range(1, n_x))])
    opposite = rolled(quarters, n_x - x).reshape(tok, -1)

    table = dequantize(teacher_codes, teacher_scales)
    weight_p = shift(student_weight, "c", 1)
    table_p = shift(table, "c", 1)

    pairs = (jnp.concatenate([hidden, opposite]), jnp.concatenate([after, before]))
    logits, stats = [], []
    for pair in pairs:
        pt, ps = pair[:, :width_t], pair[:, width_t:]
        t = [rows_by_tokens(rows, pt) for rows in (table, table_p)]
        s = [rows_by_tokens(rows, ps) for rows in (student_weight, weight_p)]
        t_top = jnp.maximum(jnp.max(t[0], axis=0), jnp.max(t[1], axis=0))
        s_top = jnp.maximum(jnp.max(s[0], axis=0), jnp.max(s[1], axis=0))
        t_sum = cross = s_sum = 0.0
        for a, b in zip(t, s):
            e = jnp.exp(a - t_top)
            t_sum += jnp.sum(e, axis=0)
            cross += jnp.sum(e * (a - b), axis=0)
            s_sum += jnp.sum(jnp.exp(b - s_top), axis=0)
        logits.append((t, s))
        stats.append(jnp.stack([t_top, t_sum, cross, s_top, s_sum]).reshape(5, 2, tok))
    rel = jnp.stack([stats[0][:, 0], stats[1][:, 0], stats[0][:, 1], stats[1][:, 1]])
    scale_row = loss_scale.astype(F32)[None, None]
    scale_rel = jnp.concatenate([scale_row, jnp.zeros((n_y - 1, 1, tok), F32)])
    block_abs = rolled(jnp.concatenate([rel, scale_rel], axis=1), n_y - y)
    seen = to_all(block_abs.transpose(1, 0, 2).reshape(6, -1), ("x", "y"))
    scales = jnp.sum(seen[:n_y, 5], axis=0)
    totals = combine(to_all(combine(seen), "z"))
    t_lse = totals[0] + jnp.log(totals[1])
    s_lse = totals[3] + jnp.log(totals[4])
    divergence = totals[2] / totals[1] - t_lse + s_lse
    back = rolled(jnp.stack([t_lse, s_lse, scales, divergence]).reshape(4, n_y, tok).transpose(1, 0, 2), y)
    kl = back[0, 3]

    own, other = [], []
    for p, (t, s) in enumerate(logits):
        tl, sl, sc = (jnp.concatenate([back[p, i], back[p + 2, i]]) for i in range(3))
        for k, out in ((0, own), (1, other)):
            out.append((sc * (jnp.exp(s[k] - sl) - jnp.exp(t[k] - tl))).astype(BF16))
    own, other = jnp.concatenate(own, axis=1), jnp.concatenate(other, axis=1)
    from_p = shift(other, "c", 1)
    students = jnp.concatenate([p[:, width_t:] for p in pairs])
    students_p = shift(students, "c", 1)

    def into(rows, tokens):
        return jnp.dot(rows, tokens, preferred_element_type=F32)

    grad_t = lax.dot_general(
        jnp.concatenate([student_weight, weight_p]),
        jnp.concatenate([own, other]),
        (((0,), (0,)), ((), ())),
        preferred_element_type=F32,
    ).astype(BF16)
    blocks = grad_t.reshape(n_x, width_s // n_x, n_y, tok).transpose(2, 0, 1, 3)
    blocks = jnp.stack([blocks[0], blocks[2], blocks[1], blocks[3]])
    blocks = rolled(blocks, n_y - y).transpose(1, 0, 2, 3)
    blocks = blocks.reshape(n_x * n_y, width_s // n_x, tok)
    got = lax.all_to_all(blocks, ("x", "y"), 0, 0, tiled=True)
    got = jnp.sum(got.astype(F32), axis=0).astype(BF16).reshape(n_z, -1, tok)
    got = lax.all_to_all(got, "z", 0, 0, tiled=True)
    grad_hidden = jnp.sum(got.astype(F32), axis=0).astype(BF16).T

    grad_weight = (into(own, students) + into(from_p, students_p)).astype(BF16)
    return kl, grad_hidden, grad_weight


def solution(mesh):
    split = Mesh(mesh.devices.reshape(4, 8, 4, 2), AXES)
    rows = P(("x", "z", "y", "c"), None)
    return jax.shard_map(
        local,
        mesh=split,
        in_specs=(P(DP, None), P(DP, None), rows, rows, rows, P(DP)),
        out_specs=(P(DP), P(DP, VOCAB), rows),
        check_vma=False,
    )
```

```python
import functools

import jax
import jax.numpy as jnp
from jax import lax
from jax.experimental import pallas as pl
from jax.experimental.pallas import tpu as pltpu
from jax.sharding import Mesh
from jax.sharding import PartitionSpec as P

GROUP = 128
AXES = ("x", "z", "y", "c")
DP = ("y", "c")
VOCAB = ("x", "z")
F32, BF16 = jnp.float32, jnp.bfloat16


def shift(a, axis, by):
    n = lax.axis_size(axis)
    return lax.ppermute(a, axis, [((i + by) % n, i) for i in range(n)])


def rolled(blocks, start):
    n = blocks.shape[0]
    return lax.dynamic_slice_in_dim(jnp.concatenate([blocks, blocks[:-1]]), start % n, n, 0)


NT = (((1,), (1,)), ((), ()))
VMEM_LIMIT = 56 * 1024 * 1024
DEQUANT_ROWS = 128
LOGIT_ROWS = 256


def dequant_kernel(own_steps, own_ref, other_ref, own_scale_ref, other_scale_ref, out_ref):
    def write(codes_ref, scale_ref):
        for g in range(codes_ref.shape[1] // GROUP):
            at = slice(g * GROUP, (g + 1) * GROUP)
            wide = codes_ref[:, at].astype(F32) * scale_ref[:, g : g + 1]
            out_ref[:, at] = wide.astype(BF16)

    @pl.when(pl.program_id(0) < own_steps)
    def _():
        write(own_ref, own_scale_ref)

    @pl.when(pl.program_id(0) >= own_steps)
    def _():
        write(other_ref, other_scale_ref)


def dequantize(codes, codes_p, scales, scales_p):
    rows, width = codes.shape
    steps = rows // DEQUANT_ROWS

    def own(i):
        return (jnp.minimum(i, steps - 1), 0)

    def other(i):
        return (jnp.maximum(i - steps, 0), 0)

    return pl.pallas_call(
        functools.partial(dequant_kernel, steps),
        grid=(2 * steps,),
        in_specs=[
            pl.BlockSpec((DEQUANT_ROWS, width), own),
            pl.BlockSpec((DEQUANT_ROWS, width), other),
            pl.BlockSpec((DEQUANT_ROWS, scales.shape[1]), own),
            pl.BlockSpec((DEQUANT_ROWS, scales.shape[1]), other),
        ],
        out_specs=pl.BlockSpec((DEQUANT_ROWS, width), lambda i: (i, 0)),
        out_shape=jax.ShapeDtypeStruct((2 * rows, width), BF16),
        compiler_params=pltpu.CompilerParams(vmem_limit_bytes=VMEM_LIMIT),
        cost_estimate=pl.CostEstimate(
            flops=2 * rows * width, transcendentals=0, bytes_accessed=8 * rows * width
        ),
        name="dequantize",
    )(codes, codes_p, scales, scales_p)


def logits_kernel(width_t, a_hbm, b_hbm, table_ref, weight_ref, t_ref, s_ref, stat_ref, pair, sem):
    step = pl.program_id(0)
    tok = a_hbm.shape[0]

    @pl.when(step == 0)
    def _():
        copies = [
            pltpu.make_async_copy(a_hbm, pair.at[pl.ds(0, tok)], sem.at[0]),
            pltpu.make_async_copy(b_hbm, pair.at[pl.ds(tok, tok)], sem.at[1]),
        ]
        for copy in copies:
            copy.start()
        for copy in copies:
            copy.wait()

    t = lax.dot_general(table_ref[...], pair[:, :width_t], NT, preferred_element_type=F32)
    s = lax.dot_general(weight_ref[...], pair[:, width_t:], NT, preferred_element_type=F32)
    t_ref[...] = t
    s_ref[...] = s
    t_top = jnp.max(t, axis=0, keepdims=True)
    s_top = jnp.max(s, axis=0, keepdims=True)

    def sums(t_top, s_top):
        e = jnp.exp(t - t_top)
        return (
            jnp.sum(e, axis=0, keepdims=True),
            jnp.sum(e * (t - s), axis=0, keepdims=True),
            jnp.sum(jnp.exp(s - s_top), axis=0, keepdims=True),
        )

    @pl.when(step == 0)
    def _():
        total, cross, s_total = sums(t_top, s_top)
        for k, row in enumerate((t_top, total, cross, s_top, s_total)):
            stat_ref[k : k + 1] = row
        stat_ref[5:8] = jnp.zeros((3, t.shape[1]), F32)

    @pl.when(step > 0)
    def _():
        t_old, s_old = stat_ref[0:1], stat_ref[3:4]
        t_new, s_new = jnp.maximum(t_old, t_top), jnp.maximum(s_old, s_top)
        total, cross, s_total = sums(t_new, s_new)
        t_keep, s_keep = jnp.exp(t_old - t_new), jnp.exp(s_old - s_new)
        stat_ref[0:1] = t_new
        stat_ref[1:2] = stat_ref[1:2] * t_keep + total
        stat_ref[2:3] = stat_ref[2:3] * t_keep + cross
        stat_ref[3:4] = s_new
        stat_ref[4:5] = stat_ref[4:5] * s_keep + s_total


def logits_of(a, b, table, weight):
    rows, width_t = table.shape
    width_s = weight.shape[1]
    tokens = 2 * a.shape[0]
    tile = jax.ShapeDtypeStruct((rows, tokens), F32)
    return pl.pallas_call(
        functools.partial(logits_kernel, width_t),
        grid=(rows // LOGIT_ROWS,),
        in_specs=[
            pl.BlockSpec(memory_space=pl.ANY),
            pl.BlockSpec(memory_space=pl.ANY),
            pl.BlockSpec((LOGIT_ROWS, width_t), lambda i: (i, 0)),
            pl.BlockSpec((LOGIT_ROWS, width_s), lambda i: (i, 0)),
        ],
        out_specs=[
            pl.BlockSpec((LOGIT_ROWS, tokens), lambda i: (i, 0)),
            pl.BlockSpec((LOGIT_ROWS, tokens), lambda i: (i, 0)),
            pl.BlockSpec((8, tokens), lambda i: (0, 0)),
        ],
        out_shape=[tile, tile, jax.ShapeDtypeStruct((8, tokens), F32)],
        scratch_shapes=[
            pltpu.VMEM((tokens, width_t + width_s), BF16),
            pltpu.SemaphoreType.DMA((2,)),
        ],
        compiler_params=pltpu.CompilerParams(vmem_limit_bytes=VMEM_LIMIT),
        cost_estimate=pl.CostEstimate(
            flops=2 * rows * tokens * (width_t + width_s),
            transcendentals=2 * rows * tokens,
            bytes_accessed=2 * (rows + tokens) * (width_t + width_s) + 8 * rows * tokens,
        ),
        name="logits",
    )(a, b, table, weight)


def grad_kernel(y_ref, rows_ref, t0, s0, t1, s1, turned_ref, own_ref, other_ref, out_ref):
    half = own_ref.shape[0]
    n_y, tok = out_ref.shape[1], out_ref.shape[3]

    @pl.when(pl.program_id(0) == 0)
    def _():
        for p, (t, s) in enumerate(((t0, s0), (t1, s1))):
            at = slice(2 * p * tok, 2 * (p + 1) * tok)
            t_lse, s_lse, scale = (rows_ref[k : k + 1, at] for k in range(3))
            for q, ref in enumerate((own_ref, other_ref)):
                rows = slice(q * half, (q + 1) * half)
                gap = jnp.exp(s[rows] - s_lse) - jnp.exp(t[rows] - t_lse)
                ref[:, at] = (scale * gap).astype(BF16)

    total = jnp.dot(turned_ref[:, :half], own_ref[...], preferred_element_type=F32)
    total += jnp.dot(turned_ref[:, half:], other_ref[...], preferred_element_type=F32)
    for k, r in enumerate((0, 2, 1, 3)):
        at = lax.rem(y_ref[0] + r, n_y)
        out_ref[0, at] = total[:, k * tok : (k + 1) * tok].astype(BF16)


def gradients(y, rows, logits, turned, n_x, n_y):
    (t0, s0), (t1, s1) = logits
    vocab, tokens = t0.shape
    width = turned.shape[0]
    lg = jax.ShapeDtypeStruct((vocab // 2, 2 * tokens), BF16)
    whole = pl.BlockSpec((vocab, tokens), lambda i, y: (0, 0))
    lg_spec = pl.BlockSpec((vocab // 2, 2 * tokens), lambda i, y: (0, 0))
    cut = (width // n_x, 2 * tokens // n_y)
    return pl.pallas_call(
        grad_kernel,
        grid_spec=pltpu.PrefetchScalarGridSpec(
            num_scalar_prefetch=1,
            grid=(n_x,),
            in_specs=[
                pl.BlockSpec(rows.shape, lambda i, y: (0, 0)),
                whole,
                whole,
                whole,
                whole,
                pl.BlockSpec((width // n_x, vocab), lambda i, y: (i, 0)),
            ],
            out_specs=[lg_spec, lg_spec, pl.BlockSpec((1, n_y, *cut), lambda i, y: (i, 0, 0, 0))],
        ),
        out_shape=[lg, lg, jax.ShapeDtypeStruct((n_x, n_y, *cut), BF16)],
        compiler_params=pltpu.CompilerParams(vmem_limit_bytes=VMEM_LIMIT),
        cost_estimate=pl.CostEstimate(
            flops=4 * vocab * tokens * width,
            transcendentals=4 * vocab * tokens,
            bytes_accessed=2 * width * (vocab + 2 * tokens) + 20 * vocab * tokens,
        ),
        name="gradients",
    )(y, rows, t0, s0, t1, s1, turned)


def to_all(a, axes):
    n = lax.axis_size(axes)
    return lax.all_to_all(jnp.broadcast_to(a[None], (n, *a.shape)), axes, 0, 0, tiled=True)


def combine(stats):
    teacher_top = jnp.max(stats[:, 0], axis=0)
    student_top = jnp.max(stats[:, 3], axis=0)
    teacher_factor = jnp.exp(stats[:, 0] - teacher_top)
    student_factor = jnp.exp(stats[:, 3] - student_top)
    return jnp.stack(
        [
            teacher_top,
            jnp.sum(stats[:, 1] * teacher_factor, axis=0),
            jnp.sum(stats[:, 2] * teacher_factor, axis=0),
            student_top,
            jnp.sum(stats[:, 4] * student_factor, axis=0),
        ]
    )


def local(
    teacher_hidden, student_hidden, teacher_codes, teacher_scales, student_weight, loss_scale
):
    tok, width_t = teacher_hidden.shape
    width_s = student_hidden.shape[1]
    n_x, n_z, n_y = (lax.axis_size(a) for a in ("x", "z", "y"))
    x, y = lax.axis_index("x"), lax.axis_index("y")
    part = tok // n_x

    hidden = jnp.concatenate([teacher_hidden, student_hidden], axis=1)
    quarter = shift(lax.dynamic_slice_in_dim(hidden, x * part, part, 0), "y", 2)
    after, before = shift(hidden, "y", 1), shift(hidden, "y", 3)
    codes_p = shift(teacher_codes, "c", 1)
    weight_p = shift(student_weight, "c", 1)
    scales_p = shift(teacher_scales, "c", 1)
    quarter, codes_p, weight_p, scales_p = lax.optimization_barrier(
        (quarter, codes_p, weight_p, scales_p)
    )
    quarters = jnp.stack([quarter, *(shift(quarter, "x", k) for k in range(1, n_x))])
    opposite = rolled(quarters, n_x - x).reshape(tok, -1)

    table = dequantize(teacher_codes, codes_p, teacher_scales, scales_p)
    weight = jnp.concatenate([student_weight, weight_p])
    turned = weight.T

    t0, s0, stats0 = logits_of(hidden, opposite, table, weight)
    t1, s1, stats1 = logits_of(after, before, table, weight)
    pieces = [stats0[:, :tok], stats1[:, :tok], stats0[:, tok:], stats1[:, tok:]]
    row = lax.broadcasted_iota(jnp.int32, (8, tok), 0)
    pieces[0] = jnp.where(row == 5, loss_scale.astype(F32)[None], pieces[0])
    twice = jnp.concatenate(pieces + pieces[:-1], axis=1)
    mine = lax.dynamic_slice_in_dim(twice, lax.rem(n_y - y, n_y) * tok, n_y * tok, 1)
    seen = to_all(mine, ("x", "y"))
    scales = jnp.sum(seen[:n_y, 5], axis=0)
    totals = combine(to_all(combine(seen), "z"))
    t_lse = totals[0] + jnp.log(totals[1])
    s_lse = totals[3] + jnp.log(totals[4])
    divergence = totals[2] / totals[1] - t_lse + s_lse
    found = jnp.stack([t_lse, s_lse, scales, divergence])
    found = jnp.concatenate([found, jnp.zeros_like(found)])
    found = jnp.concatenate([found, found[:, : (n_y - 1) * tok]], axis=1)
    found = lax.dynamic_slice_in_dim(found, y * tok, n_y * tok, 1)
    kl = found[3, :tok]
    order = [found[:, k * tok : (k + 1) * tok] for k in (0, 2, 1, 3)]
    own, other, blocks = gradients(
        y.astype(jnp.int32)[None],
        jnp.concatenate(order, axis=1),
        ((t0, s0), (t1, s1)),
        turned,
        n_x,
        n_y,
    )
    from_p = shift(other, "c", 1)
    students = jnp.concatenate([p[:, width_t:] for p in (hidden, opposite, after, before)])
    students_p = shift(students, "c", 1)

    blocks = blocks.reshape(n_x * n_y, width_s // n_x, tok)
    got = lax.all_to_all(blocks, ("x", "y"), 0, 0, tiled=True)
    got = jnp.sum(got.astype(F32), axis=0).astype(BF16).reshape(n_z, -1, tok)
    got = lax.all_to_all(got, "z", 0, 0, tiled=True)
    grad_hidden = jnp.sum(got.astype(F32), axis=0).astype(BF16).T

    grad_weight = jnp.dot(own, students, preferred_element_type=F32)
    grad_weight += jnp.dot(from_p, students_p, preferred_element_type=F32)
    return kl, grad_hidden, grad_weight.astype(BF16)


def solution(mesh):
    split = Mesh(mesh.devices.reshape(4, 8, 4, 2), AXES)
    rows = P(("x", "z", "y", "c"), None)
    return jax.shard_map(
        local,
        mesh=split,
        in_specs=(P(DP, None), P(DP, None), rows, rows, rows, P(DP)),
        out_specs=(P(DP), P(DP, VOCAB), rows),
        check_vma=False,
    )
```

```python
import functools

import jax
import jax.numpy as jnp
from jax import lax
from jax.experimental import pallas as pl
from jax.experimental.pallas import tpu as pltpu
from jax.sharding import Mesh
from jax.sharding import PartitionSpec as P

GROUP = 128
AXES = ("x", "z", "y", "c")
DP = ("y", "c")
VOCAB = ("x", "z")
F32, BF16 = jnp.float32, jnp.bfloat16


def shift(a, axis, by):
    n = lax.axis_size(axis)
    return lax.ppermute(a, axis, [((i + by) % n, i) for i in range(n)])


def rolled(blocks, start):
    n = blocks.shape[0]
    return lax.dynamic_slice_in_dim(jnp.concatenate([blocks, blocks[:-1]]), start % n, n, 0)


NT = (((1,), (1,)), ((), ()))
VMEM_LIMIT = 56 * 1024 * 1024
DEQUANT_ROWS = 128
LOGIT_ROWS = 256


def two_sources(i, steps):
    return (jnp.minimum(i, steps - 1), 0), (jnp.maximum(i - steps, 0), 0)


def dequant_kernel(own_steps, own_ref, other_ref, own_scale_ref, other_scale_ref, out_ref):
    def write(codes_ref, scale_ref):
        for g in range(codes_ref.shape[1] // GROUP):
            at = slice(g * GROUP, (g + 1) * GROUP)
            wide = codes_ref[:, at].astype(F32) * scale_ref[:, g : g + 1]
            out_ref[:, at] = wide.astype(BF16)

    @pl.when(pl.program_id(0) < own_steps)
    def _():
        write(own_ref, own_scale_ref)

    @pl.when(pl.program_id(0) >= own_steps)
    def _():
        write(other_ref, other_scale_ref)


def dequantize(codes, codes_p, scales, scales_p):
    rows, width = codes.shape
    steps = rows // DEQUANT_ROWS

    def source(width, k):
        return pl.BlockSpec((DEQUANT_ROWS, width), lambda i: two_sources(i, steps)[k])

    return pl.pallas_call(
        functools.partial(dequant_kernel, steps),
        grid=(2 * steps,),
        in_specs=[
            source(width, 0),
            source(width, 1),
            source(scales.shape[1], 0),
            source(scales.shape[1], 1),
        ],
        out_specs=pl.BlockSpec((DEQUANT_ROWS, width), lambda i: (i, 0)),
        out_shape=jax.ShapeDtypeStruct((2 * rows, width), BF16),
        compiler_params=pltpu.CompilerParams(vmem_limit_bytes=VMEM_LIMIT),
        cost_estimate=pl.CostEstimate(
            flops=2 * rows * width, transcendentals=0, bytes_accessed=8 * rows * width
        ),
        name="dequantize",
    )(codes, codes_p, scales, scales_p)


def turn_kernel(steps, own_ref, other_ref, out_ref):
    @pl.when(pl.program_id(0) < steps)
    def _():
        out_ref[...] = own_ref[...].T

    @pl.when(pl.program_id(0) >= steps)
    def _():
        out_ref[...] = other_ref[...].T


def turned_over(own, other):
    rows, width = own.shape
    steps = rows // DEQUANT_ROWS
    return pl.pallas_call(
        functools.partial(turn_kernel, steps),
        grid=(2 * steps,),
        in_specs=[
            pl.BlockSpec((DEQUANT_ROWS, width), lambda i: two_sources(i, steps)[0]),
            pl.BlockSpec((DEQUANT_ROWS, width), lambda i: two_sources(i, steps)[1]),
        ],
        out_specs=pl.BlockSpec((width, DEQUANT_ROWS), lambda i: (0, i)),
        out_shape=jax.ShapeDtypeStruct((width, 2 * rows), BF16),
        compiler_params=pltpu.CompilerParams(vmem_limit_bytes=VMEM_LIMIT),
        cost_estimate=pl.CostEstimate(
            flops=0, transcendentals=0, bytes_accessed=8 * rows * width
        ),
        name="turn",
    )(own, other)


def logits_tile(pair, table_ref, weight_ref, t_ref, s_ref, stat_ref):
    step = pl.program_id(0)
    width_t = table_ref.shape[1]
    t = lax.dot_general(table_ref[...], pair[:, :width_t], NT, preferred_element_type=F32)
    s = lax.dot_general(weight_ref[...], pair[:, width_t:], NT, preferred_element_type=F32)
    t_ref[...] = t
    s_ref[...] = s
    t_top = jnp.max(t, axis=0, keepdims=True)
    s_top = jnp.max(s, axis=0, keepdims=True)

    def sums(t_top, s_top):
        e = jnp.exp(t - t_top)
        return (
            jnp.sum(e, axis=0, keepdims=True),
            jnp.sum(e * (t - s), axis=0, keepdims=True),
            jnp.sum(jnp.exp(s - s_top), axis=0, keepdims=True),
        )

    @pl.when(step == 0)
    def _():
        total, cross, s_total = sums(t_top, s_top)
        for k, row in enumerate((t_top, total, cross, s_top, s_total)):
            stat_ref[k : k + 1] = row
        stat_ref[5:8] = jnp.zeros((3, t.shape[1]), F32)

    @pl.when(step > 0)
    def _():
        t_old, s_old = stat_ref[0:1], stat_ref[3:4]
        t_new, s_new = jnp.maximum(t_old, t_top), jnp.maximum(s_old, s_top)
        total, cross, s_total = sums(t_new, s_new)
        t_keep, s_keep = jnp.exp(t_old - t_new), jnp.exp(s_old - s_new)
        stat_ref[0:1] = t_new
        stat_ref[1:2] = stat_ref[1:2] * t_keep + total
        stat_ref[2:3] = stat_ref[2:3] * t_keep + cross
        stat_ref[3:4] = s_new
        stat_ref[4:5] = stat_ref[4:5] * s_keep + s_total


def load_pair(x_ref, refs, pair, sem):
    tok, part = refs[0].shape[0], refs[1].shape[0]
    copies = [pltpu.make_async_copy(refs[0], pair.at[pl.ds(0, tok)], sem.at[0])]
    for k, ref in enumerate(refs[1:]):
        at = pl.multiple_of(tok + lax.rem(x_ref[1] + k, tok // part) * part, part)
        copies.append(pltpu.make_async_copy(ref, pair.at[pl.ds(at, part)], sem.at[k + 1]))
    for copy in copies:
        copy.start()
    for copy in copies:
        copy.wait()


def logits_kernel(steps, n_pieces, place_ref, *rest):
    pieces_hbm, rest = rest[:n_pieces], rest[n_pieces:]
    (table_ref, weight_ref, weight_p_ref), rest = rest[:3], rest[3:]
    tok = pieces_hbm[0].shape[0]
    spread = len(rest) > 5
    first_stat_ref, scale_ref = rest[:2] if spread else (None, None)
    rest = rest[2:] if spread else rest
    t_ref, s_ref, stat_ref = rest[:3]
    spread_ref = rest[3] if spread else None
    pair, sem = rest[-2:]
    step = pl.program_id(0)

    @pl.when(step == 0)
    def _():
        load_pair(place_ref, pieces_hbm, pair, sem)

    @pl.when(step < steps)
    def _():
        logits_tile(pair, table_ref, weight_ref, t_ref, s_ref, stat_ref)

    @pl.when(step >= steps)
    def _():
        logits_tile(pair, table_ref, weight_p_ref, t_ref, s_ref, stat_ref)

    if spread:

        @pl.when(step == 2 * steps - 1)
        def _():
            copies, _, wide = spread_ref.shape
            n_y = wide // tok
            row = lax.broadcasted_iota(jnp.int32, (8, tok), 0)
            scale = jnp.broadcast_to(scale_ref[...], (8, tok))
            first, last = first_stat_ref[...], stat_ref[...]
            pieces = (
                jnp.where(row == 5, scale, first[:, :tok]),
                last[:, :tok],
                first[:, tok:],
                last[:, tok:],
            )
            for r, piece in enumerate(pieces):
                at = pl.multiple_of(lax.rem(place_ref[0] + r, n_y) * tok, tok)
                for k in range(copies):
                    spread_ref[k, :, pl.ds(at, tok)] = piece


def logits_of(place, pieces, table, weight, weight_p, first_stats=None, scale=None, copies=0):
    width_t = table.shape[1]
    rows, width_s = weight.shape
    tok = pieces[0].shape[0]
    tokens = 2 * tok
    steps = rows // LOGIT_ROWS
    tile = jax.ShapeDtypeStruct((2 * rows, tokens), F32)

    def source(width, k):
        return pl.BlockSpec((LOGIT_ROWS, width), lambda i, y: two_sources(i, steps)[k])

    in_specs = [
        *[pl.BlockSpec(memory_space=pl.ANY) for _ in pieces],
        pl.BlockSpec((LOGIT_ROWS, width_t), lambda i, y: (i, 0)),
        source(width_s, 0),
        source(width_s, 1),
    ]
    out_specs = [
        pl.BlockSpec((LOGIT_ROWS, tokens), lambda i, y: (i, 0)),
        pl.BlockSpec((LOGIT_ROWS, tokens), lambda i, y: (i, 0)),
        pl.BlockSpec((8, tokens), lambda i, y: (0, 0)),
    ]
    out_shape = [tile, tile, jax.ShapeDtypeStruct((8, tokens), F32)]
    operands = [place, *pieces, table, weight, weight_p]
    if first_stats is not None:
        in_specs.append(pl.BlockSpec((8, tokens), lambda i, y: (0, 0)))
        in_specs.append(pl.BlockSpec((1, tok), lambda i, y: (0, 0)))
        operands += [first_stats, scale]
        out_specs.append(pl.BlockSpec((copies, 8, 2 * tokens), lambda i, y: (0, 0, 0)))
        out_shape.append(jax.ShapeDtypeStruct((copies, 8, 2 * tokens), F32))
    return pl.pallas_call(
        functools.partial(logits_kernel, steps, len(pieces)),
        grid_spec=pltpu.PrefetchScalarGridSpec(
            num_scalar_prefetch=1,
            grid=(2 * steps,),
            in_specs=in_specs,
            out_specs=out_specs,
            scratch_shapes=[
                pltpu.VMEM((tokens, width_t + width_s), BF16),
                pltpu.SemaphoreType.DMA((len(pieces),)),
            ],
        ),
        out_shape=out_shape,
        compiler_params=pltpu.CompilerParams(vmem_limit_bytes=VMEM_LIMIT),
        cost_estimate=pl.CostEstimate(
            flops=4 * rows * tokens * (width_t + width_s),
            transcendentals=4 * rows * tokens,
            bytes_accessed=2 * (2 * rows + tokens) * (width_t + width_s) + 16 * rows * tokens,
        ),
        name="logits",
    )(*operands)


def grad_kernel(y_ref, rows_ref, t0, s0, t1, s1, turned_ref, own_ref, other_ref, out_ref):
    half = own_ref.shape[0]
    n_y, tok = out_ref.shape[1], out_ref.shape[3]

    @pl.when(pl.program_id(0) == 0)
    def _():
        for p, (t, s) in enumerate(((t0, s0), (t1, s1))):
            at = slice(2 * p * tok, 2 * (p + 1) * tok)
            t_lse, s_lse, scale = (rows_ref[k : k + 1, at] for k in range(3))
            for q, ref in enumerate((own_ref, other_ref)):
                rows = slice(q * half, (q + 1) * half)
                gap = jnp.exp(s[rows] - s_lse) - jnp.exp(t[rows] - t_lse)
                ref[:, at] = (scale * gap).astype(BF16)

    total = jnp.dot(turned_ref[:, :half], own_ref[...], preferred_element_type=F32)
    total += jnp.dot(turned_ref[:, half:], other_ref[...], preferred_element_type=F32)
    for k, r in enumerate((0, 2, 1, 3)):
        at = lax.rem(y_ref[0] + r, n_y)
        out_ref[0, at] = total[:, k * tok : (k + 1) * tok].astype(BF16)


def gradients(y, rows, logits, turned, n_x, n_y):
    (t0, s0), (t1, s1) = logits
    vocab, tokens = t0.shape
    width = turned.shape[0]
    lg = jax.ShapeDtypeStruct((vocab // 2, 2 * tokens), BF16)
    whole = pl.BlockSpec((vocab, tokens), lambda i, y: (0, 0))
    lg_spec = pl.BlockSpec((vocab // 2, 2 * tokens), lambda i, y: (0, 0))
    cut = (width // n_x, 2 * tokens // n_y)
    return pl.pallas_call(
        grad_kernel,
        grid_spec=pltpu.PrefetchScalarGridSpec(
            num_scalar_prefetch=1,
            grid=(n_x,),
            in_specs=[
                pl.BlockSpec(rows.shape, lambda i, y: (0, 0)),
                whole,
                whole,
                whole,
                whole,
                pl.BlockSpec((width // n_x, vocab), lambda i, y: (i, 0)),
            ],
            out_specs=[lg_spec, lg_spec, pl.BlockSpec((1, n_y, *cut), lambda i, y: (i, 0, 0, 0))],
        ),
        out_shape=[lg, lg, jax.ShapeDtypeStruct((n_x, n_y, *cut), BF16)],
        compiler_params=pltpu.CompilerParams(vmem_limit_bytes=VMEM_LIMIT),
        cost_estimate=pl.CostEstimate(
            flops=4 * vocab * tokens * width,
            transcendentals=4 * vocab * tokens,
            bytes_accessed=2 * width * (vocab + 2 * tokens) + 20 * vocab * tokens,
        ),
        name="gradients",
    )(y, rows, t0, s0, t1, s1, turned)


def to_all(a, axes):
    n = lax.axis_size(axes)
    return lax.all_to_all(jnp.broadcast_to(a[None], (n, *a.shape)), axes, 0, 0, tiled=True)


def combine(stats):
    teacher_top = jnp.max(stats[:, 0], axis=0)
    student_top = jnp.max(stats[:, 3], axis=0)
    teacher_factor = jnp.exp(stats[:, 0] - teacher_top)
    student_factor = jnp.exp(stats[:, 3] - student_top)
    return jnp.stack(
        [
            teacher_top,
            jnp.sum(stats[:, 1] * teacher_factor, axis=0),
            jnp.sum(stats[:, 2] * teacher_factor, axis=0),
            student_top,
            jnp.sum(stats[:, 4] * student_factor, axis=0),
        ]
    )


def local(
    teacher_hidden, student_hidden, teacher_codes, teacher_scales, student_weight, loss_scale
):
    tok, width_t = teacher_hidden.shape
    width_s = student_hidden.shape[1]
    n_x, n_z, n_y = (lax.axis_size(a) for a in ("x", "z", "y"))
    x, y = lax.axis_index("x"), lax.axis_index("y")
    part = tok // n_x

    place = jnp.stack([y, x]).astype(jnp.int32)
    piece = [
        lax.dynamic_slice_in_dim(a, x * part, part, 0) for a in (teacher_hidden, student_hidden)
    ]
    quarter = shift(jnp.concatenate(piece, axis=1), "y", 2)
    hidden = jnp.concatenate([teacher_hidden, student_hidden], axis=1)
    after, before = shift(hidden, "y", 1), shift(hidden, "y", 3)
    codes_p = shift(teacher_codes, "c", 1)
    weight_p = shift(student_weight, "c", 1)
    scales_p = shift(teacher_scales, "c", 1)
    quarter, codes_p, weight_p, scales_p = lax.optimization_barrier(
        (quarter, codes_p, weight_p, scales_p)
    )
    quarters = [quarter, *(shift(quarter, "x", k) for k in range(1, n_x))]
    table = dequantize(teacher_codes, codes_p, teacher_scales, scales_p)
    turned = turned_over(student_weight, weight_p)

    tables = (table, student_weight, weight_p)
    t0, s0, stats0 = logits_of(place, [hidden, *quarters], *tables)
    after, before, stats0, turned = lax.optimization_barrier((after, before, stats0, turned))
    t1, s1, _, mine = logits_of(
        place,
        [after, before],
        *tables,
        first_stats=stats0,
        scale=loss_scale.astype(F32)[None],
        copies=n_x * n_y,
    )
    opposite_s = rolled(jnp.stack([q[:, width_t:] for q in quarters]), n_x - x).reshape(tok, -1)
    seen = lax.all_to_all(mine, ("x", "y"), 0, 0, tiled=True)
    scales = jnp.sum(seen[:n_y, 5], axis=0)
    totals = combine(to_all(combine(seen), "z"))
    t_lse = totals[0] + jnp.log(totals[1])
    s_lse = totals[3] + jnp.log(totals[4])
    divergence = totals[2] / totals[1] - t_lse + s_lse
    found = jnp.stack([t_lse, s_lse, scales, divergence])
    found = jnp.concatenate([found, jnp.zeros_like(found)])
    found = jnp.concatenate([found, found[:, : (n_y - 1) * tok]], axis=1)
    found = lax.dynamic_slice_in_dim(found, y * tok, n_y * tok, 1)
    kl = found[3, :tok]
    order = [found[:, k * tok : (k + 1) * tok] for k in (0, 2, 1, 3)]
    own, other, blocks = gradients(
        place,
        jnp.concatenate(order, axis=1),
        ((t0, s0), (t1, s1)),
        turned,
        n_x,
        n_y,
    )
    from_p = shift(other, "c", 1)
    students = jnp.concatenate(
        [student_hidden, opposite_s, after[:, width_t:], before[:, width_t:]]
    )
    students_p = shift(students, "c", 1)

    blocks = blocks.reshape(n_x * n_y, width_s // n_x, tok)
    got = lax.all_to_all(blocks, ("x", "y"), 0, 0, tiled=True)
    got = jnp.sum(got.astype(F32), axis=0).astype(BF16).reshape(n_z, -1, tok)
    got = lax.all_to_all(got, "z", 0, 0, tiled=True)
    grad_hidden = jnp.sum(got.astype(F32), axis=0).astype(BF16).T

    grad_weight = jnp.dot(own, students, preferred_element_type=F32)
    grad_weight += jnp.dot(from_p, students_p, preferred_element_type=F32)
    return kl, grad_hidden, grad_weight.astype(BF16)


def solution(mesh):
    split = Mesh(mesh.devices.reshape(4, 8, 4, 2), AXES)
    rows = P(("x", "z", "y", "c"), None)
    return jax.shard_map(
        local,
        mesh=split,
        in_specs=(P(DP, None), P(DP, None), rows, rows, rows, P(DP)),
        out_specs=(P(DP), P(DP, VOCAB), rows),
        check_vma=False,
    )
```

```python
import functools

import jax
import jax.numpy as jnp
from jax import lax
from jax.experimental import pallas as pl
from jax.experimental.pallas import tpu as pltpu
from jax.sharding import Mesh
from jax.sharding import PartitionSpec as P

GROUP = 128
AXES = ("x", "z", "y", "c")
DP = ("y", "c")
VOCAB = ("x", "z")
F32, BF16 = jnp.float32, jnp.bfloat16


def shift(a, axis, by):
    n = lax.axis_size(axis)
    return lax.ppermute(a, axis, [((i + by) % n, i) for i in range(n)])


def rolled(blocks, start):
    n = blocks.shape[0]
    return lax.dynamic_slice_in_dim(jnp.concatenate([blocks, blocks[:-1]]), start % n, n, 0)


NT = (((1,), (1,)), ((), ()))
MIB = 1024 * 1024
DEQUANT_ROWS = 128
LOGIT_ROWS = 256


def two_sources(i, steps):
    return (jnp.minimum(i, steps - 1), 0), (jnp.maximum(i - steps, 0), 0)


def dequant_kernel(own_steps, own_ref, other_ref, own_scale_ref, other_scale_ref, out_ref):
    def write(codes_ref, scale_ref):
        for g in range(codes_ref.shape[1] // GROUP):
            at = slice(g * GROUP, (g + 1) * GROUP)
            wide = codes_ref[:, at].astype(F32) * scale_ref[:, g : g + 1]
            out_ref[:, at] = wide.astype(BF16)

    @pl.when(pl.program_id(0) < own_steps)
    def _():
        write(own_ref, own_scale_ref)

    @pl.when(pl.program_id(0) >= own_steps)
    def _():
        write(other_ref, other_scale_ref)


def dequantize(codes, codes_p, scales, scales_p):
    rows, width = codes.shape
    steps = rows // DEQUANT_ROWS

    def source(width, k):
        return pl.BlockSpec((DEQUANT_ROWS, width), lambda i: two_sources(i, steps)[k])

    return pl.pallas_call(
        functools.partial(dequant_kernel, steps),
        grid=(2 * steps,),
        in_specs=[
            source(width, 0),
            source(width, 1),
            source(scales.shape[1], 0),
            source(scales.shape[1], 1),
        ],
        out_specs=pl.BlockSpec((DEQUANT_ROWS, width), lambda i: (i, 0)),
        out_shape=jax.ShapeDtypeStruct((2 * rows, width), BF16),
        compiler_params=pltpu.CompilerParams(vmem_limit_bytes=12 * MIB),
        cost_estimate=pl.CostEstimate(
            flops=2 * rows * width, transcendentals=0, bytes_accessed=8 * rows * width
        ),
        name="dequantize",
    )(codes, codes_p, scales, scales_p)


def turn_kernel(steps, own_ref, other_ref, out_ref):
    @pl.when(pl.program_id(0) < steps)
    def _():
        out_ref[...] = own_ref[...].T

    @pl.when(pl.program_id(0) >= steps)
    def _():
        out_ref[...] = other_ref[...].T


def turned_over(own, other):
    rows, width = own.shape
    steps = rows // DEQUANT_ROWS
    return pl.pallas_call(
        functools.partial(turn_kernel, steps),
        grid=(2 * steps,),
        in_specs=[
            pl.BlockSpec((DEQUANT_ROWS, width), lambda i: two_sources(i, steps)[0]),
            pl.BlockSpec((DEQUANT_ROWS, width), lambda i: two_sources(i, steps)[1]),
        ],
        out_specs=pl.BlockSpec((width, DEQUANT_ROWS), lambda i: (0, i)),
        out_shape=jax.ShapeDtypeStruct((width, 2 * rows), BF16),
        compiler_params=pltpu.CompilerParams(vmem_limit_bytes=8 * MIB),
        cost_estimate=pl.CostEstimate(
            flops=0, transcendentals=0, bytes_accessed=8 * rows * width
        ),
        name="turn",
    )(own, other)


def logits_tile(pair, table_ref, weight_ref, t_ref, s_ref, stat_ref):
    step = pl.program_id(0)
    width_t = table_ref.shape[1]
    t = lax.dot_general(table_ref[...], pair[:, :width_t], NT, preferred_element_type=F32)
    s = lax.dot_general(weight_ref[...], pair[:, width_t:], NT, preferred_element_type=F32)
    t_ref[...] = t
    s_ref[...] = s
    t_top = jnp.max(t, axis=0, keepdims=True)
    s_top = jnp.max(s, axis=0, keepdims=True)

    def sums(t_top, s_top):
        e = jnp.exp(t - t_top)
        return (
            jnp.sum(e, axis=0, keepdims=True),
            jnp.sum(e * (t - s), axis=0, keepdims=True),
            jnp.sum(jnp.exp(s - s_top), axis=0, keepdims=True),
        )

    @pl.when(step == 0)
    def _():
        total, cross, s_total = sums(t_top, s_top)
        for k, row in enumerate((t_top, total, cross, s_top, s_total)):
            stat_ref[k : k + 1] = row
        stat_ref[5:8] = jnp.zeros((3, t.shape[1]), F32)

    @pl.when(step > 0)
    def _():
        t_old, s_old = stat_ref[0:1], stat_ref[3:4]
        t_new, s_new = jnp.maximum(t_old, t_top), jnp.maximum(s_old, s_top)
        total, cross, s_total = sums(t_new, s_new)
        t_keep, s_keep = jnp.exp(t_old - t_new), jnp.exp(s_old - s_new)
        stat_ref[0:1] = t_new
        stat_ref[1:2] = stat_ref[1:2] * t_keep + total
        stat_ref[2:3] = stat_ref[2:3] * t_keep + cross
        stat_ref[3:4] = s_new
        stat_ref[4:5] = stat_ref[4:5] * s_keep + s_total


def load_pair(x_ref, refs, pair, sem):
    tok, part = refs[0].shape[0], refs[1].shape[0]
    copies = [pltpu.make_async_copy(refs[0], pair.at[pl.ds(0, tok)], sem.at[0])]
    for k, ref in enumerate(refs[1:]):
        at = pl.multiple_of(tok + lax.rem(x_ref[1] + k, tok // part) * part, part)
        copies.append(pltpu.make_async_copy(ref, pair.at[pl.ds(at, part)], sem.at[k + 1]))
    for copy in copies:
        copy.start()
    for copy in copies:
        copy.wait()


def logits_kernel(steps, n_pieces, place_ref, *rest):
    pieces_hbm, rest = rest[:n_pieces], rest[n_pieces:]
    (table_ref, weight_ref, weight_p_ref), rest = rest[:3], rest[3:]
    tok = pieces_hbm[0].shape[0]
    spread = len(rest) > 5
    first_stat_ref, scale_ref = rest[:2] if spread else (None, None)
    rest = rest[2:] if spread else rest
    t_ref, s_ref, stat_ref = rest[:3]
    spread_ref = rest[3] if spread else None
    pair, sem = rest[-2:]
    step = pl.program_id(0)

    @pl.when(step == 0)
    def _():
        load_pair(place_ref, pieces_hbm, pair, sem)

    @pl.when(step < steps)
    def _():
        logits_tile(pair, table_ref, weight_ref, t_ref, s_ref, stat_ref)

    @pl.when(step >= steps)
    def _():
        logits_tile(pair, table_ref, weight_p_ref, t_ref, s_ref, stat_ref)

    if spread:

        @pl.when(step == 2 * steps - 1)
        def _():
            copies, _, wide = spread_ref.shape
            n_y = wide // tok
            row = lax.broadcasted_iota(jnp.int32, (8, tok), 0)
            scale = jnp.broadcast_to(scale_ref[...], (8, tok))
            first, last = first_stat_ref[...], stat_ref[...]
            pieces = (
                jnp.where(row == 5, scale, first[:, :tok]),
                last[:, :tok],
                first[:, tok:],
                last[:, tok:],
            )
            for r, piece in enumerate(pieces):
                at = pl.multiple_of(lax.rem(place_ref[0] + r, n_y) * tok, tok)
                for k in range(copies):
                    spread_ref[k, :, pl.ds(at, tok)] = piece


def logits_of(place, pieces, table, weight, weight_p, first_stats=None, scale=None, copies=0):
    width_t = table.shape[1]
    rows, width_s = weight.shape
    tok = pieces[0].shape[0]
    tokens = 2 * tok
    steps = rows // LOGIT_ROWS
    tile = jax.ShapeDtypeStruct((2 * rows, tokens), F32)

    def source(width, k):
        return pl.BlockSpec((LOGIT_ROWS, width), lambda i, y: two_sources(i, steps)[k])

    in_specs = [
        *[pl.BlockSpec(memory_space=pl.ANY) for _ in pieces],
        pl.BlockSpec((LOGIT_ROWS, width_t), lambda i, y: (i, 0)),
        source(width_s, 0),
        source(width_s, 1),
    ]
    out_specs = [
        pl.BlockSpec((LOGIT_ROWS, tokens), lambda i, y: (i, 0)),
        pl.BlockSpec((LOGIT_ROWS, tokens), lambda i, y: (i, 0)),
        pl.BlockSpec((8, tokens), lambda i, y: (0, 0)),
    ]
    out_shape = [tile, tile, jax.ShapeDtypeStruct((8, tokens), F32)]
    operands = [place, *pieces, table, weight, weight_p]
    if first_stats is not None:
        in_specs.append(pl.BlockSpec((8, tokens), lambda i, y: (0, 0)))
        in_specs.append(pl.BlockSpec((1, tok), lambda i, y: (0, 0)))
        operands += [first_stats, scale]
        out_specs.append(pl.BlockSpec((copies, 8, 2 * tokens), lambda i, y: (0, 0, 0)))
        out_shape.append(jax.ShapeDtypeStruct((copies, 8, 2 * tokens), F32))
    return pl.pallas_call(
        functools.partial(logits_kernel, steps, len(pieces)),
        grid_spec=pltpu.PrefetchScalarGridSpec(
            num_scalar_prefetch=1,
            grid=(2 * steps,),
            in_specs=in_specs,
            out_specs=out_specs,
            scratch_shapes=[
                pltpu.VMEM((tokens, width_t + width_s), BF16),
                pltpu.SemaphoreType.DMA((len(pieces),)),
            ],
        ),
        out_shape=out_shape,
        compiler_params=pltpu.CompilerParams(vmem_limit_bytes=22 * MIB),
        cost_estimate=pl.CostEstimate(
            flops=4 * rows * tokens * (width_t + width_s),
            transcendentals=4 * rows * tokens,
            bytes_accessed=2 * (2 * rows + tokens) * (width_t + width_s) + 16 * rows * tokens,
        ),
        name="logits",
    )(*operands)


def grad_kernel(y_ref, rows_ref, t0, s0, t1, s1, turned_ref, own_ref, other_ref, out_ref):
    half = own_ref.shape[0]
    n_y, tok = out_ref.shape[1], out_ref.shape[3]

    @pl.when(pl.program_id(0) == 0)
    def _():
        for p, (t, s) in enumerate(((t0, s0), (t1, s1))):
            at = slice(2 * p * tok, 2 * (p + 1) * tok)
            t_lse, s_lse, scale = (rows_ref[k : k + 1, at] for k in range(3))
            for q, ref in enumerate((own_ref, other_ref)):
                rows = slice(q * half, (q + 1) * half)
                gap = jnp.exp(s[rows] - s_lse) - jnp.exp(t[rows] - t_lse)
                ref[:, at] = (scale * gap).astype(BF16)

    total = jnp.dot(turned_ref[:, :half], own_ref[...], preferred_element_type=F32)
    total += jnp.dot(turned_ref[:, half:], other_ref[...], preferred_element_type=F32)
    for k, r in enumerate((0, 2, 1, 3)):
        at = lax.rem(y_ref[0] + r, n_y)
        out_ref[0, at] = total[:, k * tok : (k + 1) * tok].astype(BF16)


def gradients(y, rows, logits, turned, n_x, n_y):
    (t0, s0), (t1, s1) = logits
    vocab, tokens = t0.shape
    width = turned.shape[0]
    lg = jax.ShapeDtypeStruct((vocab // 2, 2 * tokens), BF16)
    whole = pl.BlockSpec((vocab, tokens), lambda i, y: (0, 0))
    lg_spec = pl.BlockSpec((vocab // 2, 2 * tokens), lambda i, y: (0, 0))
    cut = (width // n_x, 2 * tokens // n_y)
    return pl.pallas_call(
        grad_kernel,
        grid_spec=pltpu.PrefetchScalarGridSpec(
            num_scalar_prefetch=1,
            grid=(n_x,),
            in_specs=[
                pl.BlockSpec(rows.shape, lambda i, y: (0, 0)),
                whole,
                whole,
                whole,
                whole,
                pl.BlockSpec((width // n_x, vocab), lambda i, y: (i, 0)),
            ],
            out_specs=[lg_spec, lg_spec, pl.BlockSpec((1, n_y, *cut), lambda i, y: (i, 0, 0, 0))],
        ),
        out_shape=[lg, lg, jax.ShapeDtypeStruct((n_x, n_y, *cut), BF16)],
        compiler_params=pltpu.CompilerParams(vmem_limit_bytes=22 * MIB),
        cost_estimate=pl.CostEstimate(
            flops=4 * vocab * tokens * width,
            transcendentals=4 * vocab * tokens,
            bytes_accessed=2 * width * (vocab + 2 * tokens) + 20 * vocab * tokens,
        ),
        name="gradients",
    )(y, rows, t0, s0, t1, s1, turned)


def to_all(a, axes):
    n = lax.axis_size(axes)
    return lax.all_to_all(jnp.broadcast_to(a[None], (n, *a.shape)), axes, 0, 0, tiled=True)


def combine(stats):
    teacher_top = jnp.max(stats[:, 0], axis=0)
    student_top = jnp.max(stats[:, 3], axis=0)
    teacher_factor = jnp.exp(stats[:, 0] - teacher_top)
    student_factor = jnp.exp(stats[:, 3] - student_top)
    return jnp.stack(
        [
            teacher_top,
            jnp.sum(stats[:, 1] * teacher_factor, axis=0),
            jnp.sum(stats[:, 2] * teacher_factor, axis=0),
            student_top,
            jnp.sum(stats[:, 4] * student_factor, axis=0),
        ]
    )


def local(
    teacher_hidden, student_hidden, teacher_codes, teacher_scales, student_weight, loss_scale
):
    tok, width_t = teacher_hidden.shape
    width_s = student_hidden.shape[1]
    n_x, n_z, n_y = (lax.axis_size(a) for a in ("x", "z", "y"))
    x, y = lax.axis_index("x"), lax.axis_index("y")
    part = tok // n_x

    place = jnp.stack([y, x]).astype(jnp.int32)
    piece = [
        lax.dynamic_slice_in_dim(a, x * part, part, 0) for a in (teacher_hidden, student_hidden)
    ]
    quarter = shift(jnp.concatenate(piece, axis=1), "y", 2)
    hidden = jnp.concatenate([teacher_hidden, student_hidden], axis=1)
    after, before = shift(hidden, "y", 1), shift(hidden, "y", 3)
    codes_p = shift(teacher_codes, "c", 1)
    weight_p = shift(student_weight, "c", 1)
    scales_p = shift(teacher_scales, "c", 1)
    quarter, codes_p, weight_p, scales_p = lax.optimization_barrier(
        (quarter, codes_p, weight_p, scales_p)
    )
    quarters = [quarter, *(shift(quarter, "x", k) for k in range(1, n_x))]
    table = dequantize(teacher_codes, codes_p, teacher_scales, scales_p)
    turned = turned_over(student_weight, weight_p)

    tables = (table, student_weight, weight_p)
    t0, s0, stats0 = logits_of(place, [hidden, *quarters], *tables)
    after, before, stats0, turned = lax.optimization_barrier((after, before, stats0, turned))
    t1, s1, _, mine = logits_of(
        place,
        [after, before],
        *tables,
        first_stats=stats0,
        scale=loss_scale.astype(F32)[None],
        copies=n_x * n_y,
    )
    mine, after, before, quarters = lax.optimization_barrier((mine, after, before, quarters))
    opposite_s = rolled(jnp.stack([q[:, width_t:] for q in quarters]), n_x - x).reshape(tok, -1)
    seen = lax.all_to_all(mine, ("x", "y"), 0, 0, tiled=True)
    scales = jnp.sum(seen[:n_y, 5], axis=0)
    totals = combine(to_all(combine(seen), "z"))
    t_lse = totals[0] + jnp.log(totals[1])
    s_lse = totals[3] + jnp.log(totals[4])
    divergence = totals[2] / totals[1] - t_lse + s_lse
    found = jnp.stack([t_lse, s_lse, scales, divergence])
    found = jnp.concatenate([found, jnp.zeros_like(found)])
    found = jnp.concatenate([found, found[:, : (n_y - 1) * tok]], axis=1)
    found = lax.dynamic_slice_in_dim(found, y * tok, n_y * tok, 1)
    kl = found[3, :tok]
    order = [found[:, k * tok : (k + 1) * tok] for k in (0, 2, 1, 3)]
    own, other, blocks = gradients(
        place,
        jnp.concatenate(order, axis=1),
        ((t0, s0), (t1, s1)),
        turned,
        n_x,
        n_y,
    )
    from_p = shift(other, "c", 1)
    students = jnp.concatenate(
        [student_hidden, opposite_s, after[:, width_t:], before[:, width_t:]]
    )
    students_p = shift(students, "c", 1)

    blocks = blocks.reshape(n_x * n_y, width_s // n_x, tok)
    got = lax.all_to_all(blocks, ("x", "y"), 0, 0, tiled=True)
    got = jnp.sum(got.astype(F32), axis=0).astype(BF16).reshape(n_z, -1, tok)
    got = lax.all_to_all(got, "z", 0, 0, tiled=True)
    grad_hidden = jnp.sum(got.astype(F32), axis=0).astype(BF16).T

    grad_weight = jnp.dot(own, students, preferred_element_type=F32)
    grad_weight += jnp.dot(from_p, students_p, preferred_element_type=F32)
    return kl, grad_hidden, grad_weight.astype(BF16)


def solution(mesh):
    split = Mesh(mesh.devices.reshape(4, 8, 4, 2), AXES)
    rows = P(("x", "z", "y", "c"), None)
    return jax.shard_map(
        local,
        mesh=split,
        in_specs=(P(DP, None), P(DP, None), rows, rows, rows, P(DP)),
        out_specs=(P(DP), P(DP, VOCAB), rows),
        check_vma=False,
    )
```

```python
import functools

import jax
import jax.numpy as jnp
from jax import lax
from jax.experimental import pallas as pl
from jax.experimental.pallas import tpu as pltpu
from jax.sharding import Mesh
from jax.sharding import PartitionSpec as P

GROUP = 128
AXES = ("x", "z", "y", "c")
DP = ("y", "c")
VOCAB = ("x", "z")
F32, BF16 = jnp.float32, jnp.bfloat16


def shift(a, axis, by):
    n = lax.axis_size(axis)
    return lax.ppermute(a, axis, [((i + by) % n, i) for i in range(n)])


def rolled(blocks, start):
    n = blocks.shape[0]
    return lax.dynamic_slice_in_dim(jnp.concatenate([blocks, blocks[:-1]]), start % n, n, 0)


NT = (((1,), (1,)), ((), ()))
MIB = 1024 * 1024
DEQUANT_ROWS = 128
LOGIT_ROWS = 256
WEIGHT_COLUMNS = 512


def two_sources(i, steps):
    return (jnp.minimum(i, steps - 1), 0), (jnp.maximum(i - steps, 0), 0)


def dequant_kernel(own_steps, own_ref, other_ref, own_scale_ref, other_scale_ref, out_ref):
    def write(codes_ref, scale_ref):
        for g in range(codes_ref.shape[1] // GROUP):
            at = slice(g * GROUP, (g + 1) * GROUP)
            wide = codes_ref[:, at].astype(F32) * scale_ref[:, g : g + 1]
            out_ref[:, at] = wide.astype(BF16)

    @pl.when(pl.program_id(0) < own_steps)
    def _():
        write(own_ref, own_scale_ref)

    @pl.when(pl.program_id(0) >= own_steps)
    def _():
        write(other_ref, other_scale_ref)


def dequantize(codes, codes_p, scales, scales_p):
    rows, width = codes.shape
    steps = rows // DEQUANT_ROWS

    def source(width, k):
        return pl.BlockSpec((DEQUANT_ROWS, width), lambda i: two_sources(i, steps)[k])

    return pl.pallas_call(
        functools.partial(dequant_kernel, steps),
        grid=(2 * steps,),
        in_specs=[
            source(width, 0),
            source(width, 1),
            source(scales.shape[1], 0),
            source(scales.shape[1], 1),
        ],
        out_specs=pl.BlockSpec((DEQUANT_ROWS, width), lambda i: (i, 0)),
        out_shape=jax.ShapeDtypeStruct((2 * rows, width), BF16),
        compiler_params=pltpu.CompilerParams(vmem_limit_bytes=12 * MIB),
        cost_estimate=pl.CostEstimate(
            flops=2 * rows * width, transcendentals=0, bytes_accessed=8 * rows * width
        ),
        name="dequantize",
    )(codes, codes_p, scales, scales_p)


def turn_kernel(steps, own_ref, other_ref, out_ref):
    @pl.when(pl.program_id(0) < steps)
    def _():
        out_ref[...] = own_ref[...].T

    @pl.when(pl.program_id(0) >= steps)
    def _():
        out_ref[...] = other_ref[...].T


def turned_over(own, other):
    rows, width = own.shape
    steps = rows // DEQUANT_ROWS
    return pl.pallas_call(
        functools.partial(turn_kernel, steps),
        grid=(2 * steps,),
        in_specs=[
            pl.BlockSpec((DEQUANT_ROWS, width), lambda i: two_sources(i, steps)[0]),
            pl.BlockSpec((DEQUANT_ROWS, width), lambda i: two_sources(i, steps)[1]),
        ],
        out_specs=pl.BlockSpec((width, DEQUANT_ROWS), lambda i: (0, i)),
        out_shape=jax.ShapeDtypeStruct((width, 2 * rows), BF16),
        compiler_params=pltpu.CompilerParams(vmem_limit_bytes=8 * MIB),
        cost_estimate=pl.CostEstimate(
            flops=0, transcendentals=0, bytes_accessed=8 * rows * width
        ),
        name="turn",
    )(own, other)


def logits_tile(pair, table_ref, weight_ref, t_ref, s_ref, stat_ref):
    step = pl.program_id(0)
    width_t = table_ref.shape[1]
    t = lax.dot_general(table_ref[...], pair[:, :width_t], NT, preferred_element_type=F32)
    s = lax.dot_general(weight_ref[...], pair[:, width_t:], NT, preferred_element_type=F32)
    t_ref[...] = t
    s_ref[...] = s
    t_top = jnp.max(t, axis=0, keepdims=True)
    s_top = jnp.max(s, axis=0, keepdims=True)

    def sums(t_top, s_top):
        e = jnp.exp(t - t_top)
        return (
            jnp.sum(e, axis=0, keepdims=True),
            jnp.sum(e * (t - s), axis=0, keepdims=True),
            jnp.sum(jnp.exp(s - s_top), axis=0, keepdims=True),
        )

    @pl.when(step == 0)
    def _():
        total, cross, s_total = sums(t_top, s_top)
        for k, row in enumerate((t_top, total, cross, s_top, s_total)):
            stat_ref[k : k + 1] = row
        stat_ref[5:8] = jnp.zeros((3, t.shape[1]), F32)

    @pl.when(step > 0)
    def _():
        t_old, s_old = stat_ref[0:1], stat_ref[3:4]
        t_new, s_new = jnp.maximum(t_old, t_top), jnp.maximum(s_old, s_top)
        total, cross, s_total = sums(t_new, s_new)
        t_keep, s_keep = jnp.exp(t_old - t_new), jnp.exp(s_old - s_new)
        stat_ref[0:1] = t_new
        stat_ref[1:2] = stat_ref[1:2] * t_keep + total
        stat_ref[2:3] = stat_ref[2:3] * t_keep + cross
        stat_ref[3:4] = s_new
        stat_ref[4:5] = stat_ref[4:5] * s_keep + s_total


def load_pair(x_ref, refs, pair, sem):
    tok, part = refs[0].shape[0], refs[1].shape[0]
    copies = [pltpu.make_async_copy(refs[0], pair.at[pl.ds(0, tok)], sem.at[0])]
    for k, ref in enumerate(refs[1:]):
        at = pl.multiple_of(tok + lax.rem(x_ref[1] + k, tok // part) * part, part)
        copies.append(pltpu.make_async_copy(ref, pair.at[pl.ds(at, part)], sem.at[k + 1]))
    for copy in copies:
        copy.start()
    for copy in copies:
        copy.wait()


def logits_kernel(steps, n_pieces, place_ref, *rest):
    pieces_hbm, rest = rest[:n_pieces], rest[n_pieces:]
    (table_ref, weight_ref, weight_p_ref), rest = rest[:3], rest[3:]
    tok = pieces_hbm[0].shape[0]
    spread = len(rest) > 6
    first_stat_ref, scale_ref = rest[:2] if spread else (None, None)
    rest = rest[2:] if spread else rest
    t_ref, s_ref, stat_ref, student_ref = rest[:4]
    spread_ref = rest[4] if spread else None
    pair, sem = rest[-2:]
    step = pl.program_id(0)

    @pl.when(step == 0)
    def _():
        load_pair(place_ref, pieces_hbm, pair, sem)
        student_ref[...] = pair[:, table_ref.shape[1] :]

    @pl.when(step < steps)
    def _():
        logits_tile(pair, table_ref, weight_ref, t_ref, s_ref, stat_ref)

    @pl.when(step >= steps)
    def _():
        logits_tile(pair, table_ref, weight_p_ref, t_ref, s_ref, stat_ref)

    if spread:

        @pl.when(step == 2 * steps - 1)
        def _():
            copies, _, wide = spread_ref.shape
            n_y = wide // tok
            row = lax.broadcasted_iota(jnp.int32, (8, tok), 0)
            scale = jnp.broadcast_to(scale_ref[...], (8, tok))
            first, last = first_stat_ref[...], stat_ref[...]
            pieces = (
                jnp.where(row == 5, scale, first[:, :tok]),
                last[:, :tok],
                first[:, tok:],
                last[:, tok:],
            )
            for r, piece in enumerate(pieces):
                at = pl.multiple_of(lax.rem(place_ref[0] + r, n_y) * tok, tok)
                for k in range(copies):
                    spread_ref[k, :, pl.ds(at, tok)] = piece


def logits_of(place, pieces, table, weight, weight_p, first_stats=None, scale=None, copies=0):
    width_t = table.shape[1]
    rows, width_s = weight.shape
    tok = pieces[0].shape[0]
    tokens = 2 * tok
    steps = rows // LOGIT_ROWS
    tile = jax.ShapeDtypeStruct((2 * rows, tokens), F32)

    def source(width, k):
        return pl.BlockSpec((LOGIT_ROWS, width), lambda i, y: two_sources(i, steps)[k])

    in_specs = [
        *[pl.BlockSpec(memory_space=pl.ANY) for _ in pieces],
        pl.BlockSpec((LOGIT_ROWS, width_t), lambda i, y: (i, 0)),
        source(width_s, 0),
        source(width_s, 1),
    ]
    out_specs = [
        pl.BlockSpec((LOGIT_ROWS, tokens), lambda i, y: (i, 0)),
        pl.BlockSpec((LOGIT_ROWS, tokens), lambda i, y: (i, 0)),
        pl.BlockSpec((8, tokens), lambda i, y: (0, 0)),
        pl.BlockSpec((tokens, width_s), lambda i, y: (0, 0)),
    ]
    out_shape = [
        tile,
        tile,
        jax.ShapeDtypeStruct((8, tokens), F32),
        jax.ShapeDtypeStruct((tokens, width_s), BF16),
    ]
    operands = [place, *pieces, table, weight, weight_p]
    if first_stats is not None:
        in_specs.append(pl.BlockSpec((8, tokens), lambda i, y: (0, 0)))
        in_specs.append(pl.BlockSpec((1, tok), lambda i, y: (0, 0)))
        operands += [first_stats, scale]
        out_specs.append(pl.BlockSpec((copies, 8, 2 * tokens), lambda i, y: (0, 0, 0)))
        out_shape.append(jax.ShapeDtypeStruct((copies, 8, 2 * tokens), F32))
    return pl.pallas_call(
        functools.partial(logits_kernel, steps, len(pieces)),
        grid_spec=pltpu.PrefetchScalarGridSpec(
            num_scalar_prefetch=1,
            grid=(2 * steps,),
            in_specs=in_specs,
            out_specs=out_specs,
            scratch_shapes=[
                pltpu.VMEM((tokens, width_t + width_s), BF16),
                pltpu.SemaphoreType.DMA((len(pieces),)),
            ],
        ),
        out_shape=out_shape,
        compiler_params=pltpu.CompilerParams(vmem_limit_bytes=22 * MIB),
        cost_estimate=pl.CostEstimate(
            flops=4 * rows * tokens * (width_t + width_s),
            transcendentals=4 * rows * tokens,
            bytes_accessed=2 * (2 * rows + tokens) * (width_t + width_s) + 16 * rows * tokens,
        ),
        name="logits",
    )(*operands)


def grad_kernel(y_ref, rows_ref, t0, s0, t1, s1, turned_ref, own_ref, other_ref, out_ref):
    half = own_ref.shape[0]
    n_y, tok = out_ref.shape[1], out_ref.shape[3]

    @pl.when(pl.program_id(0) == 0)
    def _():
        for p, (t, s) in enumerate(((t0, s0), (t1, s1))):
            at = slice(2 * p * tok, 2 * (p + 1) * tok)
            t_lse, s_lse, scale = (rows_ref[k : k + 1, at] for k in range(3))
            for q, ref in enumerate((own_ref, other_ref)):
                rows = slice(q * half, (q + 1) * half)
                gap = jnp.exp(s[rows] - s_lse) - jnp.exp(t[rows] - t_lse)
                ref[:, at] = (scale * gap).astype(BF16)

    total = jnp.dot(turned_ref[:, :half], own_ref[...], preferred_element_type=F32)
    total += jnp.dot(turned_ref[:, half:], other_ref[...], preferred_element_type=F32)
    for k, r in enumerate((0, 2, 1, 3)):
        at = lax.rem(y_ref[0] + r, n_y)
        out_ref[0, at] = total[:, k * tok : (k + 1) * tok].astype(BF16)


def gradients(y, rows, logits, turned, n_x, n_y):
    (t0, s0), (t1, s1) = logits
    vocab, tokens = t0.shape
    width = turned.shape[0]
    lg = jax.ShapeDtypeStruct((vocab // 2, 2 * tokens), BF16)
    whole = pl.BlockSpec((vocab, tokens), lambda i, y: (0, 0))
    lg_spec = pl.BlockSpec((vocab // 2, 2 * tokens), lambda i, y: (0, 0))
    cut = (width // n_x, 2 * tokens // n_y)
    return pl.pallas_call(
        grad_kernel,
        grid_spec=pltpu.PrefetchScalarGridSpec(
            num_scalar_prefetch=1,
            grid=(n_x,),
            in_specs=[
                pl.BlockSpec(rows.shape, lambda i, y: (0, 0)),
                whole,
                whole,
                whole,
                whole,
                pl.BlockSpec((width // n_x, vocab), lambda i, y: (i, 0)),
            ],
            out_specs=[lg_spec, lg_spec, pl.BlockSpec((1, n_y, *cut), lambda i, y: (i, 0, 0, 0))],
        ),
        out_shape=[lg, lg, jax.ShapeDtypeStruct((n_x, n_y, *cut), BF16)],
        compiler_params=pltpu.CompilerParams(vmem_limit_bytes=22 * MIB),
        cost_estimate=pl.CostEstimate(
            flops=4 * vocab * tokens * width,
            transcendentals=4 * vocab * tokens,
            bytes_accessed=2 * width * (vocab + 2 * tokens) + 20 * vocab * tokens,
        ),
        name="gradients",
    )(y, rows, t0, s0, t1, s1, turned)


def to_all(a, axes):
    n = lax.axis_size(axes)
    return lax.all_to_all(jnp.broadcast_to(a[None], (n, *a.shape)), axes, 0, 0, tiled=True)


def combine(stats):
    teacher_top = jnp.max(stats[:, 0], axis=0)
    student_top = jnp.max(stats[:, 3], axis=0)
    teacher_factor = jnp.exp(stats[:, 0] - teacher_top)
    student_factor = jnp.exp(stats[:, 3] - student_top)
    return jnp.stack(
        [
            teacher_top,
            jnp.sum(stats[:, 1] * teacher_factor, axis=0),
            jnp.sum(stats[:, 2] * teacher_factor, axis=0),
            student_top,
            jnp.sum(stats[:, 4] * student_factor, axis=0),
        ]
    )


def weight_kernel(own_ref, from_ref, s0_ref, s1_ref, s0_p_ref, s1_p_ref, out_ref):
    half = s0_ref.shape[0]
    total = jnp.dot(own_ref[:, :half], s0_ref[...], preferred_element_type=F32)
    total += jnp.dot(own_ref[:, half:], s1_ref[...], preferred_element_type=F32)
    total += jnp.dot(from_ref[:, :half], s0_p_ref[...], preferred_element_type=F32)
    total += jnp.dot(from_ref[:, half:], s1_p_ref[...], preferred_element_type=F32)
    out_ref[...] = total.astype(BF16)


def weight_gradient(own, from_p, *students):
    rows, tokens = own.shape
    half, width = students[0].shape
    whole = pl.BlockSpec((rows, tokens), lambda i: (0, 0))
    return pl.pallas_call(
        weight_kernel,
        grid=(width // WEIGHT_COLUMNS,),
        in_specs=[whole, whole] + [pl.BlockSpec((half, WEIGHT_COLUMNS), lambda i: (0, i))] * 4,
        out_specs=pl.BlockSpec((rows, WEIGHT_COLUMNS), lambda i: (0, i)),
        out_shape=jax.ShapeDtypeStruct((rows, width), BF16),
        compiler_params=pltpu.CompilerParams(vmem_limit_bytes=14 * MIB),
        cost_estimate=pl.CostEstimate(
            flops=4 * rows * tokens * width,
            transcendentals=0,
            bytes_accessed=2 * width * (rows + 4 * half) + 4 * rows * tokens,
        ),
        name="weight_gradient",
    )(own, from_p, *students)


def local(
    teacher_hidden, student_hidden, teacher_codes, teacher_scales, student_weight, loss_scale
):
    tok, width_t = teacher_hidden.shape
    width_s = student_hidden.shape[1]
    n_x, n_z, n_y = (lax.axis_size(a) for a in ("x", "z", "y"))
    x, y = lax.axis_index("x"), lax.axis_index("y")
    part = tok // n_x

    place = jnp.stack([y, x]).astype(jnp.int32)
    piece = [
        lax.dynamic_slice_in_dim(a, x * part, part, 0) for a in (teacher_hidden, student_hidden)
    ]
    quarter = shift(jnp.concatenate(piece, axis=1), "y", 2)
    hidden = jnp.concatenate([teacher_hidden, student_hidden], axis=1)
    quarter, whole = lax.optimization_barrier((quarter, hidden))
    after, before = shift(whole, "y", 1), shift(whole, "y", 3)
    codes_p = shift(teacher_codes, "c", 1)
    weight_p = shift(student_weight, "c", 1)
    scales_p = shift(teacher_scales, "c", 1)
    quarter, codes_p, weight_p, scales_p = lax.optimization_barrier(
        (quarter, codes_p, weight_p, scales_p)
    )
    quarters = [quarter, *(shift(quarter, "x", k) for k in range(1, n_x))]
    table = dequantize(teacher_codes, codes_p, teacher_scales, scales_p)
    turned = turned_over(student_weight, weight_p)

    tables = (table, student_weight, weight_p)
    t0, s0, stats0, students0 = logits_of(place, [hidden, *quarters], *tables)
    after, before, stats0, turned = lax.optimization_barrier((after, before, stats0, turned))
    students0_p = shift(students0, "c", 1)
    t1, s1, _, students1, mine = logits_of(
        place,
        [after, before],
        *tables,
        first_stats=stats0,
        scale=loss_scale.astype(F32)[None],
        copies=n_x * n_y,
    )
    seen = lax.all_to_all(mine, ("x", "y"), 0, 0, tiled=True)
    scales = jnp.sum(seen[:n_y, 5], axis=0)
    totals = combine(to_all(combine(seen), "z"))
    t_lse = totals[0] + jnp.log(totals[1])
    s_lse = totals[3] + jnp.log(totals[4])
    divergence = totals[2] / totals[1] - t_lse + s_lse
    found = jnp.stack([t_lse, s_lse, scales, divergence])
    found = jnp.concatenate([found, jnp.zeros_like(found)])
    found = jnp.concatenate([found, found[:, : (n_y - 1) * tok]], axis=1)
    found = lax.dynamic_slice_in_dim(found, y * tok, n_y * tok, 1)
    kl = found[3, :tok]
    order = [found[:, k * tok : (k + 1) * tok] for k in (0, 2, 1, 3)]
    own, other, blocks = gradients(
        place,
        jnp.concatenate(order, axis=1),
        ((t0, s0), (t1, s1)),
        turned,
        n_x,
        n_y,
    )
    from_p = shift(other, "c", 1)
    students1_p = shift(students1, "c", 1)
    grad_weight = weight_gradient(own, from_p, students0, students1, students0_p, students1_p)

    blocks = blocks.reshape(n_x * n_y, width_s // n_x, tok)
    got = lax.all_to_all(blocks, ("x", "y"), 0, 0, tiled=True)
    got = jnp.sum(got.astype(F32), axis=0).astype(BF16).reshape(n_z, -1, tok)
    got = lax.all_to_all(got, "z", 0, 0, tiled=True)
    grad_hidden = jnp.sum(got.astype(F32), axis=0).astype(BF16).T

    return kl, grad_hidden, grad_weight


def solution(mesh):
    split = Mesh(mesh.devices.reshape(4, 8, 4, 2), AXES)
    rows = P(("x", "z", "y", "c"), None)
    return jax.shard_map(
        local,
        mesh=split,
        in_specs=(P(DP, None), P(DP, None), rows, rows, rows, P(DP)),
        out_specs=(P(DP), P(DP, VOCAB), rows),
        check_vma=False,
    )
```

```python
import functools

import jax
import jax.numpy as jnp
from jax import lax
from jax.experimental import pallas as pl
from jax.experimental.pallas import tpu as pltpu
from jax.sharding import Mesh
from jax.sharding import PartitionSpec as P

GROUP = 128
AXES = ("x", "z", "y", "c")
DP = ("y", "c")
VOCAB = ("x", "z")
F32, BF16 = jnp.float32, jnp.bfloat16


def shift(a, axis, by):
    n = lax.axis_size(axis)
    return lax.ppermute(a, axis, [((i + by) % n, i) for i in range(n)])


def rolled(blocks, start):
    n = blocks.shape[0]
    return lax.dynamic_slice_in_dim(jnp.concatenate([blocks, blocks[:-1]]), start % n, n, 0)


NT = (((1,), (1,)), ((), ()))
MIB = 1024 * 1024
DEQUANT_ROWS = 128
LOGIT_ROWS = 256
WEIGHT_COLUMNS = 512


def two_sources(i, steps):
    return (jnp.minimum(i, steps - 1), 0), (jnp.maximum(i - steps, 0), 0)


def dequant_kernel(own_steps, own_ref, other_ref, own_scale_ref, other_scale_ref, out_ref):
    def write(codes_ref, scale_ref):
        for g in range(codes_ref.shape[1] // GROUP):
            at = slice(g * GROUP, (g + 1) * GROUP)
            wide = codes_ref[:, at].astype(F32) * scale_ref[:, g : g + 1]
            out_ref[:, at] = wide.astype(BF16)

    @pl.when(pl.program_id(0) < own_steps)
    def _():
        write(own_ref, own_scale_ref)

    @pl.when(pl.program_id(0) >= own_steps)
    def _():
        write(other_ref, other_scale_ref)


def dequantize(codes, codes_p, scales, scales_p):
    rows, width = codes.shape
    steps = rows // DEQUANT_ROWS

    def source(width, k):
        return pl.BlockSpec((DEQUANT_ROWS, width), lambda i: two_sources(i, steps)[k])

    return pl.pallas_call(
        functools.partial(dequant_kernel, steps),
        grid=(2 * steps,),
        in_specs=[
            source(width, 0),
            source(width, 1),
            source(scales.shape[1], 0),
            source(scales.shape[1], 1),
        ],
        out_specs=pl.BlockSpec((DEQUANT_ROWS, width), lambda i: (i, 0)),
        out_shape=jax.ShapeDtypeStruct((2 * rows, width), BF16),
        compiler_params=pltpu.CompilerParams(vmem_limit_bytes=12 * MIB),
        cost_estimate=pl.CostEstimate(
            flops=2 * rows * width, transcendentals=0, bytes_accessed=8 * rows * width
        ),
        name="dequantize",
    )(codes, codes_p, scales, scales_p)


def turn_kernel(steps, own_ref, other_ref, out_ref):
    @pl.when(pl.program_id(0) < steps)
    def _():
        out_ref[...] = own_ref[...].T

    @pl.when(pl.program_id(0) >= steps)
    def _():
        out_ref[...] = other_ref[...].T


def turned_over(own, other):
    rows, width = own.shape
    steps = rows // DEQUANT_ROWS
    return pl.pallas_call(
        functools.partial(turn_kernel, steps),
        grid=(2 * steps,),
        in_specs=[
            pl.BlockSpec((DEQUANT_ROWS, width), lambda i: two_sources(i, steps)[0]),
            pl.BlockSpec((DEQUANT_ROWS, width), lambda i: two_sources(i, steps)[1]),
        ],
        out_specs=pl.BlockSpec((width, DEQUANT_ROWS), lambda i: (0, i)),
        out_shape=pltpu.HBM((width, 2 * rows), BF16),
        compiler_params=pltpu.CompilerParams(vmem_limit_bytes=8 * MIB),
        cost_estimate=pl.CostEstimate(
            flops=0, transcendentals=0, bytes_accessed=8 * rows * width
        ),
        name="turn",
    )(own, other)


def logits_tile(pair, table_ref, weight_ref, t_ref, s_ref, stat_ref):
    step = pl.program_id(0)
    width_t = table_ref.shape[1]
    t = lax.dot_general(table_ref[...], pair[:, :width_t], NT, preferred_element_type=F32)
    s = lax.dot_general(weight_ref[...], pair[:, width_t:], NT, preferred_element_type=F32)
    t_ref[...] = t
    s_ref[...] = s
    t_top = jnp.max(t, axis=0, keepdims=True)
    s_top = jnp.max(s, axis=0, keepdims=True)

    def sums(t_top, s_top):
        e = jnp.exp(t - t_top)
        return (
            jnp.sum(e, axis=0, keepdims=True),
            jnp.sum(e * (t - s), axis=0, keepdims=True),
            jnp.sum(jnp.exp(s - s_top), axis=0, keepdims=True),
        )

    @pl.when(step == 0)
    def _():
        total, cross, s_total = sums(t_top, s_top)
        for k, row in enumerate((t_top, total, cross, s_top, s_total)):
            stat_ref[k : k + 1] = row
        stat_ref[5:8] = jnp.zeros((3, t.shape[1]), F32)

    @pl.when(step > 0)
    def _():
        t_old, s_old = stat_ref[0:1], stat_ref[3:4]
        t_new, s_new = jnp.maximum(t_old, t_top), jnp.maximum(s_old, s_top)
        total, cross, s_total = sums(t_new, s_new)
        t_keep, s_keep = jnp.exp(t_old - t_new), jnp.exp(s_old - s_new)
        stat_ref[0:1] = t_new
        stat_ref[1:2] = stat_ref[1:2] * t_keep + total
        stat_ref[2:3] = stat_ref[2:3] * t_keep + cross
        stat_ref[3:4] = s_new
        stat_ref[4:5] = stat_ref[4:5] * s_keep + s_total


def load_pair(x_ref, refs, pair, sem):
    tok, part = refs[0].shape[0], refs[1].shape[0]
    copies = [pltpu.make_async_copy(refs[0], pair.at[pl.ds(0, tok)], sem.at[0])]
    for k, ref in enumerate(refs[1:]):
        at = pl.multiple_of(tok + lax.rem(x_ref[1] + k, tok // part) * part, part)
        copies.append(pltpu.make_async_copy(ref, pair.at[pl.ds(at, part)], sem.at[k + 1]))
    for copy in copies:
        copy.start()
    for copy in copies:
        copy.wait()


def logits_kernel(steps, n_pieces, place_ref, *rest):
    pieces_hbm, rest = rest[:n_pieces], rest[n_pieces:]
    (table_ref, weight_ref, weight_p_ref), rest = rest[:3], rest[3:]
    tok = pieces_hbm[0].shape[0]
    spread = len(rest) > 6
    first_stat_ref, scale_ref = rest[:2] if spread else (None, None)
    rest = rest[2:] if spread else rest
    t_ref, s_ref, stat_ref, student_ref = rest[:4]
    spread_ref = rest[4] if spread else None
    pair, sem = rest[-2:]
    step = pl.program_id(0)

    @pl.when(step == 0)
    def _():
        load_pair(place_ref, pieces_hbm, pair, sem)
        student_ref[...] = pair[:, table_ref.shape[1] :]

    @pl.when(step < steps)
    def _():
        logits_tile(pair, table_ref, weight_ref, t_ref, s_ref, stat_ref)

    @pl.when(step >= steps)
    def _():
        logits_tile(pair, table_ref, weight_p_ref, t_ref, s_ref, stat_ref)

    if spread:

        @pl.when(step == 2 * steps - 1)
        def _():
            copies, _, wide = spread_ref.shape
            n_y = wide // tok
            row = lax.broadcasted_iota(jnp.int32, (8, tok), 0)
            scale = jnp.broadcast_to(scale_ref[...], (8, tok))
            first, last = first_stat_ref[...], stat_ref[...]
            pieces = (
                jnp.where(row == 5, scale, first[:, :tok]),
                last[:, :tok],
                first[:, tok:],
                last[:, tok:],
            )
            for r, piece in enumerate(pieces):
                at = pl.multiple_of(lax.rem(place_ref[0] + r, n_y) * tok, tok)
                for k in range(copies):
                    spread_ref[k, :, pl.ds(at, tok)] = piece


def logits_of(place, pieces, table, weight, weight_p, first_stats=None, scale=None, copies=0):
    width_t = table.shape[1]
    rows, width_s = weight.shape
    tok = pieces[0].shape[0]
    tokens = 2 * tok
    steps = rows // LOGIT_ROWS
    tile = pltpu.HBM((2 * rows, tokens), F32)

    def source(width, k):
        return pl.BlockSpec((LOGIT_ROWS, width), lambda i, y: two_sources(i, steps)[k])

    in_specs = [
        *[pl.BlockSpec(memory_space=pl.ANY) for _ in pieces],
        pl.BlockSpec((LOGIT_ROWS, width_t), lambda i, y: (i, 0)),
        source(width_s, 0),
        source(width_s, 1),
    ]
    out_specs = [
        pl.BlockSpec((LOGIT_ROWS, tokens), lambda i, y: (i, 0)),
        pl.BlockSpec((LOGIT_ROWS, tokens), lambda i, y: (i, 0)),
        pl.BlockSpec((8, tokens), lambda i, y: (0, 0)),
        pl.BlockSpec((tokens, width_s), lambda i, y: (0, 0)),
    ]
    out_shape = [
        tile,
        tile,
        jax.ShapeDtypeStruct((8, tokens), F32),
        pltpu.HBM((tokens, width_s), BF16),
    ]
    operands = [place, *pieces, table, weight, weight_p]
    if first_stats is not None:
        in_specs.append(pl.BlockSpec((8, tokens), lambda i, y: (0, 0)))
        in_specs.append(pl.BlockSpec((1, tok), lambda i, y: (0, 0)))
        operands += [first_stats, scale]
        out_specs.append(pl.BlockSpec((copies, 8, 2 * tokens), lambda i, y: (0, 0, 0)))
        out_shape.append(jax.ShapeDtypeStruct((copies, 8, 2 * tokens), F32))
    return pl.pallas_call(
        functools.partial(logits_kernel, steps, len(pieces)),
        grid_spec=pltpu.PrefetchScalarGridSpec(
            num_scalar_prefetch=1,
            grid=(2 * steps,),
            in_specs=in_specs,
            out_specs=out_specs,
            scratch_shapes=[
                pltpu.VMEM((tokens, width_t + width_s), BF16),
                pltpu.SemaphoreType.DMA((len(pieces),)),
            ],
        ),
        out_shape=out_shape,
        compiler_params=pltpu.CompilerParams(vmem_limit_bytes=22 * MIB),
        cost_estimate=pl.CostEstimate(
            flops=4 * rows * tokens * (width_t + width_s),
            transcendentals=4 * rows * tokens,
            bytes_accessed=2 * (2 * rows + tokens) * (width_t + width_s) + 16 * rows * tokens,
        ),
        name="logits",
    )(*operands)


def grad_kernel(y_ref, rows_ref, t0, s0, t1, s1, turned_ref, own_ref, other_ref, out_ref):
    half = own_ref.shape[0]
    n_y, tok = out_ref.shape[1], out_ref.shape[3]

    @pl.when(pl.program_id(0) == 0)
    def _():
        for p, (t, s) in enumerate(((t0, s0), (t1, s1))):
            at = slice(2 * p * tok, 2 * (p + 1) * tok)
            t_lse, s_lse, scale = (rows_ref[k : k + 1, at] for k in range(3))
            for q, ref in enumerate((own_ref, other_ref)):
                rows = slice(q * half, (q + 1) * half)
                gap = jnp.exp(s[rows] - s_lse) - jnp.exp(t[rows] - t_lse)
                ref[:, at] = (scale * gap).astype(BF16)

    total = jnp.dot(turned_ref[:, :half], own_ref[...], preferred_element_type=F32)
    total += jnp.dot(turned_ref[:, half:], other_ref[...], preferred_element_type=F32)
    for k, r in enumerate((0, 2, 1, 3)):
        at = lax.rem(y_ref[0] + r, n_y)
        out_ref[0, at] = total[:, k * tok : (k + 1) * tok].astype(BF16)


def gradients(y, rows, logits, turned, n_x, n_y):
    (t0, s0), (t1, s1) = logits
    vocab, tokens = t0.shape
    width = turned.shape[0]
    lg = pltpu.HBM((vocab // 2, 2 * tokens), BF16)
    whole = pl.BlockSpec((vocab, tokens), lambda i, y: (0, 0))
    lg_spec = pl.BlockSpec((vocab // 2, 2 * tokens), lambda i, y: (0, 0))
    cut = (width // n_x, 2 * tokens // n_y)
    return pl.pallas_call(
        grad_kernel,
        grid_spec=pltpu.PrefetchScalarGridSpec(
            num_scalar_prefetch=1,
            grid=(n_x,),
            in_specs=[
                pl.BlockSpec(rows.shape, lambda i, y: (0, 0)),
                whole,
                whole,
                whole,
                whole,
                pl.BlockSpec((width // n_x, vocab), lambda i, y: (i, 0)),
            ],
            out_specs=[lg_spec, lg_spec, pl.BlockSpec((1, n_y, *cut), lambda i, y: (i, 0, 0, 0))],
        ),
        out_shape=[lg, lg, pltpu.HBM((n_x, n_y, *cut), BF16)],
        compiler_params=pltpu.CompilerParams(vmem_limit_bytes=56 * MIB),
        cost_estimate=pl.CostEstimate(
            flops=4 * vocab * tokens * width,
            transcendentals=4 * vocab * tokens,
            bytes_accessed=2 * width * (vocab + 2 * tokens) + 20 * vocab * tokens,
        ),
        name="gradients",
    )(y, rows, t0, s0, t1, s1, turned)


def to_all(a, axes):
    n = lax.axis_size(axes)
    return lax.all_to_all(jnp.broadcast_to(a[None], (n, *a.shape)), axes, 0, 0, tiled=True)


def combine(stats):
    teacher_top = jnp.max(stats[:, 0], axis=0)
    student_top = jnp.max(stats[:, 3], axis=0)
    teacher_factor = jnp.exp(stats[:, 0] - teacher_top)
    student_factor = jnp.exp(stats[:, 3] - student_top)
    return jnp.stack(
        [
            teacher_top,
            jnp.sum(stats[:, 1] * teacher_factor, axis=0),
            jnp.sum(stats[:, 2] * teacher_factor, axis=0),
            student_top,
            jnp.sum(stats[:, 4] * student_factor, axis=0),
        ]
    )


def weight_kernel(own_ref, from_ref, s0_ref, s1_ref, s0_p_ref, s1_p_ref, out_ref):
    half = s0_ref.shape[0]
    total = jnp.dot(own_ref[:, :half], s0_ref[...], preferred_element_type=F32)
    total += jnp.dot(own_ref[:, half:], s1_ref[...], preferred_element_type=F32)
    total += jnp.dot(from_ref[:, :half], s0_p_ref[...], preferred_element_type=F32)
    total += jnp.dot(from_ref[:, half:], s1_p_ref[...], preferred_element_type=F32)
    out_ref[...] = total.astype(BF16)


def weight_gradient(own, from_p, *students):
    rows, tokens = own.shape
    half, width = students[0].shape
    whole = pl.BlockSpec((rows, tokens), lambda i: (0, 0))
    return pl.pallas_call(
        weight_kernel,
        grid=(width // WEIGHT_COLUMNS,),
        in_specs=[whole, whole] + [pl.BlockSpec((half, WEIGHT_COLUMNS), lambda i: (0, i))] * 4,
        out_specs=pl.BlockSpec((rows, WEIGHT_COLUMNS), lambda i: (0, i)),
        out_shape=jax.ShapeDtypeStruct((rows, width), BF16),
        compiler_params=pltpu.CompilerParams(vmem_limit_bytes=56 * MIB),
        cost_estimate=pl.CostEstimate(
            flops=4 * rows * tokens * width,
            transcendentals=0,
            bytes_accessed=2 * width * (rows + 4 * half) + 4 * rows * tokens,
        ),
        name="weight_gradient",
    )(own, from_p, *students)


def local(
    teacher_hidden, student_hidden, teacher_codes, teacher_scales, student_weight, loss_scale
):
    tok, width_t = teacher_hidden.shape
    width_s = student_hidden.shape[1]
    n_x, n_z, n_y = (lax.axis_size(a) for a in ("x", "z", "y"))
    x, y = lax.axis_index("x"), lax.axis_index("y")
    part = tok // n_x

    place = jnp.stack([y, x]).astype(jnp.int32)
    piece = [
        lax.dynamic_slice_in_dim(a, x * part, part, 0) for a in (teacher_hidden, student_hidden)
    ]
    quarter = shift(jnp.concatenate(piece, axis=1), "y", 2)
    hidden = jnp.concatenate([teacher_hidden, student_hidden], axis=1)
    quarter, whole = lax.optimization_barrier((quarter, hidden))
    after, before = shift(whole, "y", 1), shift(whole, "y", 3)
    codes_p = shift(teacher_codes, "c", 1)
    weight_p = shift(student_weight, "c", 1)
    scales_p = shift(teacher_scales, "c", 1)
    quarter, codes_p, weight_p, scales_p = lax.optimization_barrier(
        (quarter, codes_p, weight_p, scales_p)
    )
    quarters = [quarter, *(shift(quarter, "x", k) for k in range(1, n_x))]
    table = dequantize(teacher_codes, codes_p, teacher_scales, scales_p)
    turned = turned_over(student_weight, weight_p)

    tables = (table, student_weight, weight_p)
    t0, s0, stats0, students0 = logits_of(place, [hidden, *quarters], *tables)
    after, before, stats0, turned = lax.optimization_barrier((after, before, stats0, turned))
    students0_p = shift(students0, "c", 1)
    t1, s1, _, students1, mine = logits_of(
        place,
        [after, before],
        *tables,
        first_stats=stats0,
        scale=loss_scale.astype(F32)[None],
        copies=n_x * n_y,
    )
    seen = lax.all_to_all(mine, ("x", "y"), 0, 0, tiled=True)
    scales = jnp.sum(seen[:n_y, 5], axis=0)
    totals = combine(to_all(combine(seen), "z"))
    t_lse = totals[0] + jnp.log(totals[1])
    s_lse = totals[3] + jnp.log(totals[4])
    divergence = totals[2] / totals[1] - t_lse + s_lse
    found = jnp.stack([t_lse, s_lse, scales, divergence])
    found = jnp.concatenate([found, jnp.zeros_like(found)])
    found = jnp.concatenate([found, found[:, : (n_y - 1) * tok]], axis=1)
    found = lax.dynamic_slice_in_dim(found, y * tok, n_y * tok, 1)
    kl = found[3, :tok]
    order = [found[:, k * tok : (k + 1) * tok] for k in (0, 2, 1, 3)]
    own, other, blocks = gradients(
        place,
        jnp.concatenate(order, axis=1),
        ((t0, s0), (t1, s1)),
        turned,
        n_x,
        n_y,
    )
    from_p = shift(other, "c", 1)
    students1_p = shift(students1, "c", 1)
    grad_weight = weight_gradient(own, from_p, students0, students1, students0_p, students1_p)

    blocks = blocks.reshape(n_x * n_y, width_s // n_x, tok)
    got = lax.all_to_all(blocks, ("x", "y"), 0, 0, tiled=True)
    got = jnp.sum(got.astype(F32), axis=0).astype(BF16).reshape(n_z, -1, tok)
    got = lax.all_to_all(got, "z", 0, 0, tiled=True)
    grad_hidden = jnp.sum(got.astype(F32), axis=0).astype(BF16).T

    return kl, grad_hidden, grad_weight


def solution(mesh):
    split = Mesh(mesh.devices.reshape(4, 8, 4, 2), AXES)
    rows = P(("x", "z", "y", "c"), None)
    return jax.shard_map(
        local,
        mesh=split,
        in_specs=(P(DP, None), P(DP, None), rows, rows, rows, P(DP)),
        out_specs=(P(DP), P(DP, VOCAB), rows),
        check_vma=False,
    )
```

```python
import functools

import jax
import jax.numpy as jnp
from jax import lax
from jax.experimental import pallas as pl
from jax.experimental.pallas import tpu as pltpu
from jax.sharding import Mesh
from jax.sharding import PartitionSpec as P

GROUP = 128
AXES = ("x", "z", "y", "c")
DP = ("y", "c")
VOCAB = ("x", "z")
F32, BF16 = jnp.float32, jnp.bfloat16


def shift(a, axis, by):
    n = lax.axis_size(axis)
    return lax.ppermute(a, axis, [((i + by) % n, i) for i in range(n)])


def rolled(blocks, start):
    n = blocks.shape[0]
    return lax.dynamic_slice_in_dim(jnp.concatenate([blocks, blocks[:-1]]), start % n, n, 0)


NT = (((1,), (1,)), ((), ()))
MIB = 1024 * 1024
DEQUANT_ROWS = 128
LOGIT_ROWS = 256
WEIGHT_COLUMNS = 512


def two_sources(i, steps):
    return (jnp.minimum(i, steps - 1), 0), (jnp.maximum(i - steps, 0), 0)


def dequant_kernel(own_steps, own_ref, other_ref, own_scale_ref, other_scale_ref, out_ref):
    def write(codes_ref, scale_ref):
        for g in range(codes_ref.shape[1] // GROUP):
            at = slice(g * GROUP, (g + 1) * GROUP)
            wide = codes_ref[:, at].astype(F32) * scale_ref[:, g : g + 1]
            out_ref[:, at] = wide.astype(BF16)

    @pl.when(pl.program_id(0) < own_steps)
    def _():
        write(own_ref, own_scale_ref)

    @pl.when(pl.program_id(0) >= own_steps)
    def _():
        write(other_ref, other_scale_ref)


def dequantize(codes, codes_p, scales, scales_p):
    rows, width = codes.shape
    steps = rows // DEQUANT_ROWS

    def source(width, k):
        return pl.BlockSpec((DEQUANT_ROWS, width), lambda i: two_sources(i, steps)[k])

    return pl.pallas_call(
        functools.partial(dequant_kernel, steps),
        grid=(2 * steps,),
        in_specs=[
            source(width, 0),
            source(width, 1),
            source(scales.shape[1], 0),
            source(scales.shape[1], 1),
        ],
        out_specs=pl.BlockSpec((DEQUANT_ROWS, width), lambda i: (i, 0)),
        out_shape=jax.ShapeDtypeStruct((2 * rows, width), BF16),
        compiler_params=pltpu.CompilerParams(vmem_limit_bytes=12 * MIB),
        cost_estimate=pl.CostEstimate(
            flops=2 * rows * width, transcendentals=0, bytes_accessed=8 * rows * width
        ),
        name="dequantize",
    )(codes, codes_p, scales, scales_p)


def turn_kernel(steps, own_ref, other_ref, out_ref):
    @pl.when(pl.program_id(0) < steps)
    def _():
        out_ref[...] = own_ref[...].T

    @pl.when(pl.program_id(0) >= steps)
    def _():
        out_ref[...] = other_ref[...].T


def turned_over(own, other):
    rows, width = own.shape
    steps = rows // DEQUANT_ROWS
    return pl.pallas_call(
        functools.partial(turn_kernel, steps),
        grid=(2 * steps,),
        in_specs=[
            pl.BlockSpec((DEQUANT_ROWS, width), lambda i: two_sources(i, steps)[0]),
            pl.BlockSpec((DEQUANT_ROWS, width), lambda i: two_sources(i, steps)[1]),
        ],
        out_specs=pl.BlockSpec((width, DEQUANT_ROWS), lambda i: (0, i)),
        out_shape=pltpu.HBM((width, 2 * rows), BF16),
        compiler_params=pltpu.CompilerParams(vmem_limit_bytes=8 * MIB),
        cost_estimate=pl.CostEstimate(
            flops=0, transcendentals=0, bytes_accessed=8 * rows * width
        ),
        name="turn",
    )(own, other)


def logits_tile(pair, table_ref, weight_ref, t_ref, s_ref, stat_ref):
    step = pl.program_id(0)
    width_t = table_ref.shape[1]
    t = lax.dot_general(table_ref[...], pair[:, :width_t], NT, preferred_element_type=F32)
    s = lax.dot_general(weight_ref[...], pair[:, width_t:], NT, preferred_element_type=F32)
    t_ref[...] = t
    s_ref[...] = s
    t_top = jnp.max(t, axis=0, keepdims=True)
    s_top = jnp.max(s, axis=0, keepdims=True)

    def sums(t_top, s_top):
        e = jnp.exp(t - t_top)
        return (
            jnp.sum(e, axis=0, keepdims=True),
            jnp.sum(e * (t - s), axis=0, keepdims=True),
            jnp.sum(jnp.exp(s - s_top), axis=0, keepdims=True),
        )

    @pl.when(step == 0)
    def _():
        total, cross, s_total = sums(t_top, s_top)
        for k, row in enumerate((t_top, total, cross, s_top, s_total)):
            stat_ref[k : k + 1] = row
        stat_ref[5:8] = jnp.zeros((3, t.shape[1]), F32)

    @pl.when(step > 0)
    def _():
        t_old, s_old = stat_ref[0:1], stat_ref[3:4]
        t_new, s_new = jnp.maximum(t_old, t_top), jnp.maximum(s_old, s_top)
        total, cross, s_total = sums(t_new, s_new)
        t_keep, s_keep = jnp.exp(t_old - t_new), jnp.exp(s_old - s_new)
        stat_ref[0:1] = t_new
        stat_ref[1:2] = stat_ref[1:2] * t_keep + total
        stat_ref[2:3] = stat_ref[2:3] * t_keep + cross
        stat_ref[3:4] = s_new
        stat_ref[4:5] = stat_ref[4:5] * s_keep + s_total


def load_pair(x_ref, refs, pair, sem):
    tok, part = refs[0].shape[0], refs[1].shape[0]
    copies = [pltpu.make_async_copy(refs[0], pair.at[pl.ds(0, tok)], sem.at[0])]
    for k, ref in enumerate(refs[1:]):
        at = pl.multiple_of(tok + lax.rem(x_ref[1] + k, tok // part) * part, part)
        copies.append(pltpu.make_async_copy(ref, pair.at[pl.ds(at, part)], sem.at[k + 1]))
    for copy in copies:
        copy.start()
    for copy in copies:
        copy.wait()


def logits_kernel(steps, n_pieces, place_ref, *rest):
    pieces_hbm, rest = rest[:n_pieces], rest[n_pieces:]
    (table_ref, weight_ref, weight_p_ref), rest = rest[:3], rest[3:]
    tok = pieces_hbm[0].shape[0]
    spread = len(rest) > 6
    first_stat_ref, scale_ref = rest[:2] if spread else (None, None)
    rest = rest[2:] if spread else rest
    t_ref, s_ref, stat_ref, student_ref = rest[:4]
    spread_ref = rest[4] if spread else None
    pair, sem = rest[-2:]
    step = pl.program_id(0)

    @pl.when(step == 0)
    def _():
        load_pair(place_ref, pieces_hbm, pair, sem)
        student_ref[...] = pair[:, table_ref.shape[1] :]

    @pl.when(step < steps)
    def _():
        logits_tile(pair, table_ref, weight_ref, t_ref, s_ref, stat_ref)

    @pl.when(step >= steps)
    def _():
        logits_tile(pair, table_ref, weight_p_ref, t_ref, s_ref, stat_ref)

    if spread:

        @pl.when(step == 2 * steps - 1)
        def _():
            copies, _, wide = spread_ref.shape
            n_y = wide // tok
            row = lax.broadcasted_iota(jnp.int32, (8, tok), 0)
            scale = jnp.broadcast_to(scale_ref[...], (8, tok))
            first, last = first_stat_ref[...], stat_ref[...]
            pieces = (
                jnp.where(row == 5, scale, first[:, :tok]),
                last[:, :tok],
                first[:, tok:],
                last[:, tok:],
            )
            for r, piece in enumerate(pieces):
                at = pl.multiple_of(lax.rem(place_ref[0] + r, n_y) * tok, tok)
                for k in range(copies):
                    spread_ref[k, :, pl.ds(at, tok)] = piece


def logits_of(place, pieces, table, weight, weight_p, first_stats=None, scale=None, copies=0):
    width_t = table.shape[1]
    rows, width_s = weight.shape
    tok = pieces[0].shape[0]
    tokens = 2 * tok
    steps = rows // LOGIT_ROWS
    tile = pltpu.HBM((2 * rows, tokens), F32)

    def source(width, k):
        return pl.BlockSpec((LOGIT_ROWS, width), lambda i, y: two_sources(i, steps)[k])

    in_specs = [
        *[pl.BlockSpec(memory_space=pl.ANY) for _ in pieces],
        pl.BlockSpec((LOGIT_ROWS, width_t), lambda i, y: (i, 0)),
        source(width_s, 0),
        source(width_s, 1),
    ]
    out_specs = [
        pl.BlockSpec((LOGIT_ROWS, tokens), lambda i, y: (i, 0)),
        pl.BlockSpec((LOGIT_ROWS, tokens), lambda i, y: (i, 0)),
        pl.BlockSpec((8, tokens), lambda i, y: (0, 0)),
        pl.BlockSpec((tokens, width_s), lambda i, y: (0, 0)),
    ]
    out_shape = [
        tile,
        tile,
        jax.ShapeDtypeStruct((8, tokens), F32),
        pltpu.HBM((tokens, width_s), BF16),
    ]
    operands = [place, *pieces, table, weight, weight_p]
    if first_stats is not None:
        in_specs.append(pl.BlockSpec((8, tokens), lambda i, y: (0, 0)))
        in_specs.append(pl.BlockSpec((1, tok), lambda i, y: (0, 0)))
        operands += [first_stats, scale]
        out_specs.append(pl.BlockSpec((copies, 8, 2 * tokens), lambda i, y: (0, 0, 0)))
        out_shape.append(jax.ShapeDtypeStruct((copies, 8, 2 * tokens), F32))
    return pl.pallas_call(
        functools.partial(logits_kernel, steps, len(pieces)),
        grid_spec=pltpu.PrefetchScalarGridSpec(
            num_scalar_prefetch=1,
            grid=(2 * steps,),
            in_specs=in_specs,
            out_specs=out_specs,
            scratch_shapes=[
                pltpu.VMEM((tokens, width_t + width_s), BF16),
                pltpu.SemaphoreType.DMA((len(pieces),)),
            ],
        ),
        out_shape=out_shape,
        compiler_params=pltpu.CompilerParams(vmem_limit_bytes=22 * MIB),
        cost_estimate=pl.CostEstimate(
            flops=4 * rows * tokens * (width_t + width_s),
            transcendentals=4 * rows * tokens,
            bytes_accessed=2 * (2 * rows + tokens) * (width_t + width_s) + 16 * rows * tokens,
        ),
        name="logits",
    )(*operands)


def grad_kernel(y_ref, rows_ref, t0, s0, t1, s1, turned_ref, own_ref, other_ref, out_ref):
    half = own_ref.shape[0]
    n_y, tok = out_ref.shape[1], out_ref.shape[3]

    @pl.when(pl.program_id(0) == 0)
    def _():
        for p, (t, s) in enumerate(((t0, s0), (t1, s1))):
            at = slice(2 * p * tok, 2 * (p + 1) * tok)
            t_lse, s_lse, scale = (rows_ref[k : k + 1, at] for k in range(3))
            for q, ref in enumerate((own_ref, other_ref)):
                rows = slice(q * half, (q + 1) * half)
                gap = jnp.exp(s[rows] - s_lse) - jnp.exp(t[rows] - t_lse)
                ref[:, at] = (scale * gap).astype(BF16)

    total = jnp.dot(turned_ref[:, :half], own_ref[...], preferred_element_type=F32)
    total += jnp.dot(turned_ref[:, half:], other_ref[...], preferred_element_type=F32)
    for k, r in enumerate((0, 2, 1, 3)):
        at = lax.rem(y_ref[0] + r, n_y)
        out_ref[0, at] = total[:, k * tok : (k + 1) * tok].astype(BF16)


def gradients(y, rows, logits, turned, n_x, n_y):
    (t0, s0), (t1, s1) = logits
    vocab, tokens = t0.shape
    width = turned.shape[0]
    lg = pltpu.HBM((vocab // 2, 2 * tokens), BF16)
    whole = pl.BlockSpec((vocab, tokens), lambda i, y: (0, 0))
    lg_spec = pl.BlockSpec((vocab // 2, 2 * tokens), lambda i, y: (0, 0))
    cut = (width // n_x, 2 * tokens // n_y)
    return pl.pallas_call(
        grad_kernel,
        grid_spec=pltpu.PrefetchScalarGridSpec(
            num_scalar_prefetch=1,
            grid=(n_x,),
            in_specs=[
                pl.BlockSpec(rows.shape, lambda i, y: (0, 0)),
                whole,
                whole,
                whole,
                whole,
                pl.BlockSpec((width // n_x, vocab), lambda i, y: (i, 0)),
            ],
            out_specs=[lg_spec, lg_spec, pl.BlockSpec((1, n_y, *cut), lambda i, y: (i, 0, 0, 0))],
        ),
        out_shape=[lg, lg, pltpu.HBM((n_x, n_y, *cut), BF16)],
        compiler_params=pltpu.CompilerParams(vmem_limit_bytes=56 * MIB),
        cost_estimate=pl.CostEstimate(
            flops=4 * vocab * tokens * width,
            transcendentals=4 * vocab * tokens,
            bytes_accessed=2 * width * (vocab + 2 * tokens) + 20 * vocab * tokens,
        ),
        name="gradients",
    )(y, rows, t0, s0, t1, s1, turned)


def to_all(a, axes):
    n = lax.axis_size(axes)
    return lax.all_to_all(jnp.broadcast_to(a[None], (n, *a.shape)), axes, 0, 0, tiled=True)


def combine(stats):
    teacher_top = jnp.max(stats[:, 0], axis=0)
    student_top = jnp.max(stats[:, 3], axis=0)
    teacher_factor = jnp.exp(stats[:, 0] - teacher_top)
    student_factor = jnp.exp(stats[:, 3] - student_top)
    return jnp.stack(
        [
            teacher_top,
            jnp.sum(stats[:, 1] * teacher_factor, axis=0),
            jnp.sum(stats[:, 2] * teacher_factor, axis=0),
            student_top,
            jnp.sum(stats[:, 4] * student_factor, axis=0),
        ]
    )


def weight_kernel(own_ref, from_ref, s0_ref, s1_ref, s0_p_ref, s1_p_ref, out_ref):
    half = s0_ref.shape[0]
    total = jnp.dot(own_ref[:, :half], s0_ref[...], preferred_element_type=F32)
    total += jnp.dot(own_ref[:, half:], s1_ref[...], preferred_element_type=F32)
    total += jnp.dot(from_ref[:, :half], s0_p_ref[...], preferred_element_type=F32)
    total += jnp.dot(from_ref[:, half:], s1_p_ref[...], preferred_element_type=F32)
    out_ref[...] = total.astype(BF16)


def weight_gradient(own, from_p, *students):
    rows, tokens = own.shape
    half, width = students[0].shape
    whole = pl.BlockSpec((rows, tokens), lambda i: (0, 0))
    return pl.pallas_call(
        weight_kernel,
        grid=(width // WEIGHT_COLUMNS,),
        in_specs=[whole, whole] + [pl.BlockSpec((half, WEIGHT_COLUMNS), lambda i: (0, i))] * 4,
        out_specs=pl.BlockSpec((rows, WEIGHT_COLUMNS), lambda i: (0, i)),
        out_shape=jax.ShapeDtypeStruct((rows, width), BF16),
        compiler_params=pltpu.CompilerParams(vmem_limit_bytes=56 * MIB),
        cost_estimate=pl.CostEstimate(
            flops=4 * rows * tokens * width,
            transcendentals=0,
            bytes_accessed=2 * width * (rows + 4 * half) + 4 * rows * tokens,
        ),
        name="weight_gradient",
    )(own, from_p, *students)


def local(
    teacher_hidden, student_hidden, teacher_codes, teacher_scales, student_weight, loss_scale
):
    tok, width_t = teacher_hidden.shape
    width_s = student_hidden.shape[1]
    n_x, n_z, n_y = (lax.axis_size(a) for a in ("x", "z", "y"))
    x, y = lax.axis_index("x"), lax.axis_index("y")

    place = jnp.stack([y, x]).astype(jnp.int32)
    eighth = tok // (2 * n_x)
    odd = lax.rem(lax.axis_index("z"), 2)
    piece = [
        lax.dynamic_slice_in_dim(a, (2 * x + odd) * eighth, eighth, 0)
        for a in (teacher_hidden, student_hidden)
    ]
    piece = shift(jnp.concatenate(piece, axis=1), "y", 2)
    hidden = jnp.concatenate([teacher_hidden, student_hidden], axis=1)
    piece, whole = lax.optimization_barrier((piece, hidden))
    swapped = lax.ppermute(piece, "z", [(i, i ^ 1) for i in range(n_z)])
    quarter = jnp.where(
        odd == 0, jnp.concatenate([piece, swapped]), jnp.concatenate([swapped, piece])
    )
    after, before = shift(whole, "y", 1), shift(whole, "y", 3)
    codes_p = shift(teacher_codes, "c", 1)
    weight_p = shift(student_weight, "c", 1)
    scales_p = shift(teacher_scales, "c", 1)
    quarter, codes_p, weight_p, scales_p = lax.optimization_barrier(
        (quarter, codes_p, weight_p, scales_p)
    )
    quarters = [quarter, *(shift(quarter, "x", k) for k in range(1, n_x))]
    table = dequantize(teacher_codes, codes_p, teacher_scales, scales_p)
    turned = turned_over(student_weight, weight_p)

    tables = (table, student_weight, weight_p)
    t0, s0, stats0, students0 = logits_of(place, [hidden, *quarters], *tables)
    after, before, stats0, turned = lax.optimization_barrier((after, before, stats0, turned))
    students0_p = shift(students0, "c", 1)
    t1, s1, _, students1, mine = logits_of(
        place,
        [after, before],
        *tables,
        first_stats=stats0,
        scale=loss_scale.astype(F32)[None],
        copies=n_x * n_y,
    )
    seen = lax.all_to_all(mine, ("x", "y"), 0, 0, tiled=True)
    scales = jnp.sum(seen[:n_y, 5], axis=0)
    totals = combine(to_all(combine(seen), "z"))
    t_lse = totals[0] + jnp.log(totals[1])
    s_lse = totals[3] + jnp.log(totals[4])
    divergence = totals[2] / totals[1] - t_lse + s_lse
    found = jnp.stack([t_lse, s_lse, scales, divergence])
    found = jnp.concatenate([found, jnp.zeros_like(found)])
    found = jnp.concatenate([found, found[:, : (n_y - 1) * tok]], axis=1)
    found = lax.dynamic_slice_in_dim(found, y * tok, n_y * tok, 1)
    kl = found[3, :tok]
    order = [found[:, k * tok : (k + 1) * tok] for k in (0, 2, 1, 3)]
    own, other, blocks = gradients(
        place,
        jnp.concatenate(order, axis=1),
        ((t0, s0), (t1, s1)),
        turned,
        n_x,
        n_y,
    )
    from_p = shift(other, "c", 1)
    students1_p = shift(students1, "c", 1)
    grad_weight = weight_gradient(own, from_p, students0, students1, students0_p, students1_p)

    blocks = blocks.reshape(n_x * n_y, width_s // n_x, tok)
    got = lax.all_to_all(blocks, ("x", "y"), 0, 0, tiled=True)
    got = jnp.sum(got.astype(F32), axis=0).astype(BF16).reshape(n_z, -1, tok)
    got = lax.all_to_all(got, "z", 0, 0, tiled=True)
    grad_hidden = jnp.sum(got.astype(F32), axis=0).astype(BF16).T

    return kl, grad_hidden, grad_weight


def solution(mesh):
    split = Mesh(mesh.devices.reshape(4, 8, 4, 2), AXES)
    rows = P(("x", "z", "y", "c"), None)
    return jax.shard_map(
        local,
        mesh=split,
        in_specs=(P(DP, None), P(DP, None), rows, rows, rows, P(DP)),
        out_specs=(P(DP), P(DP, VOCAB), rows),
        check_vma=False,
    )
```

```python
import functools

import jax
import jax.numpy as jnp
from jax import lax
from jax.experimental import pallas as pl
from jax.experimental.pallas import tpu as pltpu
from jax.sharding import Mesh
from jax.sharding import PartitionSpec as P

GROUP = 128
AXES = ("x", "z", "y", "c")
DP = ("y", "c")
VOCAB = ("x", "z")
F32, BF16 = jnp.float32, jnp.bfloat16


def shift(a, axis, by):
    n = lax.axis_size(axis)
    return lax.ppermute(a, axis, [((i + by) % n, i) for i in range(n)])


NT = (((1,), (1,)), ((), ()))
MIB = 1024 * 1024
DEQUANT_ROWS = 128
LOGIT_ROWS = 256
ROW_STEP = 16
WEIGHT_COLUMNS = 512


def two_sources(i, steps):
    return (jnp.minimum(i, steps - 1), 0), (jnp.maximum(i - steps, 0), 0)


def dequant_kernel(own_steps, own_ref, other_ref, own_scale_ref, other_scale_ref, out_ref):
    def write(codes_ref, scale_ref):
        for g in range(codes_ref.shape[1] // GROUP):
            at = slice(g * GROUP, (g + 1) * GROUP)
            wide = codes_ref[:, at].astype(F32) * scale_ref[:, g : g + 1]
            out_ref[:, at] = wide.astype(BF16)

    @pl.when(pl.program_id(0) < own_steps)
    def _():
        write(own_ref, own_scale_ref)

    @pl.when(pl.program_id(0) >= own_steps)
    def _():
        write(other_ref, other_scale_ref)


def dequantize(codes, codes_p, scales, scales_p):
    rows, width = codes.shape
    steps = rows // DEQUANT_ROWS

    def source(width, k):
        return pl.BlockSpec((DEQUANT_ROWS, width), lambda i: two_sources(i, steps)[k])

    return pl.pallas_call(
        functools.partial(dequant_kernel, steps),
        grid=(2 * steps,),
        in_specs=[
            source(width, 0),
            source(width, 1),
            source(scales.shape[1], 0),
            source(scales.shape[1], 1),
        ],
        out_specs=pl.BlockSpec((DEQUANT_ROWS, width), lambda i: (i, 0)),
        out_shape=jax.ShapeDtypeStruct((2 * rows, width), BF16),
        compiler_params=pltpu.CompilerParams(vmem_limit_bytes=56 * MIB),
        cost_estimate=pl.CostEstimate(
            flops=2 * rows * width, transcendentals=0, bytes_accessed=8 * rows * width
        ),
        name="dequantize",
    )(codes, codes_p, scales, scales_p)


def turn_kernel(steps, own_ref, other_ref, out_ref):
    @pl.when(pl.program_id(0) < steps)
    def _():
        out_ref[...] = own_ref[...].T

    @pl.when(pl.program_id(0) >= steps)
    def _():
        out_ref[...] = other_ref[...].T


def turned_over(own, other):
    rows, width = own.shape
    steps = rows // DEQUANT_ROWS
    return pl.pallas_call(
        functools.partial(turn_kernel, steps),
        grid=(2 * steps,),
        in_specs=[
            pl.BlockSpec((DEQUANT_ROWS, width), lambda i: two_sources(i, steps)[0]),
            pl.BlockSpec((DEQUANT_ROWS, width), lambda i: two_sources(i, steps)[1]),
        ],
        out_specs=pl.BlockSpec((width, DEQUANT_ROWS), lambda i: (0, i)),
        out_shape=pltpu.HBM((width, 2 * rows), BF16),
        compiler_params=pltpu.CompilerParams(vmem_limit_bytes=8 * MIB),
        cost_estimate=pl.CostEstimate(
            flops=0, transcendentals=0, bytes_accessed=8 * rows * width
        ),
        name="turn",
    )(own, other)


def logits_tile(pair, table_ref, weight_ref, t_ref, s_ref, stat_ref):
    step = pl.program_id(0)
    width_t = table_ref.shape[1]
    t = lax.dot_general(table_ref[...], pair[:, :width_t], NT, preferred_element_type=F32)
    s = lax.dot_general(weight_ref[...], pair[:, width_t:], NT, preferred_element_type=F32)
    t_ref[...] = t
    s_ref[...] = s
    t_top = jnp.max(t, axis=0, keepdims=True)
    s_top = jnp.max(s, axis=0, keepdims=True)

    def sums(t_top, s_top):
        e = jnp.exp(t - t_top)
        return (
            jnp.sum(e, axis=0, keepdims=True),
            jnp.sum(e * (t - s), axis=0, keepdims=True),
            jnp.sum(jnp.exp(s - s_top), axis=0, keepdims=True),
        )

    @pl.when(step == 0)
    def _():
        total, cross, s_total = sums(t_top, s_top)
        for k, row in enumerate((t_top, total, cross, s_top, s_total)):
            stat_ref[k : k + 1] = row
        stat_ref[5:8] = jnp.zeros((3, t.shape[1]), F32)

    @pl.when(step > 0)
    def _():
        t_old, s_old = stat_ref[0:1], stat_ref[3:4]
        t_new, s_new = jnp.maximum(t_old, t_top), jnp.maximum(s_old, s_top)
        total, cross, s_total = sums(t_new, s_new)
        t_keep, s_keep = jnp.exp(t_old - t_new), jnp.exp(s_old - s_new)
        stat_ref[0:1] = t_new
        stat_ref[1:2] = stat_ref[1:2] * t_keep + total
        stat_ref[2:3] = stat_ref[2:3] * t_keep + cross
        stat_ref[3:4] = s_new
        stat_ref[4:5] = stat_ref[4:5] * s_keep + s_total


def load_blocks(place_ref, refs, block, sem):
    copies = []
    for k, ref in enumerate(refs):
        at = pl.multiple_of(place_ref[k + 1], ROW_STEP)
        copies.append(pltpu.make_async_copy(ref, block.at[pl.ds(at, ref.shape[0])], sem.at[k]))
    for copy in copies:
        copy.start()
    for copy in copies:
        copy.wait()


def logits_kernel(steps, n_pieces, place_ref, *rest):
    pieces_hbm, rest = rest[:n_pieces], rest[n_pieces:]
    (table_ref, weight_ref, weight_p_ref), rest = rest[:3], rest[3:]
    spread = len(rest) > 6
    first_stat_ref, scale_ref = rest[:2] if spread else (None, None)
    rest = rest[2:] if spread else rest
    t_ref, s_ref, stat_ref, student_ref = rest[:4]
    spread_ref = rest[4] if spread else None
    pair, sem = rest[-2:]
    step = pl.program_id(0)

    @pl.when(step == 0)
    def _():
        load_blocks(place_ref, pieces_hbm, pair, sem)
        student_ref[...] = pair[:, table_ref.shape[1] :]

    @pl.when(step < steps)
    def _():
        logits_tile(pair, table_ref, weight_ref, t_ref, s_ref, stat_ref)

    @pl.when(step >= steps)
    def _():
        logits_tile(pair, table_ref, weight_p_ref, t_ref, s_ref, stat_ref)

    if spread:

        @pl.when(step == 2 * steps - 1)
        def _():
            copies, _, wide = spread_ref.shape
            tok = scale_ref.shape[1]
            n_y = wide // tok
            row = lax.broadcasted_iota(jnp.int32, (8, tok), 0)
            scale = jnp.broadcast_to(scale_ref[...], (8, tok))
            first, last = first_stat_ref[...], stat_ref[...]
            pieces = (
                jnp.where(row == 5, scale, first),
                last[:, tok : 2 * tok],
                last[:, :tok],
                last[:, 2 * tok :],
            )
            for r, piece in enumerate(pieces):
                at = pl.multiple_of(lax.rem(place_ref[0] + r, n_y) * tok, tok)
                for k in range(copies):
                    spread_ref[k, :, pl.ds(at, tok)] = piece


def logits_of(place, pieces, table, weight, weight_p, first_stats=None, scale=None, copies=0):
    width_t = table.shape[1]
    rows, width_s = weight.shape
    tokens = sum(p.shape[0] for p in pieces)
    steps = rows // LOGIT_ROWS
    tile = pltpu.HBM((2 * rows, tokens), F32)

    def source(width, k):
        return pl.BlockSpec((LOGIT_ROWS, width), lambda i, y: two_sources(i, steps)[k])

    in_specs = [
        *[pl.BlockSpec(memory_space=pl.ANY) for _ in pieces],
        pl.BlockSpec((LOGIT_ROWS, width_t), lambda i, y: (i, 0)),
        source(width_s, 0),
        source(width_s, 1),
    ]
    out_specs = [
        pl.BlockSpec((LOGIT_ROWS, tokens), lambda i, y: (i, 0)),
        pl.BlockSpec((LOGIT_ROWS, tokens), lambda i, y: (i, 0)),
        pl.BlockSpec((8, tokens), lambda i, y: (0, 0)),
        pl.BlockSpec((tokens, width_s), lambda i, y: (0, 0)),
    ]
    out_shape = [
        tile,
        tile,
        jax.ShapeDtypeStruct((8, tokens), F32),
        pltpu.HBM((tokens, width_s), BF16),
    ]
    operands = [place, *pieces, table, weight, weight_p]
    if first_stats is not None:
        every = tokens + first_stats.shape[1]
        in_specs.append(pl.BlockSpec(first_stats.shape, lambda i, y: (0, 0)))
        in_specs.append(pl.BlockSpec(scale.shape, lambda i, y: (0, 0)))
        operands += [first_stats, scale]
        out_specs.append(pl.BlockSpec((copies, 8, every), lambda i, y: (0, 0, 0)))
        out_shape.append(jax.ShapeDtypeStruct((copies, 8, every), F32))
    return pl.pallas_call(
        functools.partial(logits_kernel, steps, len(pieces)),
        grid_spec=pltpu.PrefetchScalarGridSpec(
            num_scalar_prefetch=1,
            grid=(2 * steps,),
            in_specs=in_specs,
            out_specs=out_specs,
            scratch_shapes=[
                pltpu.VMEM((tokens, width_t + width_s), BF16),
                pltpu.SemaphoreType.DMA((len(pieces),)),
            ],
        ),
        out_shape=out_shape,
        compiler_params=pltpu.CompilerParams(vmem_limit_bytes=56 * MIB),
        cost_estimate=pl.CostEstimate(
            flops=4 * rows * tokens * (width_t + width_s),
            transcendentals=4 * rows * tokens,
            bytes_accessed=2 * (2 * rows + tokens) * (width_t + width_s) + 16 * rows * tokens,
        ),
        name="logits",
    )(*operands)


def grad_kernel(y_ref, rows_ref, t0, s0, t1, s1, turned_ref, own_ref, other_ref, out_ref):
    half = own_ref.shape[0]
    n_y, tok = out_ref.shape[1], out_ref.shape[3]

    @pl.when(pl.program_id(0) == 0)
    def _():
        split = t0.shape[1]
        for t, s, at in ((t0, s0, slice(0, split)), (t1, s1, slice(split, None))):
            t_lse, s_lse, scale = (rows_ref[k : k + 1, at] for k in range(3))
            for q, ref in enumerate((own_ref, other_ref)):
                rows = slice(q * half, (q + 1) * half)
                gap = jnp.exp(s[rows] - s_lse) - jnp.exp(t[rows] - t_lse)
                ref[:, at] = (scale * gap).astype(BF16)

    total = jnp.dot(turned_ref[:, :half], own_ref[...], preferred_element_type=F32)
    total += jnp.dot(turned_ref[:, half:], other_ref[...], preferred_element_type=F32)
    for k, r in enumerate((0, 2, 1, 3)):
        at = lax.rem(y_ref[0] + r, n_y)
        out_ref[0, at] = total[:, k * tok : (k + 1) * tok].astype(BF16)


def gradients(y, rows, logits, turned, n_x, n_y):
    (t0, s0), (t1, s1) = logits
    vocab, tokens = t0.shape[0], t0.shape[1] + t1.shape[1]
    width = turned.shape[0]
    lg = pltpu.HBM((vocab // 2, tokens), BF16)
    first = pl.BlockSpec(t0.shape, lambda i, y: (0, 0))
    others = pl.BlockSpec(t1.shape, lambda i, y: (0, 0))
    lg_spec = pl.BlockSpec((vocab // 2, tokens), lambda i, y: (0, 0))
    cut = (width // n_x, tokens // n_y)
    return pl.pallas_call(
        grad_kernel,
        grid_spec=pltpu.PrefetchScalarGridSpec(
            num_scalar_prefetch=1,
            grid=(n_x,),
            in_specs=[
                pl.BlockSpec(rows.shape, lambda i, y: (0, 0)),
                first,
                first,
                others,
                others,
                pl.BlockSpec((width // n_x, vocab), lambda i, y: (i, 0)),
            ],
            out_specs=[lg_spec, lg_spec, pl.BlockSpec((1, n_y, *cut), lambda i, y: (i, 0, 0, 0))],
        ),
        out_shape=[lg, lg, pltpu.HBM((n_x, n_y, *cut), BF16)],
        compiler_params=pltpu.CompilerParams(vmem_limit_bytes=56 * MIB),
        cost_estimate=pl.CostEstimate(
            flops=2 * vocab * tokens * width,
            transcendentals=2 * vocab * tokens,
            bytes_accessed=2 * width * (vocab + tokens) + 10 * vocab * tokens,
        ),
        name="gradients",
    )(y, rows, t0, s0, t1, s1, turned)


def to_all(a, axes):
    n = lax.axis_size(axes)
    return lax.all_to_all(jnp.broadcast_to(a[None], (n, *a.shape)), axes, 0, 0, tiled=True)


def combine(stats):
    teacher_top = jnp.max(stats[:, 0], axis=0)
    student_top = jnp.max(stats[:, 3], axis=0)
    teacher_factor = jnp.exp(stats[:, 0] - teacher_top)
    student_factor = jnp.exp(stats[:, 3] - student_top)
    return jnp.stack(
        [
            teacher_top,
            jnp.sum(stats[:, 1] * teacher_factor, axis=0),
            jnp.sum(stats[:, 2] * teacher_factor, axis=0),
            student_top,
            jnp.sum(stats[:, 4] * student_factor, axis=0),
        ]
    )


def weight_kernel(own_ref, from_ref, s0_ref, s1_ref, s0_p_ref, s1_p_ref, out_ref):
    half = s0_ref.shape[0]
    total = jnp.dot(own_ref[:, :half], s0_ref[...], preferred_element_type=F32)
    total += jnp.dot(own_ref[:, half:], s1_ref[...], preferred_element_type=F32)
    total += jnp.dot(from_ref[:, :half], s0_p_ref[...], preferred_element_type=F32)
    total += jnp.dot(from_ref[:, half:], s1_p_ref[...], preferred_element_type=F32)
    out_ref[...] = total.astype(BF16)


def weight_gradient(own, from_p, *students):
    rows, tokens = own.shape
    width = students[0].shape[1]
    whole = pl.BlockSpec((rows, tokens), lambda i: (0, 0))
    return pl.pallas_call(
        weight_kernel,
        grid=(width // WEIGHT_COLUMNS,),
        in_specs=[whole, whole]
        + [pl.BlockSpec((a.shape[0], WEIGHT_COLUMNS), lambda i: (0, i)) for a in students],
        out_specs=pl.BlockSpec((rows, WEIGHT_COLUMNS), lambda i: (0, i)),
        out_shape=jax.ShapeDtypeStruct((rows, width), BF16),
        compiler_params=pltpu.CompilerParams(vmem_limit_bytes=56 * MIB),
        cost_estimate=pl.CostEstimate(
            flops=4 * rows * tokens * width,
            transcendentals=0,
            bytes_accessed=2 * width * (rows + 2 * tokens) + 4 * rows * tokens,
        ),
        name="weight_gradient",
    )(own, from_p, *students)


def local(
    teacher_hidden, student_hidden, teacher_codes, teacher_scales, student_weight, loss_scale
):
    tok, width_t = teacher_hidden.shape
    width_s = student_hidden.shape[1]
    n_x, n_z, n_y = (lax.axis_size(a) for a in ("x", "z", "y"))
    x, y = lax.axis_index("x"), lax.axis_index("y")

    def packed(start, size):
        cut = [
            lax.dynamic_slice_in_dim(a, start, size, 0) for a in (teacher_hidden, student_hidden)
        ]
        return jnp.concatenate(cut, axis=1)

    def z_swapped(a):
        return lax.ppermute(a, "z", [(i, i ^ 1) for i in range(n_z)])

    eighth, share = tok // (2 * n_x), tok // 4
    odd = lax.rem(lax.axis_index("z"), 2)
    hidden = packed(0, tok)
    piece = shift(packed((2 * x + odd) * eighth, eighth), "y", 2)
    piece, part = lax.optimization_barrier((piece, packed(odd * share, share)))
    after, before = shift(part, "y", 1), shift(part, "y", 3)
    after, before, rest = lax.optimization_barrier((after, before, packed(2 * share, 2 * share)))
    blocks = [
        [a, z_swapped(a), shift(rest, "y", by)] for a, by in ((after, 1), (before, 3))
    ]
    swapped = z_swapped(piece)
    quarter = jnp.where(
        odd == 0, jnp.concatenate([piece, swapped]), jnp.concatenate([swapped, piece])
    )
    codes_p = shift(teacher_codes, "c", 1)
    weight_p = shift(student_weight, "c", 1)
    scales_p = shift(teacher_scales, "c", 1)
    quarter, codes_p, weight_p, scales_p = lax.optimization_barrier(
        (quarter, codes_p, weight_p, scales_p)
    )
    opposite = to_all(quarter, "x").reshape(tok, -1)
    table = dequantize(teacher_codes, codes_p, teacher_scales, scales_p)

    tables = (table, student_weight, weight_p)
    place = jnp.stack([y, jnp.zeros_like(y)]).astype(jnp.int32)
    t0, s0, stats0, students0 = logits_of(place, [hidden], *tables)
    students0_p = shift(students0, "c", 1)
    rows = [y, jnp.zeros_like(y)]
    for k in (1, 2):
        rows += [k * tok + odd * share, k * tok + (1 - odd) * share, y * 0 + k * tok + 2 * share]
    pieces, stats0 = lax.optimization_barrier(([opposite, *blocks[0], *blocks[1]], stats0))
    t1, s1, _, students1, mine = logits_of(
        jnp.stack(rows).astype(jnp.int32),
        pieces,
        *tables,
        first_stats=stats0,
        scale=loss_scale.astype(F32)[None],
        copies=n_x * n_y,
    )
    mine, weight_own, weight_other = lax.optimization_barrier((mine, student_weight, weight_p))
    turned = turned_over(weight_own, weight_other)
    seen = lax.all_to_all(mine, ("x", "y"), 0, 0, tiled=True)
    scales = jnp.sum(seen[:n_y, 5], axis=0)
    totals = combine(to_all(combine(seen), "z"))
    t_lse = totals[0] + jnp.log(totals[1])
    s_lse = totals[3] + jnp.log(totals[4])
    divergence = totals[2] / totals[1] - t_lse + s_lse
    found = jnp.stack([t_lse, s_lse, scales, divergence])
    found = jnp.concatenate([found, jnp.zeros_like(found)])
    found = jnp.concatenate([found, found[:, : (n_y - 1) * tok]], axis=1)
    found = lax.dynamic_slice_in_dim(found, y * tok, n_y * tok, 1)
    kl = found[3, :tok]
    order = [found[:, k * tok : (k + 1) * tok] for k in (0, 2, 1, 3)]
    own, other, blocks = gradients(
        place,
        jnp.concatenate(order, axis=1),
        ((t0, s0), (t1, s1)),
        turned,
        n_x,
        n_y,
    )
    from_p = shift(other, "c", 1)
    students1_p = shift(students1, "c", 1)
    grad_weight = weight_gradient(own, from_p, students0, students1, students0_p, students1_p)

    blocks = blocks.reshape(n_x * n_y, width_s // n_x, tok)
    got = lax.all_to_all(blocks, ("x", "y"), 0, 0, tiled=True)
    got = jnp.sum(got.astype(F32), axis=0).astype(BF16).reshape(n_z, -1, tok)
    got = lax.all_to_all(got, "z", 0, 0, tiled=True)
    grad_hidden = jnp.sum(got.astype(F32), axis=0).astype(BF16).T

    return kl, grad_hidden, grad_weight


def solution(mesh):
    split = Mesh(mesh.devices.reshape(4, 8, 4, 2), AXES)
    rows = P(("x", "z", "y", "c"), None)
    return jax.shard_map(
        local,
        mesh=split,
        in_specs=(P(DP, None), P(DP, None), rows, rows, rows, P(DP)),
        out_specs=(P(DP), P(DP, VOCAB), rows),
        check_vma=False,
    )
```

```python
import functools

import jax
import jax.numpy as jnp
from jax import lax
from jax.experimental import pallas as pl
from jax.experimental.pallas import tpu as pltpu
from jax.sharding import Mesh
from jax.sharding import PartitionSpec as P

GROUP = 128
AXES = ("x", "z", "y", "c")
DP = ("y", "c")
VOCAB = ("x", "z")
F32, BF16 = jnp.float32, jnp.bfloat16


def shift(a, axis, by):
    n = lax.axis_size(axis)
    return lax.ppermute(a, axis, [((i + by) % n, i) for i in range(n)])


def rolled(blocks, start):
    n = blocks.shape[0]
    return lax.dynamic_slice_in_dim(jnp.concatenate([blocks, blocks[:-1]]), start % n, n, 0)


NT = (((1,), (1,)), ((), ()))
MIB = 1024 * 1024
VMEM_LOGITS = 18 * MIB
DEQUANT_ROWS = 128
LOGIT_ROWS = 256
WEIGHT_COLUMNS = 512


def two_sources(i, steps):
    return (jnp.minimum(i, steps - 1), 0), (jnp.maximum(i - steps, 0), 0)


def dequant_kernel(own_steps, own_ref, other_ref, own_scale_ref, other_scale_ref, out_ref):
    def write(codes_ref, scale_ref):
        for g in range(codes_ref.shape[1] // GROUP):
            at = slice(g * GROUP, (g + 1) * GROUP)
            wide = codes_ref[:, at].astype(F32) * scale_ref[:, g : g + 1]
            out_ref[:, at] = wide.astype(BF16)

    @pl.when(pl.program_id(0) < own_steps)
    def _():
        write(own_ref, own_scale_ref)

    @pl.when(pl.program_id(0) >= own_steps)
    def _():
        write(other_ref, other_scale_ref)


def dequantize(codes, codes_p, scales, scales_p):
    rows, width = codes.shape
    steps = rows // DEQUANT_ROWS

    def source(width, k):
        return pl.BlockSpec((DEQUANT_ROWS, width), lambda i: two_sources(i, steps)[k])

    return pl.pallas_call(
        functools.partial(dequant_kernel, steps),
        grid=(2 * steps,),
        in_specs=[
            source(width, 0),
            source(width, 1),
            source(scales.shape[1], 0),
            source(scales.shape[1], 1),
        ],
        out_specs=pl.BlockSpec((DEQUANT_ROWS, width), lambda i: (i, 0)),
        out_shape=jax.ShapeDtypeStruct((2 * rows, width), BF16),
        compiler_params=pltpu.CompilerParams(vmem_limit_bytes=12 * MIB),
        cost_estimate=pl.CostEstimate(
            flops=2 * rows * width, transcendentals=0, bytes_accessed=8 * rows * width
        ),
        name="dequantize",
    )(codes, codes_p, scales, scales_p)


def turn_kernel(steps, own_ref, other_ref, out_ref):
    @pl.when(pl.program_id(0) < steps)
    def _():
        out_ref[...] = own_ref[...].T

    @pl.when(pl.program_id(0) >= steps)
    def _():
        out_ref[...] = other_ref[...].T


def turned_over(own, other):
    rows, width = own.shape
    steps = rows // DEQUANT_ROWS
    return pl.pallas_call(
        functools.partial(turn_kernel, steps),
        grid=(2 * steps,),
        in_specs=[
            pl.BlockSpec((DEQUANT_ROWS, width), lambda i: two_sources(i, steps)[0]),
            pl.BlockSpec((DEQUANT_ROWS, width), lambda i: two_sources(i, steps)[1]),
        ],
        out_specs=pl.BlockSpec((width, DEQUANT_ROWS), lambda i: (0, i)),
        out_shape=pltpu.HBM((width, 2 * rows), BF16),
        compiler_params=pltpu.CompilerParams(vmem_limit_bytes=8 * MIB),
        cost_estimate=pl.CostEstimate(
            flops=0, transcendentals=0, bytes_accessed=8 * rows * width
        ),
        name="turn",
    )(own, other)


def update_stats(first, t, s, stat_ref):
    t_top = jnp.max(t, axis=0, keepdims=True)
    s_top = jnp.max(s, axis=0, keepdims=True)
    if not first:
        t_old, s_old = stat_ref[0:1], stat_ref[3:4]
        t_top, s_top = jnp.maximum(t_old, t_top), jnp.maximum(s_old, s_top)
    e = jnp.exp(t - t_top)
    total = jnp.sum(e, axis=0, keepdims=True)
    cross = jnp.sum(e * (t - s), axis=0, keepdims=True)
    s_total = jnp.sum(jnp.exp(s - s_top), axis=0, keepdims=True)
    if first:
        stat_ref[5:8] = jnp.zeros((3, t.shape[1]), F32)
    else:
        t_keep, s_keep = jnp.exp(t_old - t_top), jnp.exp(s_old - s_top)
        total += stat_ref[1:2] * t_keep
        cross += stat_ref[2:3] * t_keep
        s_total += stat_ref[4:5] * s_keep
    for k, row in enumerate((t_top, total, cross, s_top, s_total)):
        stat_ref[k : k + 1] = row


def load_pair(x_ref, refs, pair, sem):
    tok, part = refs[0].shape[0], refs[1].shape[0]
    copies = [pltpu.make_async_copy(refs[0], pair.at[pl.ds(0, tok)], sem.at[0])]
    for k, ref in enumerate(refs[1:]):
        at = pl.multiple_of(tok + lax.rem(x_ref[1] + k, tok // part) * part, part)
        copies.append(pltpu.make_async_copy(ref, pair.at[pl.ds(at, part)], sem.at[k + 1]))
    for copy in copies:
        copy.start()
    for copy in copies:
        copy.wait()


def logits_kernel(n_pieces, place_ref, *rest):
    pieces_hbm, rest = rest[:n_pieces], rest[n_pieces:]
    (table_ref, weight_ref, weight_p_ref), rest = rest[:3], rest[3:]
    tok = pieces_hbm[0].shape[0]
    spread = len(rest) > 9
    first_stat_ref, scale_ref = rest[:2] if spread else (None, None)
    rest = rest[2:] if spread else rest
    t_hbm, s_hbm, stat_ref, student_hbm = rest[:4]
    spread_ref = rest[4] if spread else None
    pair, t_buf, s_buf, load_sem, out_sem = rest[-5:]
    width_t = table_ref.shape[1]
    rows = weight_ref.shape[0]

    load_pair(place_ref, pieces_hbm, pair, load_sem)
    students = pltpu.make_async_copy(pair.at[:, pl.ds(width_t, weight_ref.shape[1])], student_hbm, out_sem.at[2, 0])
    students.start()
    waiting = []
    for i in range(2 * rows // LOGIT_ROWS):
        slot, at = i % 2, i * LOGIT_ROWS
        source, low = (weight_ref, at) if at < rows else (weight_p_ref, at - rows)
        t = lax.dot_general(
            table_ref[at : at + LOGIT_ROWS], pair[:, :width_t], NT, preferred_element_type=F32
        )
        s = lax.dot_general(
            source[low : low + LOGIT_ROWS], pair[:, width_t:], NT, preferred_element_type=F32
        )
        if i >= 2:
            for copy in waiting[i - 2]:
                copy.wait()
        t_buf[slot] = t
        s_buf[slot] = s
        copies = [
            pltpu.make_async_copy(
                buf.at[slot], hbm.at[pl.ds(at, LOGIT_ROWS)], out_sem.at[k, slot]
            )
            for k, (buf, hbm) in enumerate(((t_buf, t_hbm), (s_buf, s_hbm)))
        ]
        for copy in copies:
            copy.start()
        waiting.append(copies)
        update_stats(i == 0, t, s, stat_ref)

    if spread:
        copies, _, wide = spread_ref.shape
        n_y = wide // tok
        row = lax.broadcasted_iota(jnp.int32, (8, tok), 0)
        scale = jnp.broadcast_to(scale_ref[...], (8, tok))
        first, last = first_stat_ref[...], stat_ref[...]
        pieces = (
            jnp.where(row == 5, scale, first[:, :tok]),
            last[:, :tok],
            first[:, tok:],
            last[:, tok:],
        )
        for r, piece in enumerate(pieces):
            at = pl.multiple_of(lax.rem(place_ref[0] + r, n_y) * tok, tok)
            for k in range(copies):
                spread_ref[k, :, pl.ds(at, tok)] = piece
    for copies in waiting[-2:]:
        for copy in copies:
            copy.wait()
    students.wait()


def logits_of(place, pieces, table, weight, weight_p, first_stats=None, scale=None, copies=0):
    width_t = table.shape[1]
    rows, width_s = weight.shape
    tok = pieces[0].shape[0]
    tokens = 2 * tok
    anywhere, on_chip = pl.BlockSpec(memory_space=pl.ANY), pl.BlockSpec(memory_space=pltpu.VMEM)
    in_specs = [pl.BlockSpec(memory_space=pltpu.SMEM)]
    in_specs += [anywhere] * len(pieces) + [on_chip] * 3
    out_specs = [anywhere, anywhere, on_chip, anywhere]
    tile = pltpu.HBM((2 * rows, tokens), F32)
    out_shape = [tile, tile, jax.ShapeDtypeStruct((8, tokens), F32), pltpu.HBM((tokens, width_s), BF16)]
    operands = [place, *pieces, table, weight, weight_p]
    if first_stats is not None:
        in_specs += [on_chip, on_chip]
        operands += [first_stats, scale]
        out_specs.append(on_chip)
        out_shape.append(jax.ShapeDtypeStruct((copies, 8, 2 * tokens), F32))
    return pl.pallas_call(
        functools.partial(logits_kernel, len(pieces)),
        in_specs=in_specs,
        out_specs=out_specs,
        out_shape=out_shape,
        scratch_shapes=[
            pltpu.VMEM((tokens, width_t + width_s), BF16),
            pltpu.VMEM((2, LOGIT_ROWS, tokens), F32),
            pltpu.VMEM((2, LOGIT_ROWS, tokens), F32),
            pltpu.SemaphoreType.DMA((len(pieces),)),
            pltpu.SemaphoreType.DMA((3, 2)),
        ],
        compiler_params=pltpu.CompilerParams(vmem_limit_bytes=VMEM_LOGITS),
        cost_estimate=pl.CostEstimate(
            flops=4 * rows * tokens * (width_t + width_s),
            transcendentals=4 * rows * tokens,
            bytes_accessed=2 * tokens * (width_t + 2 * width_s) + 16 * rows * tokens,
        ),
        name="logits",
    )(*operands)


def grad_kernel(y_ref, rows_ref, t0, s0, t1, s1, turned_ref, own_ref, other_ref, out_ref):
    half = own_ref.shape[0]
    n_y, tok = out_ref.shape[1], out_ref.shape[3]

    @pl.when(pl.program_id(0) == 0)
    def _():
        for p, (t, s) in enumerate(((t0, s0), (t1, s1))):
            at = slice(2 * p * tok, 2 * (p + 1) * tok)
            t_lse, s_lse, scale = (rows_ref[k : k + 1, at] for k in range(3))
            for q, ref in enumerate((own_ref, other_ref)):
                rows = slice(q * half, (q + 1) * half)
                gap = jnp.exp(s[rows] - s_lse) - jnp.exp(t[rows] - t_lse)
                ref[:, at] = (scale * gap).astype(BF16)

    total = jnp.dot(turned_ref[:, :half], own_ref[...], preferred_element_type=F32)
    total += jnp.dot(turned_ref[:, half:], other_ref[...], preferred_element_type=F32)
    for k, r in enumerate((0, 2, 1, 3)):
        at = lax.rem(y_ref[0] + r, n_y)
        out_ref[0, at] = total[:, k * tok : (k + 1) * tok].astype(BF16)


def gradients(y, rows, logits, turned, n_x, n_y):
    (t0, s0), (t1, s1) = logits
    vocab, tokens = t0.shape
    width = turned.shape[0]
    lg = pltpu.HBM((vocab // 2, 2 * tokens), BF16)
    whole = pl.BlockSpec((vocab, tokens), lambda i, y: (0, 0))
    lg_spec = pl.BlockSpec((vocab // 2, 2 * tokens), lambda i, y: (0, 0))
    cut = (width // n_x, 2 * tokens // n_y)
    return pl.pallas_call(
        grad_kernel,
        grid_spec=pltpu.PrefetchScalarGridSpec(
            num_scalar_prefetch=1,
            grid=(n_x,),
            in_specs=[
                pl.BlockSpec(rows.shape, lambda i, y: (0, 0)),
                whole,
                whole,
                whole,
                whole,
                pl.BlockSpec((width // n_x, vocab), lambda i, y: (i, 0)),
            ],
            out_specs=[lg_spec, lg_spec, pl.BlockSpec((1, n_y, *cut), lambda i, y: (i, 0, 0, 0))],
        ),
        out_shape=[lg, lg, pltpu.HBM((n_x, n_y, *cut), BF16)],
        compiler_params=pltpu.CompilerParams(vmem_limit_bytes=56 * MIB),
        cost_estimate=pl.CostEstimate(
            flops=4 * vocab * tokens * width,
            transcendentals=4 * vocab * tokens,
            bytes_accessed=2 * width * (vocab + 2 * tokens) + 20 * vocab * tokens,
        ),
        name="gradients",
    )(y, rows, t0, s0, t1, s1, turned)


def to_all(a, axes):
    n = lax.axis_size(axes)
    return lax.all_to_all(jnp.broadcast_to(a[None], (n, *a.shape)), axes, 0, 0, tiled=True)


def combine(stats):
    teacher_top = jnp.max(stats[:, 0], axis=0)
    student_top = jnp.max(stats[:, 3], axis=0)
    teacher_factor = jnp.exp(stats[:, 0] - teacher_top)
    student_factor = jnp.exp(stats[:, 3] - student_top)
    return jnp.stack(
        [
            teacher_top,
            jnp.sum(stats[:, 1] * teacher_factor, axis=0),
            jnp.sum(stats[:, 2] * teacher_factor, axis=0),
            student_top,
            jnp.sum(stats[:, 4] * student_factor, axis=0),
        ]
    )


def weight_kernel(own_ref, from_ref, s0_ref, s1_ref, s0_p_ref, s1_p_ref, out_ref):
    half = s0_ref.shape[0]
    total = jnp.dot(own_ref[:, :half], s0_ref[...], preferred_element_type=F32)
    total += jnp.dot(own_ref[:, half:], s1_ref[...], preferred_element_type=F32)
    total += jnp.dot(from_ref[:, :half], s0_p_ref[...], preferred_element_type=F32)
    total += jnp.dot(from_ref[:, half:], s1_p_ref[...], preferred_element_type=F32)
    out_ref[...] = total.astype(BF16)


def weight_gradient(own, from_p, *students):
    rows, tokens = own.shape
    half, width = students[0].shape
    whole = pl.BlockSpec((rows, tokens), lambda i: (0, 0))
    return pl.pallas_call(
        weight_kernel,
        grid=(width // WEIGHT_COLUMNS,),
        in_specs=[whole, whole] + [pl.BlockSpec((half, WEIGHT_COLUMNS), lambda i: (0, i))] * 4,
        out_specs=pl.BlockSpec((rows, WEIGHT_COLUMNS), lambda i: (0, i)),
        out_shape=jax.ShapeDtypeStruct((rows, width), BF16),
        compiler_params=pltpu.CompilerParams(vmem_limit_bytes=56 * MIB),
        cost_estimate=pl.CostEstimate(
            flops=4 * rows * tokens * width,
            transcendentals=0,
            bytes_accessed=2 * width * (rows + 4 * half) + 4 * rows * tokens,
        ),
        name="weight_gradient",
    )(own, from_p, *students)


def local(
    teacher_hidden, student_hidden, teacher_codes, teacher_scales, student_weight, loss_scale
):
    tok, width_t = teacher_hidden.shape
    width_s = student_hidden.shape[1]
    n_x, n_z, n_y = (lax.axis_size(a) for a in ("x", "z", "y"))
    x, y = lax.axis_index("x"), lax.axis_index("y")

    place = jnp.stack([y, x]).astype(jnp.int32)
    eighth = tok // (2 * n_x)
    odd = lax.rem(lax.axis_index("z"), 2)
    piece = [
        lax.dynamic_slice_in_dim(a, (2 * x + odd) * eighth, eighth, 0)
        for a in (teacher_hidden, student_hidden)
    ]
    piece = shift(jnp.concatenate(piece, axis=1), "y", 2)
    hidden = jnp.concatenate([teacher_hidden, student_hidden], axis=1)
    piece, whole = lax.optimization_barrier((piece, hidden))
    swapped = lax.ppermute(piece, "z", [(i, i ^ 1) for i in range(n_z)])
    quarter = jnp.where(
        odd == 0, jnp.concatenate([piece, swapped]), jnp.concatenate([swapped, piece])
    )
    after, before = shift(whole, "y", 1), shift(whole, "y", 3)
    codes_p = shift(teacher_codes, "c", 1)
    weight_p = shift(student_weight, "c", 1)
    scales_p = shift(teacher_scales, "c", 1)
    quarter, codes_p, weight_p, scales_p = lax.optimization_barrier(
        (quarter, codes_p, weight_p, scales_p)
    )
    quarters = [quarter, *(shift(quarter, "x", k) for k in range(1, n_x))]
    table = dequantize(teacher_codes, codes_p, teacher_scales, scales_p)
    turned = turned_over(student_weight, weight_p)

    tables = (table, student_weight, weight_p)
    t0, s0, stats0, students0 = logits_of(place, [hidden, *quarters], *tables)
    after, before, stats0, turned = lax.optimization_barrier((after, before, stats0, turned))
    students0_p = shift(students0, "c", 1)
    t1, s1, _, students1, mine = logits_of(
        place,
        [after, before],
        *tables,
        first_stats=stats0,
        scale=loss_scale.astype(F32)[None],
        copies=n_x * n_y,
    )
    seen = lax.all_to_all(mine, ("x", "y"), 0, 0, tiled=True)
    scales = jnp.sum(seen[:n_y, 5], axis=0)
    totals = combine(to_all(combine(seen), "z"))
    t_lse = totals[0] + jnp.log(totals[1])
    s_lse = totals[3] + jnp.log(totals[4])
    divergence = totals[2] / totals[1] - t_lse + s_lse
    found = jnp.stack([t_lse, s_lse, scales, divergence])
    found = jnp.concatenate([found, jnp.zeros_like(found)])
    found = jnp.concatenate([found, found[:, : (n_y - 1) * tok]], axis=1)
    found = lax.dynamic_slice_in_dim(found, y * tok, n_y * tok, 1)
    kl = found[3, :tok]
    order = [found[:, k * tok : (k + 1) * tok] for k in (0, 2, 1, 3)]
    own, other, blocks = gradients(
        place,
        jnp.concatenate(order, axis=1),
        ((t0, s0), (t1, s1)),
        turned,
        n_x,
        n_y,
    )
    from_p = shift(other, "c", 1)
    students1_p = shift(students1, "c", 1)
    grad_weight = weight_gradient(own, from_p, students0, students1, students0_p, students1_p)

    blocks = blocks.reshape(n_x * n_y, width_s // n_x, tok)
    got = lax.all_to_all(blocks, ("x", "y"), 0, 0, tiled=True)
    got = jnp.sum(got.astype(F32), axis=0).astype(BF16).reshape(n_z, -1, tok)
    got = lax.all_to_all(got, "z", 0, 0, tiled=True)
    grad_hidden = jnp.sum(got.astype(F32), axis=0).astype(BF16).T

    return kl, grad_hidden, grad_weight


def solution(mesh):
    split = Mesh(mesh.devices.reshape(4, 8, 4, 2), AXES)
    rows = P(("x", "z", "y", "c"), None)
    return jax.shard_map(
        local,
        mesh=split,
        in_specs=(P(DP, None), P(DP, None), rows, rows, rows, P(DP)),
        out_specs=(P(DP), P(DP, VOCAB), rows),
        check_vma=False,
    )
```

```python
import functools

import jax
import jax.numpy as jnp
from jax import lax
from jax.experimental import pallas as pl
from jax.experimental.pallas import tpu as pltpu
from jax.sharding import Mesh
from jax.sharding import PartitionSpec as P

GROUP = 128
AXES = ("x", "z", "y", "c")
DP = ("y", "c")
VOCAB = ("x", "z")
F32, BF16 = jnp.float32, jnp.bfloat16


def shift(a, axis, by):
    n = lax.axis_size(axis)
    return lax.ppermute(a, axis, [((i + by) % n, i) for i in range(n)])


def rolled(blocks, start):
    n = blocks.shape[0]
    return lax.dynamic_slice_in_dim(jnp.concatenate([blocks, blocks[:-1]]), start % n, n, 0)


NT = (((1,), (1,)), ((), ()))
MIB = 1024 * 1024
VMEM_LOGITS = 20 * MIB
DEQUANT_ROWS = 128
LOGIT_ROWS = 512
WEIGHT_COLUMNS = 512


def two_sources(i, steps):
    return (jnp.minimum(i, steps - 1), 0), (jnp.maximum(i - steps, 0), 0)


def dequant_kernel(own_steps, own_ref, other_ref, own_scale_ref, other_scale_ref, out_ref):
    def write(codes_ref, scale_ref):
        for g in range(codes_ref.shape[1] // GROUP):
            at = slice(g * GROUP, (g + 1) * GROUP)
            wide = codes_ref[:, at].astype(F32) * scale_ref[:, g : g + 1]
            out_ref[:, at] = wide.astype(BF16)

    @pl.when(pl.program_id(0) < own_steps)
    def _():
        write(own_ref, own_scale_ref)

    @pl.when(pl.program_id(0) >= own_steps)
    def _():
        write(other_ref, other_scale_ref)


def dequantize(codes, codes_p, scales, scales_p):
    rows, width = codes.shape
    steps = rows // DEQUANT_ROWS

    def source(width, k):
        return pl.BlockSpec((DEQUANT_ROWS, width), lambda i: two_sources(i, steps)[k])

    return pl.pallas_call(
        functools.partial(dequant_kernel, steps),
        grid=(2 * steps,),
        in_specs=[
            source(width, 0),
            source(width, 1),
            source(scales.shape[1], 0),
            source(scales.shape[1], 1),
        ],
        out_specs=pl.BlockSpec((DEQUANT_ROWS, width), lambda i: (i, 0)),
        out_shape=jax.ShapeDtypeStruct((2 * rows, width), BF16),
        compiler_params=pltpu.CompilerParams(vmem_limit_bytes=12 * MIB),
        cost_estimate=pl.CostEstimate(
            flops=2 * rows * width, transcendentals=0, bytes_accessed=8 * rows * width
        ),
        name="dequantize",
    )(codes, codes_p, scales, scales_p)


def turn_kernel(steps, own_ref, other_ref, out_ref):
    @pl.when(pl.program_id(0) < steps)
    def _():
        out_ref[...] = own_ref[...].T

    @pl.when(pl.program_id(0) >= steps)
    def _():
        out_ref[...] = other_ref[...].T


def turned_over(own, other):
    rows, width = own.shape
    steps = rows // DEQUANT_ROWS
    return pl.pallas_call(
        functools.partial(turn_kernel, steps),
        grid=(2 * steps,),
        in_specs=[
            pl.BlockSpec((DEQUANT_ROWS, width), lambda i: two_sources(i, steps)[0]),
            pl.BlockSpec((DEQUANT_ROWS, width), lambda i: two_sources(i, steps)[1]),
        ],
        out_specs=pl.BlockSpec((width, DEQUANT_ROWS), lambda i: (0, i)),
        out_shape=pltpu.HBM((width, 2 * rows), BF16),
        compiler_params=pltpu.CompilerParams(vmem_limit_bytes=8 * MIB),
        cost_estimate=pl.CostEstimate(
            flops=0, transcendentals=0, bytes_accessed=8 * rows * width
        ),
        name="turn",
    )(own, other)


def update_stats(first, t, s, stat_ref):
    t_top = jnp.max(t, axis=0, keepdims=True)
    s_top = jnp.max(s, axis=0, keepdims=True)
    if not first:
        t_old, s_old = stat_ref[0:1], stat_ref[3:4]
        t_top, s_top = jnp.maximum(t_old, t_top), jnp.maximum(s_old, s_top)
    e = jnp.exp(t - t_top)
    total = jnp.sum(e, axis=0, keepdims=True)
    cross = jnp.sum(e * (t - s), axis=0, keepdims=True)
    s_total = jnp.sum(jnp.exp(s - s_top), axis=0, keepdims=True)
    if first:
        stat_ref[5:8] = jnp.zeros((3, t.shape[1]), F32)
    else:
        t_keep, s_keep = jnp.exp(t_old - t_top), jnp.exp(s_old - s_top)
        total += stat_ref[1:2] * t_keep
        cross += stat_ref[2:3] * t_keep
        s_total += stat_ref[4:5] * s_keep
    for k, row in enumerate((t_top, total, cross, s_top, s_total)):
        stat_ref[k : k + 1] = row


def load_pair(x_ref, refs, pair, sem):
    tok, part = refs[0].shape[0], refs[1].shape[0]
    copies = [pltpu.make_async_copy(refs[0], pair.at[pl.ds(0, tok)], sem.at[0])]
    for k, ref in enumerate(refs[1:]):
        at = pl.multiple_of(tok + lax.rem(x_ref[1] + k, tok // part) * part, part)
        copies.append(pltpu.make_async_copy(ref, pair.at[pl.ds(at, part)], sem.at[k + 1]))
    for copy in copies:
        copy.start()
    for copy in copies:
        copy.wait()


def logits_kernel(n_pieces, place_ref, *rest):
    pieces_hbm, rest = rest[:n_pieces], rest[n_pieces:]
    (table_ref, weight_ref, weight_p_ref), rest = rest[:3], rest[3:]
    tok = pieces_hbm[0].shape[0]
    spread = len(rest) > 9
    first_stat_ref, scale_ref = rest[:2] if spread else (None, None)
    rest = rest[2:] if spread else rest
    t_hbm, s_hbm, stat_ref, student_hbm = rest[:4]
    spread_ref = rest[4] if spread else None
    pair, t_buf, s_buf, load_sem, out_sem = rest[-5:]
    width_t = table_ref.shape[1]
    rows = weight_ref.shape[0]

    load_pair(place_ref, pieces_hbm, pair, load_sem)
    students = pltpu.make_async_copy(pair.at[:, pl.ds(width_t, weight_ref.shape[1])], student_hbm, out_sem.at[2, 0])
    students.start()
    waiting = []
    for i in range(2 * rows // LOGIT_ROWS):
        slot, at = i % 2, i * LOGIT_ROWS
        source, low = (weight_ref, at) if at < rows else (weight_p_ref, at - rows)
        t = lax.dot_general(
            table_ref[at : at + LOGIT_ROWS], pair[:, :width_t], NT, preferred_element_type=F32
        )
        s = lax.dot_general(
            source[low : low + LOGIT_ROWS], pair[:, width_t:], NT, preferred_element_type=F32
        )
        if i >= 2:
            for copy in waiting[i - 2]:
                copy.wait()
        t_buf[slot] = t
        s_buf[slot] = s
        copies = [
            pltpu.make_async_copy(
                buf.at[slot], hbm.at[pl.ds(at, LOGIT_ROWS)], out_sem.at[k, slot]
            )
            for k, (buf, hbm) in enumerate(((t_buf, t_hbm), (s_buf, s_hbm)))
        ]
        for copy in copies:
            copy.start()
        waiting.append(copies)
        update_stats(i == 0, t, s, stat_ref)

    if spread:
        copies, _, wide = spread_ref.shape
        n_y = wide // tok
        row = lax.broadcasted_iota(jnp.int32, (8, tok), 0)
        scale = jnp.broadcast_to(scale_ref[...], (8, tok))
        first, last = first_stat_ref[...], stat_ref[...]
        pieces = (
            jnp.where(row == 5, scale, first[:, :tok]),
            last[:, :tok],
            first[:, tok:],
            last[:, tok:],
        )
        for r, piece in enumerate(pieces):
            at = pl.multiple_of(lax.rem(place_ref[0] + r, n_y) * tok, tok)
            for k in range(copies):
                spread_ref[k, :, pl.ds(at, tok)] = piece
    for copies in waiting[-2:]:
        for copy in copies:
            copy.wait()
    students.wait()


def logits_of(place, pieces, table, weight, weight_p, first_stats=None, scale=None, copies=0):
    width_t = table.shape[1]
    rows, width_s = weight.shape
    tok = pieces[0].shape[0]
    tokens = 2 * tok
    anywhere, on_chip = pl.BlockSpec(memory_space=pl.ANY), pl.BlockSpec(memory_space=pltpu.VMEM)
    in_specs = [pl.BlockSpec(memory_space=pltpu.SMEM)]
    in_specs += [anywhere] * len(pieces) + [on_chip] * 3
    out_specs = [anywhere, anywhere, on_chip, anywhere]
    tile = pltpu.HBM((2 * rows, tokens), F32)
    out_shape = [tile, tile, jax.ShapeDtypeStruct((8, tokens), F32), pltpu.HBM((tokens, width_s), BF16)]
    operands = [place, *pieces, table, weight, weight_p]
    if first_stats is not None:
        in_specs += [on_chip, on_chip]
        operands += [first_stats, scale]
        out_specs.append(on_chip)
        out_shape.append(jax.ShapeDtypeStruct((copies, 8, 2 * tokens), F32))
    return pl.pallas_call(
        functools.partial(logits_kernel, len(pieces)),
        in_specs=in_specs,
        out_specs=out_specs,
        out_shape=out_shape,
        scratch_shapes=[
            pltpu.VMEM((tokens, width_t + width_s), BF16),
            pltpu.VMEM((2, LOGIT_ROWS, tokens), F32),
            pltpu.VMEM((2, LOGIT_ROWS, tokens), F32),
            pltpu.SemaphoreType.DMA((len(pieces),)),
            pltpu.SemaphoreType.DMA((3, 2)),
        ],
        compiler_params=pltpu.CompilerParams(vmem_limit_bytes=VMEM_LOGITS),
        cost_estimate=pl.CostEstimate(
            flops=4 * rows * tokens * (width_t + width_s),
            transcendentals=4 * rows * tokens,
            bytes_accessed=2 * tokens * (width_t + 2 * width_s) + 16 * rows * tokens,
        ),
        name="logits",
    )(*operands)


def grad_kernel(y_ref, rows_ref, t0, s0, t1, s1, turned_ref, own_ref, other_ref, out_ref):
    half = own_ref.shape[0]
    n_y, tok = out_ref.shape[1], out_ref.shape[3]

    @pl.when(pl.program_id(0) == 0)
    def _():
        for p, (t, s) in enumerate(((t0, s0), (t1, s1))):
            at = slice(2 * p * tok, 2 * (p + 1) * tok)
            t_lse, s_lse, scale = (rows_ref[k : k + 1, at] for k in range(3))
            for q, ref in enumerate((own_ref, other_ref)):
                rows = slice(q * half, (q + 1) * half)
                gap = jnp.exp(s[rows] - s_lse) - jnp.exp(t[rows] - t_lse)
                ref[:, at] = (scale * gap).astype(BF16)

    total = jnp.dot(turned_ref[:, :half], own_ref[...], preferred_element_type=F32)
    total += jnp.dot(turned_ref[:, half:], other_ref[...], preferred_element_type=F32)
    for k, r in enumerate((0, 2, 1, 3)):
        at = lax.rem(y_ref[0] + r, n_y)
        out_ref[0, at] = total[:, k * tok : (k + 1) * tok].astype(BF16)


def gradients(y, rows, logits, turned, n_x, n_y):
    (t0, s0), (t1, s1) = logits
    vocab, tokens = t0.shape
    width = turned.shape[0]
    lg = pltpu.HBM((vocab // 2, 2 * tokens), BF16)
    whole = pl.BlockSpec((vocab, tokens), lambda i, y: (0, 0))
    lg_spec = pl.BlockSpec((vocab // 2, 2 * tokens), lambda i, y: (0, 0))
    cut = (width // n_x, 2 * tokens // n_y)
    return pl.pallas_call(
        grad_kernel,
        grid_spec=pltpu.PrefetchScalarGridSpec(
            num_scalar_prefetch=1,
            grid=(n_x,),
            in_specs=[
                pl.BlockSpec(rows.shape, lambda i, y: (0, 0)),
                whole,
                whole,
                whole,
                whole,
                pl.BlockSpec((width // n_x, vocab), lambda i, y: (i, 0)),
            ],
            out_specs=[lg_spec, lg_spec, pl.BlockSpec((1, n_y, *cut), lambda i, y: (i, 0, 0, 0))],
        ),
        out_shape=[lg, lg, pltpu.HBM((n_x, n_y, *cut), BF16)],
        compiler_params=pltpu.CompilerParams(vmem_limit_bytes=56 * MIB),
        cost_estimate=pl.CostEstimate(
            flops=4 * vocab * tokens * width,
            transcendentals=4 * vocab * tokens,
            bytes_accessed=2 * width * (vocab + 2 * tokens) + 20 * vocab * tokens,
        ),
        name="gradients",
    )(y, rows, t0, s0, t1, s1, turned)


def to_all(a, axes):
    n = lax.axis_size(axes)
    return lax.all_to_all(jnp.broadcast_to(a[None], (n, *a.shape)), axes, 0, 0, tiled=True)


def combine(stats):
    teacher_top = jnp.max(stats[:, 0], axis=0)
    student_top = jnp.max(stats[:, 3], axis=0)
    teacher_factor = jnp.exp(stats[:, 0] - teacher_top)
    student_factor = jnp.exp(stats[:, 3] - student_top)
    return jnp.stack(
        [
            teacher_top,
            jnp.sum(stats[:, 1] * teacher_factor, axis=0),
            jnp.sum(stats[:, 2] * teacher_factor, axis=0),
            student_top,
            jnp.sum(stats[:, 4] * student_factor, axis=0),
        ]
    )


def weight_kernel(own_ref, from_ref, s0_ref, s1_ref, s0_p_ref, s1_p_ref, out_ref):
    half = s0_ref.shape[0]
    total = jnp.dot(own_ref[:, :half], s0_ref[...], preferred_element_type=F32)
    total += jnp.dot(own_ref[:, half:], s1_ref[...], preferred_element_type=F32)
    total += jnp.dot(from_ref[:, :half], s0_p_ref[...], preferred_element_type=F32)
    total += jnp.dot(from_ref[:, half:], s1_p_ref[...], preferred_element_type=F32)
    out_ref[...] = total.astype(BF16)


def weight_gradient(own, from_p, *students):
    rows, tokens = own.shape
    half, width = students[0].shape
    whole = pl.BlockSpec((rows, tokens), lambda i: (0, 0))
    return pl.pallas_call(
        weight_kernel,
        grid=(width // WEIGHT_COLUMNS,),
        in_specs=[whole, whole] + [pl.BlockSpec((half, WEIGHT_COLUMNS), lambda i: (0, i))] * 4,
        out_specs=pl.BlockSpec((rows, WEIGHT_COLUMNS), lambda i: (0, i)),
        out_shape=jax.ShapeDtypeStruct((rows, width), BF16),
        compiler_params=pltpu.CompilerParams(vmem_limit_bytes=56 * MIB),
        cost_estimate=pl.CostEstimate(
            flops=4 * rows * tokens * width,
            transcendentals=0,
            bytes_accessed=2 * width * (rows + 4 * half) + 4 * rows * tokens,
        ),
        name="weight_gradient",
    )(own, from_p, *students)


def local(
    teacher_hidden, student_hidden, teacher_codes, teacher_scales, student_weight, loss_scale
):
    tok, width_t = teacher_hidden.shape
    width_s = student_hidden.shape[1]
    n_x, n_z, n_y = (lax.axis_size(a) for a in ("x", "z", "y"))
    x, y = lax.axis_index("x"), lax.axis_index("y")

    place = jnp.stack([y, x]).astype(jnp.int32)
    eighth = tok // (2 * n_x)
    odd = lax.rem(lax.axis_index("z"), 2)
    piece = [
        lax.dynamic_slice_in_dim(a, (2 * x + odd) * eighth, eighth, 0)
        for a in (teacher_hidden, student_hidden)
    ]
    piece = shift(jnp.concatenate(piece, axis=1), "y", 2)
    hidden = jnp.concatenate([teacher_hidden, student_hidden], axis=1)
    piece, whole = lax.optimization_barrier((piece, hidden))
    swapped = lax.ppermute(piece, "z", [(i, i ^ 1) for i in range(n_z)])
    quarter = jnp.where(
        odd == 0, jnp.concatenate([piece, swapped]), jnp.concatenate([swapped, piece])
    )
    after, before = shift(whole, "y", 1), shift(whole, "y", 3)
    codes_p = shift(teacher_codes, "c", 1)
    weight_p = shift(student_weight, "c", 1)
    scales_p = shift(teacher_scales, "c", 1)
    quarter, codes_p, weight_p, scales_p = lax.optimization_barrier(
        (quarter, codes_p, weight_p, scales_p)
    )
    quarters = [quarter, *(shift(quarter, "x", k) for k in range(1, n_x))]
    table = dequantize(teacher_codes, codes_p, teacher_scales, scales_p)
    turned = turned_over(student_weight, weight_p)

    tables = (table, student_weight, weight_p)
    t0, s0, stats0, students0 = logits_of(place, [hidden, *quarters], *tables)
    after, before, stats0, turned = lax.optimization_barrier((after, before, stats0, turned))
    students0_p = shift(students0, "c", 1)
    t1, s1, _, students1, mine = logits_of(
        place,
        [after, before],
        *tables,
        first_stats=stats0,
        scale=loss_scale.astype(F32)[None],
        copies=n_x * n_y,
    )
    seen = lax.all_to_all(mine, ("x", "y"), 0, 0, tiled=True)
    scales = jnp.sum(seen[:n_y, 5], axis=0)
    totals = combine(to_all(combine(seen), "z"))
    t_lse = totals[0] + jnp.log(totals[1])
    s_lse = totals[3] + jnp.log(totals[4])
    divergence = totals[2] / totals[1] - t_lse + s_lse
    found = jnp.stack([t_lse, s_lse, scales, divergence])
    found = jnp.concatenate([found, jnp.zeros_like(found)])
    found = jnp.concatenate([found, found[:, : (n_y - 1) * tok]], axis=1)
    found = lax.dynamic_slice_in_dim(found, y * tok, n_y * tok, 1)
    kl = found[3, :tok]
    order = [found[:, k * tok : (k + 1) * tok] for k in (0, 2, 1, 3)]
    own, other, blocks = gradients(
        place,
        jnp.concatenate(order, axis=1),
        ((t0, s0), (t1, s1)),
        turned,
        n_x,
        n_y,
    )
    from_p = shift(other, "c", 1)
    students1_p = shift(students1, "c", 1)
    grad_weight = weight_gradient(own, from_p, students0, students1, students0_p, students1_p)

    blocks = blocks.reshape(n_x * n_y, width_s // n_x, tok)
    got = lax.all_to_all(blocks, ("x", "y"), 0, 0, tiled=True)
    got = jnp.sum(got.astype(F32), axis=0).astype(BF16).reshape(n_z, -1, tok)
    got = lax.all_to_all(got, "z", 0, 0, tiled=True)
    grad_hidden = jnp.sum(got.astype(F32), axis=0).astype(BF16).T

    return kl, grad_hidden, grad_weight


def solution(mesh):
    split = Mesh(mesh.devices.reshape(4, 8, 4, 2), AXES)
    rows = P(("x", "z", "y", "c"), None)
    return jax.shard_map(
        local,
        mesh=split,
        in_specs=(P(DP, None), P(DP, None), rows, rows, rows, P(DP)),
        out_specs=(P(DP), P(DP, VOCAB), rows),
        check_vma=False,
    )
```

```python
import functools

import jax
import jax.numpy as jnp
from jax import lax
from jax.experimental import pallas as pl
from jax.experimental.pallas import tpu as pltpu
from jax.sharding import Mesh
from jax.sharding import PartitionSpec as P

GROUP = 128
AXES = ("x", "z", "y", "c")
DP = ("y", "c")
VOCAB = ("x", "z")
F32, BF16 = jnp.float32, jnp.bfloat16


def shift(a, axis, by):
    n = lax.axis_size(axis)
    return lax.ppermute(a, axis, [((i + by) % n, i) for i in range(n)])


def rolled(blocks, start):
    n = blocks.shape[0]
    return lax.dynamic_slice_in_dim(jnp.concatenate([blocks, blocks[:-1]]), start % n, n, 0)


NT = (((1,), (1,)), ((), ()))
MIB = 1024 * 1024
VMEM_LOGITS = 20 * MIB
DEQUANT_ROWS = 128
LOGIT_ROWS = 512
WEIGHT_COLUMNS = 512


def two_sources(i, steps):
    return (jnp.minimum(i, steps - 1), 0), (jnp.maximum(i - steps, 0), 0)


def dequant_kernel(own_steps, own_ref, other_ref, own_scale_ref, other_scale_ref, out_ref):
    def write(codes_ref, scale_ref):
        for g in range(codes_ref.shape[1] // GROUP):
            at = slice(g * GROUP, (g + 1) * GROUP)
            wide = codes_ref[:, at].astype(F32) * scale_ref[:, g : g + 1]
            out_ref[:, at] = wide.astype(BF16)

    @pl.when(pl.program_id(0) < own_steps)
    def _():
        write(own_ref, own_scale_ref)

    @pl.when(pl.program_id(0) >= own_steps)
    def _():
        write(other_ref, other_scale_ref)


def dequantize(codes, codes_p, scales, scales_p):
    rows, width = codes.shape
    steps = rows // DEQUANT_ROWS

    def source(width, k):
        return pl.BlockSpec((DEQUANT_ROWS, width), lambda i: two_sources(i, steps)[k])

    return pl.pallas_call(
        functools.partial(dequant_kernel, steps),
        grid=(2 * steps,),
        in_specs=[
            source(width, 0),
            source(width, 1),
            source(scales.shape[1], 0),
            source(scales.shape[1], 1),
        ],
        out_specs=pl.BlockSpec((DEQUANT_ROWS, width), lambda i: (i, 0)),
        out_shape=jax.ShapeDtypeStruct((2 * rows, width), BF16),
        compiler_params=pltpu.CompilerParams(vmem_limit_bytes=12 * MIB),
        cost_estimate=pl.CostEstimate(
            flops=2 * rows * width, transcendentals=0, bytes_accessed=8 * rows * width
        ),
        name="dequantize",
    )(codes, codes_p, scales, scales_p)


def turn_kernel(steps, own_ref, other_ref, out_ref):
    @pl.when(pl.program_id(0) < steps)
    def _():
        out_ref[...] = own_ref[...].T

    @pl.when(pl.program_id(0) >= steps)
    def _():
        out_ref[...] = other_ref[...].T


def turned_over(own, other):
    rows, width = own.shape
    steps = rows // DEQUANT_ROWS
    return pl.pallas_call(
        functools.partial(turn_kernel, steps),
        grid=(2 * steps,),
        in_specs=[
            pl.BlockSpec((DEQUANT_ROWS, width), lambda i: two_sources(i, steps)[0]),
            pl.BlockSpec((DEQUANT_ROWS, width), lambda i: two_sources(i, steps)[1]),
        ],
        out_specs=pl.BlockSpec((width, DEQUANT_ROWS), lambda i: (0, i)),
        out_shape=pltpu.HBM((width, 2 * rows), BF16),
        compiler_params=pltpu.CompilerParams(vmem_limit_bytes=8 * MIB),
        cost_estimate=pl.CostEstimate(
            flops=0, transcendentals=0, bytes_accessed=8 * rows * width
        ),
        name="turn",
    )(own, other)


def update_stats(first, t, s, stat_ref):
    t_top = jnp.max(t, axis=0, keepdims=True)
    s_top = jnp.max(s, axis=0, keepdims=True)
    if not first:
        t_old, s_old = stat_ref[0:1], stat_ref[3:4]
        t_top, s_top = jnp.maximum(t_old, t_top), jnp.maximum(s_old, s_top)
    e = jnp.exp(t - t_top)
    total = jnp.sum(e, axis=0, keepdims=True)
    cross = jnp.sum(e * (t - s), axis=0, keepdims=True)
    s_total = jnp.sum(jnp.exp(s - s_top), axis=0, keepdims=True)
    if first:
        stat_ref[5:8] = jnp.zeros((3, t.shape[1]), F32)
    else:
        t_keep, s_keep = jnp.exp(t_old - t_top), jnp.exp(s_old - s_top)
        total += stat_ref[1:2] * t_keep
        cross += stat_ref[2:3] * t_keep
        s_total += stat_ref[4:5] * s_keep
    for k, row in enumerate((t_top, total, cross, s_top, s_total)):
        stat_ref[k : k + 1] = row


def load_pair(x_ref, refs, pair, sem, turn, columns):
    tok, part = refs[0].shape[0], refs[1].shape[0]
    places = [pl.ds(0, tok)]
    for k in range(len(refs) - 1):
        at = pl.multiple_of(tok + lax.rem(x_ref[1] + k, tok // part) * part, part)
        places.append(pl.ds(at, part))
    copies = [
        pltpu.make_async_copy(ref.at[:, columns], pair.at[rows, columns], sem.at[turn, k])
        for k, (ref, rows) in enumerate(zip(refs, places))
    ]
    for copy in copies:
        copy.start()
    return copies


def logits_kernel(n_pieces, place_ref, *rest):
    pieces_hbm, rest = rest[:n_pieces], rest[n_pieces:]
    (table_ref, weight_ref, weight_p_ref), rest = rest[:3], rest[3:]
    tok = pieces_hbm[0].shape[0]
    spread = len(rest) > 9
    first_stat_ref, scale_ref = rest[:2] if spread else (None, None)
    rest = rest[2:] if spread else rest
    t_hbm, s_hbm, stat_ref, student_hbm = rest[:4]
    spread_ref = rest[4] if spread else None
    pair, t_buf, s_buf, load_sem, out_sem = rest[-5:]
    width_t = table_ref.shape[1]
    rows = weight_ref.shape[0]

    width_s = weight_ref.shape[1]
    student_in = load_pair(place_ref, pieces_hbm, pair, load_sem, 0, pl.ds(width_t, width_s))
    teacher_in = load_pair(place_ref, pieces_hbm, pair, load_sem, 1, pl.ds(0, width_t))
    for copy in student_in:
        copy.wait()
    students = pltpu.make_async_copy(pair.at[:, pl.ds(width_t, weight_ref.shape[1])], student_hbm, out_sem.at[2, 0])
    students.start()
    waiting = []
    for i in range(2 * rows // LOGIT_ROWS):
        slot, at = i % 2, i * LOGIT_ROWS
        source, low = (weight_ref, at) if at < rows else (weight_p_ref, at - rows)
        s = lax.dot_general(
            source[low : low + LOGIT_ROWS], pair[:, width_t:], NT, preferred_element_type=F32
        )
        if i == 0:
            for copy in teacher_in:
                copy.wait()
        t = lax.dot_general(
            table_ref[at : at + LOGIT_ROWS], pair[:, :width_t], NT, preferred_element_type=F32
        )
        if i >= 2:
            for copy in waiting[i - 2]:
                copy.wait()
        t_buf[slot] = t
        s_buf[slot] = s
        copies = [
            pltpu.make_async_copy(
                buf.at[slot], hbm.at[pl.ds(at, LOGIT_ROWS)], out_sem.at[k, slot]
            )
            for k, (buf, hbm) in enumerate(((t_buf, t_hbm), (s_buf, s_hbm)))
        ]
        for copy in copies:
            copy.start()
        waiting.append(copies)
        update_stats(i == 0, t, s, stat_ref)

    if spread:
        copies, _, wide = spread_ref.shape
        n_y = wide // tok
        row = lax.broadcasted_iota(jnp.int32, (8, tok), 0)
        scale = jnp.broadcast_to(scale_ref[...], (8, tok))
        first, last = first_stat_ref[...], stat_ref[...]
        pieces = (
            jnp.where(row == 5, scale, first[:, :tok]),
            last[:, :tok],
            first[:, tok:],
            last[:, tok:],
        )
        for r, piece in enumerate(pieces):
            at = pl.multiple_of(lax.rem(place_ref[0] + r, n_y) * tok, tok)
            for k in range(copies):
                spread_ref[k, :, pl.ds(at, tok)] = piece
    for copies in waiting[-2:]:
        for copy in copies:
            copy.wait()
    students.wait()


def logits_of(place, pieces, table, weight, weight_p, first_stats=None, scale=None, copies=0):
    width_t = table.shape[1]
    rows, width_s = weight.shape
    tok = pieces[0].shape[0]
    tokens = 2 * tok
    anywhere, on_chip = pl.BlockSpec(memory_space=pl.ANY), pl.BlockSpec(memory_space=pltpu.VMEM)
    in_specs = [pl.BlockSpec(memory_space=pltpu.SMEM)]
    in_specs += [anywhere] * len(pieces) + [on_chip] * 3
    out_specs = [anywhere, anywhere, on_chip, anywhere]
    tile = pltpu.HBM((2 * rows, tokens), F32)
    out_shape = [tile, tile, jax.ShapeDtypeStruct((8, tokens), F32), pltpu.HBM((tokens, width_s), BF16)]
    operands = [place, *pieces, table, weight, weight_p]
    if first_stats is not None:
        in_specs += [on_chip, on_chip]
        operands += [first_stats, scale]
        out_specs.append(on_chip)
        out_shape.append(jax.ShapeDtypeStruct((copies, 8, 2 * tokens), F32))
    return pl.pallas_call(
        functools.partial(logits_kernel, len(pieces)),
        in_specs=in_specs,
        out_specs=out_specs,
        out_shape=out_shape,
        scratch_shapes=[
            pltpu.VMEM((tokens, width_t + width_s), BF16),
            pltpu.VMEM((2, LOGIT_ROWS, tokens), F32),
            pltpu.VMEM((2, LOGIT_ROWS, tokens), F32),
            pltpu.SemaphoreType.DMA((2, len(pieces))),
            pltpu.SemaphoreType.DMA((3, 2)),
        ],
        compiler_params=pltpu.CompilerParams(vmem_limit_bytes=VMEM_LOGITS),
        cost_estimate=pl.CostEstimate(
            flops=4 * rows * tokens * (width_t + width_s),
            transcendentals=4 * rows * tokens,
            bytes_accessed=2 * tokens * (width_t + 2 * width_s) + 16 * rows * tokens,
        ),
        name="logits",
    )(*operands)


def grad_kernel(y_ref, rows_ref, t0, s0, t1, s1, turned_ref, own_ref, other_ref, out_ref):
    half = own_ref.shape[0]
    n_y, tok = out_ref.shape[1], out_ref.shape[3]

    @pl.when(pl.program_id(0) == 0)
    def _():
        for p, (t, s) in enumerate(((t0, s0), (t1, s1))):
            at = slice(2 * p * tok, 2 * (p + 1) * tok)
            t_lse, s_lse, scale = (rows_ref[k : k + 1, at] for k in range(3))
            for q, ref in enumerate((own_ref, other_ref)):
                rows = slice(q * half, (q + 1) * half)
                gap = jnp.exp(s[rows] - s_lse) - jnp.exp(t[rows] - t_lse)
                ref[:, at] = (scale * gap).astype(BF16)

    total = jnp.dot(turned_ref[:, :half], own_ref[...], preferred_element_type=F32)
    total += jnp.dot(turned_ref[:, half:], other_ref[...], preferred_element_type=F32)
    for k, r in enumerate((0, 2, 1, 3)):
        at = lax.rem(y_ref[0] + r, n_y)
        out_ref[0, at] = total[:, k * tok : (k + 1) * tok].astype(BF16)


def gradients(y, rows, logits, turned, n_x, n_y):
    (t0, s0), (t1, s1) = logits
    vocab, tokens = t0.shape
    width = turned.shape[0]
    lg = pltpu.HBM((vocab // 2, 2 * tokens), BF16)
    whole = pl.BlockSpec((vocab, tokens), lambda i, y: (0, 0))
    lg_spec = pl.BlockSpec((vocab // 2, 2 * tokens), lambda i, y: (0, 0))
    cut = (width // n_x, 2 * tokens // n_y)
    return pl.pallas_call(
        grad_kernel,
        grid_spec=pltpu.PrefetchScalarGridSpec(
            num_scalar_prefetch=1,
            grid=(n_x,),
            in_specs=[
                pl.BlockSpec(rows.shape, lambda i, y: (0, 0)),
                whole,
                whole,
                whole,
                whole,
                pl.BlockSpec((width // n_x, vocab), lambda i, y: (i, 0)),
            ],
            out_specs=[lg_spec, lg_spec, pl.BlockSpec((1, n_y, *cut), lambda i, y: (i, 0, 0, 0))],
        ),
        out_shape=[lg, lg, pltpu.HBM((n_x, n_y, *cut), BF16)],
        compiler_params=pltpu.CompilerParams(vmem_limit_bytes=56 * MIB),
        cost_estimate=pl.CostEstimate(
            flops=4 * vocab * tokens * width,
            transcendentals=4 * vocab * tokens,
            bytes_accessed=2 * width * (vocab + 2 * tokens) + 20 * vocab * tokens,
        ),
        name="gradients",
    )(y, rows, t0, s0, t1, s1, turned)


def to_all(a, axes):
    n = lax.axis_size(axes)
    return lax.all_to_all(jnp.broadcast_to(a[None], (n, *a.shape)), axes, 0, 0, tiled=True)


def combine(stats):
    teacher_top = jnp.max(stats[:, 0], axis=0)
    student_top = jnp.max(stats[:, 3], axis=0)
    teacher_factor = jnp.exp(stats[:, 0] - teacher_top)
    student_factor = jnp.exp(stats[:, 3] - student_top)
    return jnp.stack(
        [
            teacher_top,
            jnp.sum(stats[:, 1] * teacher_factor, axis=0),
            jnp.sum(stats[:, 2] * teacher_factor, axis=0),
            student_top,
            jnp.sum(stats[:, 4] * student_factor, axis=0),
        ]
    )


def weight_kernel(own_ref, from_ref, s0_ref, s1_ref, s0_p_ref, s1_p_ref, out_ref):
    half = s0_ref.shape[0]
    total = jnp.dot(own_ref[:, :half], s0_ref[...], preferred_element_type=F32)
    total += jnp.dot(own_ref[:, half:], s1_ref[...], preferred_element_type=F32)
    total += jnp.dot(from_ref[:, :half], s0_p_ref[...], preferred_element_type=F32)
    total += jnp.dot(from_ref[:, half:], s1_p_ref[...], preferred_element_type=F32)
    out_ref[...] = total.astype(BF16)


def weight_gradient(own, from_p, *students):
    rows, tokens = own.shape
    half, width = students[0].shape
    whole = pl.BlockSpec((rows, tokens), lambda i: (0, 0))
    return pl.pallas_call(
        weight_kernel,
        grid=(width // WEIGHT_COLUMNS,),
        in_specs=[whole, whole] + [pl.BlockSpec((half, WEIGHT_COLUMNS), lambda i: (0, i))] * 4,
        out_specs=pl.BlockSpec((rows, WEIGHT_COLUMNS), lambda i: (0, i)),
        out_shape=jax.ShapeDtypeStruct((rows, width), BF16),
        compiler_params=pltpu.CompilerParams(vmem_limit_bytes=56 * MIB),
        cost_estimate=pl.CostEstimate(
            flops=4 * rows * tokens * width,
            transcendentals=0,
            bytes_accessed=2 * width * (rows + 4 * half) + 4 * rows * tokens,
        ),
        name="weight_gradient",
    )(own, from_p, *students)


def local(
    teacher_hidden, student_hidden, teacher_codes, teacher_scales, student_weight, loss_scale
):
    tok, width_t = teacher_hidden.shape
    width_s = student_hidden.shape[1]
    n_x, n_z, n_y = (lax.axis_size(a) for a in ("x", "z", "y"))
    x, y = lax.axis_index("x"), lax.axis_index("y")

    place = jnp.stack([y, x]).astype(jnp.int32)
    eighth = tok // (2 * n_x)
    odd = lax.rem(lax.axis_index("z"), 2)
    piece = [
        lax.dynamic_slice_in_dim(a, (2 * x + odd) * eighth, eighth, 0)
        for a in (teacher_hidden, student_hidden)
    ]
    piece = shift(jnp.concatenate(piece, axis=1), "y", 2)
    hidden = jnp.concatenate([teacher_hidden, student_hidden], axis=1)
    piece, whole = lax.optimization_barrier((piece, hidden))
    swapped = lax.ppermute(piece, "z", [(i, i ^ 1) for i in range(n_z)])
    quarter = jnp.where(
        odd == 0, jnp.concatenate([piece, swapped]), jnp.concatenate([swapped, piece])
    )
    after, before = shift(whole, "y", 1), shift(whole, "y", 3)
    codes_p = shift(teacher_codes, "c", 1)
    weight_p = shift(student_weight, "c", 1)
    scales_p = shift(teacher_scales, "c", 1)
    quarter, codes_p, weight_p, scales_p = lax.optimization_barrier(
        (quarter, codes_p, weight_p, scales_p)
    )
    quarters = [quarter, *(shift(quarter, "x", k) for k in range(1, n_x))]
    table = dequantize(teacher_codes, codes_p, teacher_scales, scales_p)
    turned = turned_over(student_weight, weight_p)

    tables = (table, student_weight, weight_p)
    t0, s0, stats0, students0 = logits_of(place, [hidden, *quarters], *tables)
    after, before, stats0, turned = lax.optimization_barrier((after, before, stats0, turned))
    students0_p = shift(students0, "c", 1)
    t1, s1, _, students1, mine = logits_of(
        place,
        [after, before],
        *tables,
        first_stats=stats0,
        scale=loss_scale.astype(F32)[None],
        copies=n_x * n_y,
    )
    seen = lax.all_to_all(mine, ("x", "y"), 0, 0, tiled=True)
    scales = jnp.sum(seen[:n_y, 5], axis=0)
    totals = combine(to_all(combine(seen), "z"))
    t_lse = totals[0] + jnp.log(totals[1])
    s_lse = totals[3] + jnp.log(totals[4])
    divergence = totals[2] / totals[1] - t_lse + s_lse
    found = jnp.stack([t_lse, s_lse, scales, divergence])
    found = jnp.concatenate([found, jnp.zeros_like(found)])
    found = jnp.concatenate([found, found[:, : (n_y - 1) * tok]], axis=1)
    found = lax.dynamic_slice_in_dim(found, y * tok, n_y * tok, 1)
    kl = found[3, :tok]
    order = [found[:, k * tok : (k + 1) * tok] for k in (0, 2, 1, 3)]
    own, other, blocks = gradients(
        place,
        jnp.concatenate(order, axis=1),
        ((t0, s0), (t1, s1)),
        turned,
        n_x,
        n_y,
    )
    from_p = shift(other, "c", 1)
    students1_p = shift(students1, "c", 1)
    grad_weight = weight_gradient(own, from_p, students0, students1, students0_p, students1_p)

    blocks = blocks.reshape(n_x * n_y, width_s // n_x, tok)
    got = lax.all_to_all(blocks, ("x", "y"), 0, 0, tiled=True)
    got = jnp.sum(got.astype(F32), axis=0).astype(BF16).reshape(n_z, -1, tok)
    got = lax.all_to_all(got, "z", 0, 0, tiled=True)
    grad_hidden = jnp.sum(got.astype(F32), axis=0).astype(BF16).T

    return kl, grad_hidden, grad_weight


def solution(mesh):
    split = Mesh(mesh.devices.reshape(4, 8, 4, 2), AXES)
    rows = P(("x", "z", "y", "c"), None)
    return jax.shard_map(
        local,
        mesh=split,
        in_specs=(P(DP, None), P(DP, None), rows, rows, rows, P(DP)),
        out_specs=(P(DP), P(DP, VOCAB), rows),
        check_vma=False,
    )
```
